32 devices in a mesh: fsdp: 4 (over y, x), ctx: 8 (over z, core).
Axes of the slice: x: 2, y: 2, z: 4, core: 2. Of those that a mesh axis runs over, the one named last changes fastest.
Arguments:
- tokens: bfloat16 [8192, 768], P(('fsdp', 'ctx')), may hold values from -6 to 6
- frames: bfloat16 [12000, 768], P(('fsdp', 'ctx')), may hold values from -6 to 6
- document_starts: int32 [4, 2], P('fsdp'), may hold values from 0 to 1279, as said below
- cotangent: bfloat16 [8192, 768], P(('fsdp', 'ctx')), may hold values from -6 to 6
- gain_self: bfloat16 [768], P(('fsdp', 'ctx')), may hold values from 0.25 to 1.75
- gain_cross: bfloat16 [768], P(('fsdp', 'ctx')), may hold values from 0.25 to 1.75
- gain_feed: bfloat16 [768], P(('fsdp', 'ctx')), may hold values from 0.25 to 1.75
- gain_final: bfloat16 [768], P(('fsdp', 'ctx')), may hold values from 0.25 to 1.75
- self_query: bfloat16 [768, 768], P(('fsdp', 'ctx')), may hold values from -0.21875 to 0.21875
- self_key: bfloat16 [768, 768], P(('fsdp', 'ctx')), may hold values from -0.21875 to 0.21875
- self_value: bfloat16 [768, 768], P(('fsdp', 'ctx')), may hold values from -0.21875 to 0.21875
- self_output: bfloat16 [768, 768], P(('fsdp', 'ctx')), may hold values from -1.25 to 1.25
- cross_query: bfloat16 [768, 768], P(('fsdp', 'ctx')), may hold values from -0.21875 to 0.21875
- cross_key: bfloat16 [768, 768], P(('fsdp', 'ctx')), may hold values from -0.21875 to 0.21875
- cross_value: bfloat16 [768, 768], P(('fsdp', 'ctx')), may hold values from -0.21875 to 0.21875
- cross_output: bfloat16 [768, 768], P(('fsdp', 'ctx')), may hold values from -1.75 to 1.75
- feed_up: bfloat16 [768, 3072], P(('fsdp', 'ctx')), may hold values from -0.21875 to 0.21875
- feed_down: bfloat16 [3072, 768], P(('fsdp', 'ctx')), may hold values from -0.109375 to 0.109375
Outputs:
- layer_output: bfloat16 [8192, 768], P(('fsdp', 'ctx'))
- tokens_gradient: float32 [8192, 768], P(('fsdp', 'ctx'))
- frames_gradient: float32 [12000, 768], P(('fsdp', 'ctx'))
- gain_self_gradient: float32 [768], P(('fsdp', 'ctx'))
- gain_cross_gradient: float32 [768], P(('fsdp', 'ctx'))
- gain_feed_gradient: float32 [768], P(('fsdp', 'ctx'))
- gain_final_gradient: float32 [768], P(('fsdp', 'ctx'))
- self_query_gradient: float32 [768, 768], P(('fsdp', 'ctx'))
- self_key_gradient: float32 [768, 768], P(('fsdp', 'ctx'))
- self_value_gradient: float32 [768, 768], P(('fsdp', 'ctx'))
- self_output_gradient: float32 [768, 768], P(('fsdp', 'ctx'))
- cross_query_gradient: float32 [768, 768], P(('fsdp', 'ctx'))
- cross_key_gradient: float32 [768, 768], P(('fsdp', 'ctx'))
- cross_value_gradient: float32 [768, 768], P(('fsdp', 'ctx'))
- cross_output_gradient: float32 [768, 768], P(('fsdp', 'ctx'))
- feed_up_gradient: float32 [768, 3072], P(('fsdp', 'ctx'))
- feed_down_gradient: float32 [3072, 768], P(('fsdp', 'ctx'))
The draws below stay inside these ranges and needn't reach their ends.
Inputs may be any that keep to these rules, and one draw needn't show every extreme that they name: `document_starts`: document k of a sequence starts at position k * 1024 plus an offset in 0 to 255. The first document's offset is 0 and the last document's is exactly 255.
All inputs are finite; a program needn't handle non-finite values.
Results may differ from the reference program's by a relative error of at most 0.02.
Values may be sent and summed in bfloat16 or wider, within the bound.
No kernel may reach another device: no remote copies, remote signals or barrier semaphores. Data moves between devices by JAX's collectives and lax.ppermute only.
A program may use at most 256 MiB of HBM per device.

```python
import jax
import jax.numpy as jnp
from jax import lax

D = 768
HEAD_DIM = 64
FF = 3072
FRAMES = 1500
SPAN = 1024
JIT = 256
SEQS = 4
LEN = 2048
TOKENS = 8192
DOCS = 2
ENC_ALL = 12000


def draw_document_starts(key, part):
    first_key, second_key = jax.random.split(jax.random.fold_in(key, 17))
    offsets = jax.random.randint(first_key, (SEQS, DOCS), 0, JIT, dtype=jnp.int32)
    chosen = jax.random.randint(second_key, (SEQS, 1), 1, DOCS, dtype=jnp.int32)
    column = jnp.arange(DOCS, dtype=jnp.int32)[None, :]
    offsets = jnp.where(column == chosen, JIT - 1, offsets)
    offsets = jnp.where(column == DOCS - 1, JIT - 1, offsets)
    offsets = jnp.where(column == 0, 0, offsets)
    return (column * SPAN + offsets).astype(jnp.int32)


def with_spikes(values, own_key, source, target, parts, factor):
    def block_of(dim):
        return (jnp.arange(values.shape[dim]) // (values.shape[dim] // parts)).reshape((-1,) + (1,) * (values.ndim - 1 - dim))

    near = jax.random.permutation(own_key, parts)[block_of(target)]
    far = (block_of(target) + parts // 2) % parts
    return jnp.where((block_of(source) == near) | (block_of(source) == far), factor * values, values)


def block_levels(rng, shape, pieces, least, largest):
    def one(position, parts):
        heights = jax.random.uniform(jax.random.fold_in(jax.random.fold_in(rng, 6), position), (parts,), jnp.float32, least / len(pieces), largest / len(pieces))
        return jnp.repeat(jnp.exp(heights), shape[position] // parts).reshape((-1,) + (1,) * (len(shape) - position - 1))

    loudness = one(*pieces[0])
    for cut in pieces[1:]:
        loudness = loudness * one(*cut)
    return loudness


def scatter_about(rng, shape, width, limit, cuts=(), held_as=jnp.bfloat16):
    values = width * jax.random.normal(rng, shape, jnp.float32)
    if cuts:
        values = values * block_levels(rng, shape, cuts, -0.22, 0.18)
    return jnp.clip(values, -limit, limit).astype(held_as)


def noise_with(key, shape, deviation, limit, shards, heavy, kind=jnp.bfloat16):
    array = deviation * jax.random.normal(key, shape, jnp.float32)
    if shards:
        array = array * block_levels(key, shape, shards, -0.22, 0.18)
    return jnp.clip(with_spikes(array, jax.random.fold_in(key, 3), *heavy), -limit, limit).astype(kind)


def setup_inputs(seed: int = 0) -> dict:
    key_list = jax.random.split(jax.random.key(seed), 19)
    tokens = noise_with(key_list[0], (TOKENS, D), 1.0, 6.0, ((0, 32),), (0, 1, 32, 2.75))
    frames = scatter_about(key_list[1], (ENC_ALL, D), 1.0, 6.0, ((0, 32),))
    document_starts = draw_document_starts(jax.random.fold_in(key_list[18], 71), 0)
    cotangent = noise_with(key_list[3], (TOKENS, D), 1.0, 6.0, ((0, 32),), (0, 1, 32, 2.75))
    gain_self = jnp.clip(1.0 + 0.15 * jax.random.normal(key_list[4], (D,), jnp.float32), 0.25, 1.75).astype(jnp.bfloat16)
    gain_cross = jnp.clip(1.0 + 0.15 * jax.random.normal(key_list[5], (D,), jnp.float32), 0.25, 1.75).astype(jnp.bfloat16)
    gain_feed = jnp.clip(1.0 + 0.15 * jax.random.normal(key_list[6], (D,), jnp.float32), 0.25, 1.75).astype(jnp.bfloat16)
    gain_final = jnp.clip(1.0 + 0.15 * jax.random.normal(key_list[7], (D,), jnp.float32), 0.25, 1.75).astype(jnp.bfloat16)
    self_query = scatter_about(key_list[8], (D, D), D ** -0.5, 0.21875, ((0, 32),))
    self_key = scatter_about(key_list[9], (D, D), D ** -0.5, 0.21875, ((0, 32),))
    self_value = scatter_about(key_list[10], (D, D), D ** -0.5, 0.21875, ((0, 32),))
    self_output = scatter_about(key_list[11], (D, D), (D // 32) ** -0.5, 1.25, ((0, 32),))
    cross_query = scatter_about(key_list[12], (D, D), D ** -0.5, 0.21875, ((0, 32),))
    cross_key = scatter_about(key_list[13], (D, D), D ** -0.5, 0.21875, ((0, 32),))
    cross_value = scatter_about(key_list[14], (D, D), D ** -0.5, 0.21875, ((0, 32),))
    cross_output = scatter_about(key_list[15], (D, D), (D // 64) ** -0.5, 1.75, ((0, 32),))
    feed_up = scatter_about(key_list[16], (D, FF), D ** -0.5, 0.21875, ((0, 32),))
    feed_down = scatter_about(key_list[17], (FF, D), FF ** -0.5, 0.109375, ((0, 32),))
    return dict(tokens=tokens, frames=frames, document_starts=document_starts, cotangent=cotangent, gain_self=gain_self, gain_cross=gain_cross, gain_feed=gain_feed, gain_final=gain_final, self_query=self_query, self_key=self_key, self_value=self_value, self_output=self_output, cross_query=cross_query, cross_key=cross_key, cross_value=cross_value, cross_output=cross_output, feed_up=feed_up, feed_down=feed_down)


@jax.custom_vjp
def low(v):
    return lax.optimization_barrier(v.astype(jnp.bfloat16)).astype(jnp.float32)

@jax.custom_vjp
def low_back(v):
    return v

def low_keep(v):
    return (low(v), None)

def low_pass(kept, grad):
    return (grad,)

def back_keep(v):
    return (v, None)

def back_low(kept, grad):
    return (low(grad),)
low.defvjp(low_keep, low_pass)
low_back.defvjp(back_keep, back_low)

def matmul(left, right):
    return jnp.dot(left, right, precision=lax.Precision.HIGHEST, preferred_element_type=jnp.float32)

def normalize(states, gain):
    center = states - lax.optimization_barrier(jnp.mean(states, axis=-1, keepdims=True))
    spread = lax.optimization_barrier(jnp.mean(center * center, axis=-1, keepdims=True))
    return center * lax.rsqrt(spread + 1e-05) * gain

def exact_gelu(values):
    return jax.nn.gelu(values, approximate=False)

def attend(queries, keys, values, allowed):
    count = queries.shape[0]
    heads = queries.shape[1] // HEAD_DIM
    query_heads = queries.reshape(count, heads, HEAD_DIM)
    key_heads = keys.reshape(keys.shape[0], heads, HEAD_DIM)
    value_heads = values.reshape(values.shape[0], heads, HEAD_DIM)
    scores = jnp.einsum('qhd,khd->hqk', query_heads, key_heads, precision=lax.Precision.HIGHEST) * HEAD_DIM ** (-0.5)
    scores = low_back(scores)
    masked = jnp.where(allowed[None], scores, -jnp.inf)
    peak = lax.optimization_barrier(jnp.max(masked, axis=-1, keepdims=True))
    weights = jnp.exp(masked - peak)
    weights = low(weights / lax.optimization_barrier(jnp.sum(weights, axis=-1, keepdims=True)))
    mixed = jnp.einsum('hqk,khd->qhd', weights, value_heads, precision=lax.Precision.HIGHEST)
    return mixed.reshape(count, heads * HEAD_DIM)

def sequence_layer(states, frames, starts, weights):
    gain_self, gain_cross, gain_feed, gain_final, self_query, self_key, self_value, self_output, cross_query, cross_key, cross_value, cross_output, feed_up, feed_down = weights
    length = states.shape[0]
    block = min(512, length)
    window = min(length, block + SPAN + JIT)
    span_docs = min(DOCS, (block + JIT - 1) // SPAN + 2)
    places = jnp.arange(length, dtype=jnp.int32)
    token_docs = lax.optimization_barrier(jnp.sum((starts[None, :] <= places[:, None]).astype(jnp.int32), axis=1)) - 1
    numbers = jnp.arange(length // block, dtype=jnp.int32)
    normed = low(normalize(states, gain_self))
    queries = low_back(low(matmul(normed, self_query)))
    keys = low_back(low(matmul(normed, self_key)))
    values = low_back(low(matmul(normed, self_value)))

    def self_block(number):
        first = (number * block).astype(jnp.int32)
        edge = jnp.clip(first - SPAN - JIT, 0, length - window).astype(jnp.int32)
        query_places = first + jnp.arange(block, dtype=jnp.int32)
        key_places = edge + jnp.arange(window, dtype=jnp.int32)
        query_docs = lax.dynamic_slice_in_dim(token_docs, first, block)
        key_docs = lax.dynamic_slice_in_dim(token_docs, edge, window)
        allowed = (query_docs[:, None] == key_docs[None, :]) & (key_places[None, :] <= query_places[:, None])
        return attend(lax.dynamic_slice_in_dim(queries, first, block), lax.dynamic_slice_in_dim(keys, edge, window), lax.dynamic_slice_in_dim(values, edge, window), allowed)
    self_mixed = lax.map(jax.checkpoint(self_block), numbers).reshape(length, D)
    self_heads = low_back(low(self_mixed))
    first_sum = states + low_back(matmul(self_heads, self_output))
    normed = low(normalize(first_sum, gain_cross))
    cross_queries = low_back(low(matmul(normed, cross_query)))
    frame_keys = low_back(low(matmul(frames, cross_key)))
    frame_values = low_back(low(matmul(frames, cross_value)))
    frame_count = span_docs * FRAMES

    def cross_block(number):
        first = (number * block).astype(jnp.int32)
        lowest = jnp.clip(jnp.floor_divide(first - JIT, SPAN), 0, DOCS - span_docs).astype(jnp.int32)
        frame_first = (lowest * FRAMES).astype(jnp.int32)
        frame_docs = lowest + jnp.arange(frame_count, dtype=jnp.int32) // FRAMES
        query_docs = lax.dynamic_slice_in_dim(token_docs, first, block)
        allowed = query_docs[:, None] == frame_docs[None, :]
        return attend(lax.dynamic_slice_in_dim(cross_queries, first, block), lax.dynamic_slice_in_dim(frame_keys, frame_first, frame_count), lax.dynamic_slice_in_dim(frame_values, frame_first, frame_count), allowed)
    cross_mixed = lax.map(jax.checkpoint(cross_block), numbers).reshape(length, D)
    cross_heads = low_back(low(cross_mixed))
    second_sum = first_sum + low_back(matmul(cross_heads, cross_output))
    normed = low(normalize(second_sum, gain_feed))
    inner = low_back(matmul(normed, feed_up))
    hidden = low(exact_gelu(inner))
    third_sum = second_sum + low_back(matmul(hidden, feed_down))
    return normalize(third_sum, gain_final)

def layer(tokens, frames, document_starts, weights):
    token_rows = tokens.reshape(SEQS, LEN, D)
    frame_rows = frames.reshape(SEQS, DOCS * FRAMES, D)

    def one_sequence(packed):
        return sequence_layer(packed[0], packed[1], packed[2], weights)
    return lax.map(one_sequence, (token_rows, frame_rows, document_starts)).reshape(TOKENS, D)

def reference(tokens, frames, document_starts, cotangent, gain_self, gain_cross, gain_feed, gain_final, self_query, self_key, self_value, self_output, cross_query, cross_key, cross_value, cross_output, feed_up, feed_down):
    weights = tuple((matrix.astype(jnp.float32) for matrix in (gain_self, gain_cross, gain_feed, gain_final, self_query, self_key, self_value, self_output, cross_query, cross_key, cross_value, cross_output, feed_up, feed_down)))

    def whole(token_values, frame_values, weight_values):
        return layer(token_values, frame_values, document_starts, weight_values)
    result, pullback = jax.vjp(whole, tokens.astype(jnp.float32), frames.astype(jnp.float32), weights)
    token_gradient, frame_gradient, gradients = pullback(cotangent.astype(jnp.float32))
    return (result.astype(jnp.bfloat16), token_gradient, frame_gradient, gradients[0], gradients[1], gradients[2], gradients[3], gradients[4], gradients[5], gradients[6], gradients[7], gradients[8], gradients[9], gradients[10], gradients[11], gradients[12], gradients[13])
```

```python
import functools

import jax
import jax.numpy as jnp
from jax import lax
from jax.experimental import pallas as pl
from jax.experimental.pallas import tpu as pltpu
from jax.sharding import Mesh, PartitionSpec as P

D = 768
HD = 64
FF = 3072
SPAN = 1024
MEM = 4
ROWS = 256
WIDE = (MEM + 1) * ROWS
HEADS = 3
FR = 375
FP = 384
KEYS = MEM * FP
NEG = -1e30
ALL = ("fsdp", "grp", "mem")
LINE = ("grp", "mem")
F32 = jnp.float32
BF = jnp.bfloat16


def normalize(states, gain):
    center = states - jnp.mean(states, axis=-1, keepdims=True)
    spread = jnp.mean(center * center, axis=-1, keepdims=True)
    return center * lax.rsqrt(spread + 1e-05) * gain


def exact_gelu(values):
    return jax.nn.gelu(values, approximate=False)


def product(left, right):
    return jnp.dot(left, right, preferred_element_type=F32)


def product_left(left, right):
    return lax.dot_general(left, right, (((0,), (0,)), ((), ())), preferred_element_type=F32)


def product_right(left, right):
    return lax.dot_general(left, right, (((1,), (1,)), ((), ())), preferred_element_type=F32)


def lanes(rows):
    return lax.broadcasted_iota(jnp.int32, (rows, 128), 1)


def head_lanes(head, rows):
    lane = lanes(rows)
    return (lane >= HD) if head == 1 else (lane < HD)


def only(head, window):
    return jnp.where(head_lanes(head, window.shape[0]), window, jnp.zeros_like(window))


def swap_halves(window):
    return pltpu.roll(window.astype(F32), HD, 1).astype(BF)


def marked(head, window, value):
    spare = 0 if head == 1 else HD
    return jnp.where(lanes(window.shape[0]) == spare, value, window)


def scaled(window):
    return (window.astype(F32) * 0.125).astype(BF)


def valid_rows(scal, first, count):
    row = first + lax.broadcasted_iota(jnp.int32, (count, 128), 0)
    return (row >= scal[4]) & (row < MEM * ROWS + scal[5])


def gather_rows(scal, pieces, tail, whole, step):
    for j in range(MEM):
        start = pl.multiple_of(scal[j] * step, step)
        whole[pl.ds(start, pieces[j].shape[0]), :] = pieces[j][...]
    if tail is not None:
        whole[pl.ds(MEM * step, tail.shape[0]), :] = tail[...]


def scatter_rows(scal, whole, pieces, tail, step):
    for j in range(MEM):
        start = pl.multiple_of(scal[j] * step, step)
        pieces[j][...] = whole[pl.ds(start, pieces[j].shape[0]), :].astype(BF)
    if tail is not None:
        tail[...] = whole[pl.ds(MEM * step, tail.shape[0]), :].astype(BF)


def self_prepare(scal, whole, qa, ka):
    hidden = lax.broadcasted_iota(jnp.int32, (WIDE, 128), 0) < scal[4]
    for head in range(HEADS):
        if head < 2:
            query, key = whole[:, 0:128], whole[:, 128:256]
        else:
            query = whole[:, 384:512]
            key = swap_halves(query)
        qa[head] = marked(head, scaled(query), jnp.asarray(NEG, BF))
        ka[head] = marked(head, only(head, key), jnp.where(hidden, 1.0, 0.0).astype(BF))


def forward_finish(scal, ot, out, outs, tail):
    ot[HEADS * HD :, :] = jnp.zeros((HD, WIDE), F32)
    for i in range(MEM + 1):
        block = ot[:, i * ROWS : (i + 1) * ROWS].T
        keep = valid_rows(scal, i * ROWS, ROWS)[:, 0:1]
        out[i * ROWS : (i + 1) * ROWS, :] = jnp.where(keep, block, 0.0).astype(BF)
    scatter_rows(scal, out, outs, tail, ROWS)


def self_forward_kernel(scal, p0, p1, p2, p3, tail, o0, o1, o2, o3, otail, ot, lse, whole, qa, ka, vt, out):
    gather_rows(scal, (p0, p1, p2, p3), tail, whole, ROWS)
    self_prepare(scal, whole, qa, ka)
    turned = whole[:, 256:384].astype(F32).T.astype(BF)
    vt[0] = turned[0:HD]
    vt[1] = turned[HD:128]
    vt[2] = whole[:, 512:640].astype(F32).T.astype(BF)[0:HD]
    causal = lax.broadcasted_iota(jnp.int32, (ROWS, ROWS), 0) <= lax.broadcasted_iota(
        jnp.int32, (ROWS, ROWS), 1
    )

    def one_head(head, carry):
        for i in range(MEM + 1):
            a, b = i * ROWS, (i + 1) * ROWS
            query = qa[head, a:b, :]
            near = jnp.where(causal, product_right(ka[head, a:b, :], query), NEG)
            top = jnp.max(near, axis=0, keepdims=True)
            if i:
                far = product_right(ka[head, 0:a, :], query)
                top = jnp.maximum(top, jnp.max(far, axis=0, keepdims=True))
                far = jnp.exp(far - top)
            near = jnp.exp(near - top)
            total = jnp.sum(near, axis=0, keepdims=True)
            if i:
                total = total + jnp.sum(far, axis=0, keepdims=True)
            scale = 1.0 / total
            mixed = product(vt[head, :, a:b], (near * scale).astype(BF))
            if i:
                mixed = mixed + product(vt[head, :, 0:a], (far * scale).astype(BF))
            ot[pl.ds(pl.multiple_of(head * HD, HD), HD), a:b] = mixed
            lse[head, 0:1, a:b] = top + jnp.log(total)
        return carry

    lax.fori_loop(0, HEADS, one_head, 0)
    forward_finish(scal, ot, out, (o0, o1, o2, o3), otail)


def grads_prepare(scal, grads, ot, dm, delta):
    for i in range(MEM + 1):
        a, b = i * ROWS, (i + 1) * ROWS
        keep = valid_rows(scal, a, ROWS)[:, 0:1]
        clean = jnp.where(keep, grads[a:b, :].astype(F32), 0.0)
        turned = clean.T * ot[:, a:b]
        clean = clean.astype(BF)
        for head in range(HEADS):
            window = clean[:, 0:128] if head < 2 else clean[:, 128:256]
            dm[head, a:b, :] = only(head, window)
            delta[head, 0:1, a:b] = jnp.sum(turned[head * HD : (head + 1) * HD], axis=0, keepdims=True)


def self_backward_kernel(
    scal, p0, p1, p2, p3, tail, g0, g1, g2, g3, gtail, ot, lse,
    d0, d1, d2, d3, dtail,
    whole, grads, qa, ka, qm, kt, vm, dm, delta, dqt, dk, dv, out,
):
    gather_rows(scal, (p0, p1, p2, p3), tail, whole, ROWS)
    gather_rows(scal, (g0, g1, g2, g3), gtail, grads, ROWS)
    self_prepare(scal, whole, qa, ka)
    grads_prepare(scal, grads, ot, dm, delta)
    turned = whole[:, 128:256].astype(F32).T.astype(BF)
    kt[0] = turned[0:HD]
    kt[1] = turned[HD:128]
    kt[2] = whole[:, 384:512].astype(F32).T.astype(BF)[HD:128]
    for head in range(HEADS):
        qm[head] = only(head, scaled(whole[:, 0:128] if head < 2 else whole[:, 384:512]))
        vm[head] = only(head, whole[:, 256:384] if head < 2 else whole[:, 512:640])
    dk[...] = jnp.zeros_like(dk)
    dv[...] = jnp.zeros_like(dv)
    dqt[HEADS * HD :, :] = jnp.zeros((HD, WIDE), F32)
    causal = lax.broadcasted_iota(jnp.int32, (ROWS, ROWS), 0) <= lax.broadcasted_iota(
        jnp.int32, (ROWS, ROWS), 1
    )

    def one_head(head, carry):
        side = jnp.where(head == 2, 1, 0)
        for i in range(MEM + 1):
            a, b = i * ROWS, (i + 1) * ROWS
            query, grad, own = qa[head, a:b, :], dm[head, a:b, :], qm[head, a:b, :]
            level, offset = lse[head, 0:1, a:b], delta[head, 0:1, a:b]
            change = jnp.zeros((HD, ROWS), F32)
            for low, high in ((a, b), (0, a)):
                if low == high:
                    continue
                scores = product_right(ka[head, low:high, :], query)
                if low == a:
                    scores = jnp.where(causal, scores, NEG)
                probs = jnp.exp(scores - level)
                slopes = product_right(vm[head, low:high, :], grad)
                slopes = (probs * (slopes - offset)).astype(BF)
                dv[side, low:high, :] += product(probs.astype(BF), grad)
                dk[side, low:high, :] += product(slopes, own)
                change = change + product(kt[head, :, low:high], slopes)
            dqt[pl.ds(pl.multiple_of(head * HD, HD), HD), a:b] = change * 0.125
        return carry

    lax.fori_loop(0, HEADS, one_head, 0)
    for i in range(MEM + 1):
        a, b = i * ROWS, (i + 1) * ROWS
        query = dqt[:, a:b].T
        out[a:b, 0:128] = query[:, 0:128].astype(BF)
        out[a:b, 128:256] = dk[0, a:b, :].astype(BF)
        out[a:b, 256:384] = dv[0, a:b, :].astype(BF)
        out[a:b, 384:512] = (query[:, 128:256] + pltpu.roll(dk[1, a:b, :], HD, 1)).astype(BF)
        out[a:b, 512:640] = dv[1, a:b, :].astype(BF)
    scatter_rows(scal, out, (d0, d1, d2, d3), dtail, ROWS)


def cross_prepare(whole, queries, qa, ka):
    spare = (lax.broadcasted_iota(jnp.int32, (KEYS, 128), 0) % FP) >= FR
    for head in range(HEADS):
        query = queries[:, 0:128] if head < 2 else queries[:, 128:256]
        key = whole[:, 0:128] if head < 2 else whole[:, 256:384]
        qa[head] = marked(head, scaled(query), jnp.asarray(NEG, BF))
        ka[head] = marked(head, only(head, key), jnp.where(spare, 1.0, 0.0).astype(BF))


def cross_forward_kernel(
    scal, q0, q1, q2, q3, qtail, f0, f1, f2, f3,
    o0, o1, o2, o3, otail, ot, lse,
    whole, queries, qa, ka, vt, out,
):
    whole[...] = jnp.zeros_like(whole)
    gather_rows(scal, (f0, f1, f2, f3), None, whole, FP)
    gather_rows(scal, (q0, q1, q2, q3), qtail, queries, ROWS)
    cross_prepare(whole, queries, qa, ka)
    turned = whole[:, 128:256].astype(F32).T.astype(BF)
    vt[0] = turned[0:HD]
    vt[1] = turned[HD:128]
    vt[2] = whole[:, 256:384].astype(F32).T.astype(BF)[HD:128]

    def one_head(head, carry):
        for i in range(MEM + 1):
            a, b = i * ROWS, (i + 1) * ROWS
            scores = product_right(ka[head], qa[head, a:b, :])
            top = jnp.max(scores, axis=0, keepdims=True)
            scores = jnp.exp(scores - top)
            total = jnp.sum(scores, axis=0, keepdims=True)
            mixed = product(vt[head], (scores * (1.0 / total)).astype(BF))
            ot[pl.ds(pl.multiple_of(head * HD, HD), HD), a:b] = mixed
            lse[head, 0:1, a:b] = top + jnp.log(total)
        return carry

    lax.fori_loop(0, HEADS, one_head, 0)
    forward_finish(scal, ot, out, (o0, o1, o2, o3), otail)


def cross_backward_kernel(
    scal, q0, q1, q2, q3, qtail, f0, f1, f2, f3, g0, g1, g2, g3, gtail, ot, lse,
    d0, d1, d2, d3, dtail, e0, e1, e2, e3,
    whole, queries, grads, qa, ka, qm, kt, vm, dm, delta, dqt, dk, dv, out, fout,
):
    whole[...] = jnp.zeros_like(whole)
    gather_rows(scal, (f0, f1, f2, f3), None, whole, FP)
    gather_rows(scal, (q0, q1, q2, q3), qtail, queries, ROWS)
    gather_rows(scal, (g0, g1, g2, g3), gtail, grads, ROWS)
    cross_prepare(whole, queries, qa, ka)
    grads_prepare(scal, grads, ot, dm, delta)
    turned = whole[:, 0:128].astype(F32).T.astype(BF)
    kt[0] = turned[0:HD]
    kt[1] = turned[HD:128]
    kt[2] = whole[:, 256:384].astype(F32).T.astype(BF)[0:HD]
    for head in range(HEADS):
        qm[head] = only(head, scaled(queries[:, 0:128] if head < 2 else queries[:, 128:256]))
        vm[head] = only(head, whole[:, 128:256] if head < 2 else swap_halves(whole[:, 256:384]))
    dk[...] = jnp.zeros_like(dk)
    dv[...] = jnp.zeros_like(dv)
    dqt[HEADS * HD :, :] = jnp.zeros((HD, WIDE), F32)

    def one_head(head, carry):
        side = jnp.where(head == 2, 1, 0)
        for i in range(MEM + 1):
            a, b = i * ROWS, (i + 1) * ROWS
            grad = dm[head, a:b, :]
            scores = product_right(ka[head], qa[head, a:b, :])
            probs = jnp.exp(scores - lse[head, 0:1, a:b])
            slopes = product_right(vm[head], grad)
            slopes = (probs * (slopes - delta[head, 0:1, a:b])).astype(BF)
            dv[side] += product(probs.astype(BF), grad)
            dk[side] += product(slopes, qm[head, a:b, :])
            change = product(kt[head], slopes)
            dqt[pl.ds(pl.multiple_of(head * HD, HD), HD), a:b] = change * 0.125
        return carry

    lax.fori_loop(0, HEADS, one_head, 0)
    for i in range(MEM + 1):
        a, b = i * ROWS, (i + 1) * ROWS
        out[a:b, :] = dqt[:, a:b].T.astype(BF)
    scatter_rows(scal, out, (d0, d1, d2, d3), dtail, ROWS)
    fout[:, 0:128] = dk[0].astype(BF)
    fout[:, 128:256] = dv[0].astype(BF)
    fout[:, 256:384] = (dk[1] + pltpu.roll(dv[1], HD, 1)).astype(BF)
    scatter_rows(scal, fout, (e0, e1, e2, e3), None, FP)


def shape(*dims, dtype=BF):
    return jax.ShapeDtypeStruct(dims, dtype)


def vmem(*dims, dtype=BF):
    return pltpu.VMEM(dims, dtype)


def call(kernel, scal, args, outs, scratch, flops, exps):
    full = pl.BlockSpec(memory_space=pltpu.VMEM)
    return pl.pallas_call(
        kernel,
        out_shape=outs,
        in_specs=[pl.BlockSpec(memory_space=pltpu.SMEM)] + [full] * len(args),
        out_specs=[full] * len(outs),
        scratch_shapes=scratch,
        cost_estimate=pl.CostEstimate(flops=flops, transcendentals=exps, bytes_accessed=4 << 20),
        compiler_params=pltpu.CompilerParams(vmem_limit_bytes=60 << 20),
    )(scal, *args)


def self_forward(scal, pieces):
    outs = [shape(ROWS, 256)] * 5 + [shape(256, WIDE, dtype=F32), shape(HEADS, 8, WIDE, dtype=F32)]
    scratch = [vmem(WIDE, 640), vmem(HEADS, WIDE, 128), vmem(HEADS, WIDE, 128), vmem(HEADS, HD, WIDE), vmem(WIDE, 256)]
    got = call(self_forward_kernel, scal, pieces, outs, scratch, 3 << 30, 3 << 20)
    return (got[:5], got[5:])


def self_backward(scal, pieces, grads, kept):
    outs = [shape(ROWS, 640)] * 5
    head = vmem(HEADS, WIDE, 128)
    scratch = [
        vmem(WIDE, 640), vmem(WIDE, 256), head, head, head, vmem(HEADS, HD, WIDE), head, head,
        vmem(HEADS, 8, WIDE, dtype=F32), vmem(256, WIDE, dtype=F32),
        vmem(2, WIDE, 128, dtype=F32), vmem(2, WIDE, 128, dtype=F32), vmem(WIDE, 640),
    ]
    return call(self_backward_kernel, scal, [*pieces, *grads, *kept], outs, scratch, 8 << 30, 3 << 20)


def cross_forward(scal, queries, pieces):
    outs = [shape(ROWS, 256)] * 5 + [shape(256, WIDE, dtype=F32), shape(HEADS, 8, WIDE, dtype=F32)]
    scratch = [
        vmem(KEYS, 384), vmem(WIDE, 256), vmem(HEADS, WIDE, 128), vmem(HEADS, KEYS, 128),
        vmem(HEADS, HD, KEYS), vmem(WIDE, 256),
    ]
    got = call(cross_forward_kernel, scal, [*queries, *pieces], outs, scratch, 6 << 30, 6 << 20)
    return (got[:5], got[5:])


def cross_backward(scal, queries, pieces, grads, kept):
    outs = [shape(ROWS, 256)] * 5 + [shape(FR, 384)] * 4
    head, keys = (vmem(HEADS, WIDE, 128), vmem(HEADS, KEYS, 128))
    scratch = [
        vmem(KEYS, 384), vmem(WIDE, 256), vmem(WIDE, 256), head, keys, head, vmem(HEADS, HD, KEYS), keys, head,
        vmem(HEADS, 8, WIDE, dtype=F32), vmem(256, WIDE, dtype=F32),
        vmem(2, KEYS, 128, dtype=F32), vmem(2, KEYS, 128, dtype=F32), vmem(WIDE, 256), vmem(KEYS, 384),
    ]
    got = call(cross_backward_kernel, scal, [*queries, *pieces, *grads, *kept], outs, scratch, 16 << 30, 6 << 20)
    return (got[:5], got[5:])


def swap(value, mask):
    if mask == 0:
        return value
    count = lax.axis_size("grp") * MEM
    return lax.ppermute(value, LINE, [(s, s ^ mask) for s in range(count)])


def to_previous(value):
    count = lax.axis_size("grp") * MEM
    return lax.ppermute(value, LINE, [(s, s - MEM) for s in range(MEM, count)])


def to_next(value):
    count = lax.axis_size("grp") * MEM
    return lax.ppermute(value, LINE, [(s, s + MEM) for s in range(count - MEM)])


def spread(member, rows, width):
    return [
        swap(lax.dynamic_slice_in_dim(rows, (member ^ j) * width, width, axis=1), j)
        for j in range(MEM)
    ]


def with_tail(member, pieces):
    return [*pieces, to_previous(lax.select_n(member, *pieces))]


def join(member, pieces):
    return jnp.concatenate(
        [lax.select_n(member, *[pieces[s ^ m] for m in range(MEM)]) for s in range(MEM)], axis=1
    )


def collect(member, pieces):
    late = to_next(pieces[4])
    whole = []
    for j in range(MEM):
        piece = pieces[j].astype(F32) + jnp.where(member == j, late.astype(F32), 0.0)
        whole.append(swap(piece.astype(BF), j))
    return join(member, whole)


def self_columns(query, key, value):
    parts = []
    for m in range(MEM):
        a = 192 * m
        for matrix in (query, key, value):
            parts.append(matrix[:, a : a + 128])
        parts += [query[:, a + 128 : a + 192], key[:, a + 128 : a + 192], value[:, a + 128 : a + 192]]
        parts.append(jnp.zeros((query.shape[0], 64), query.dtype))
    return jnp.concatenate(parts, axis=1)


def self_columns_back(matrix):
    parts = [[], [], []]
    for m in range(MEM):
        a = 640 * m
        for n in range(3):
            parts[n] += [matrix[:, a + 128 * n : a + 128 * n + 128], matrix[:, a + 384 + 64 * n : a + 448 + 64 * n]]
    return [jnp.concatenate(part, axis=1) for part in parts]


def query_columns(matrix):
    zero = jnp.zeros((matrix.shape[0], 64), matrix.dtype)
    parts = []
    for m in range(MEM):
        parts += [matrix[:, 192 * m : 192 * m + 192], zero]
    return jnp.concatenate(parts, axis=1)


def query_columns_back(matrix):
    return jnp.concatenate([matrix[:, 256 * m : 256 * m + 192] for m in range(MEM)], axis=1)


def frame_columns(key, value):
    parts = []
    for m in range(MEM):
        a = 192 * m
        parts += [key[:, a : a + 128], value[:, a : a + 128], key[:, a + 128 : a + 192], value[:, a + 128 : a + 192]]
    return jnp.concatenate(parts, axis=1)


def frame_columns_back(matrix):
    key, value = ([], [])
    for m in range(MEM):
        a = 384 * m
        key += [matrix[:, a : a + 128], matrix[:, a + 256 : a + 320]]
        value += [matrix[:, a + 128 : a + 256], matrix[:, a + 320 : a + 384]]
    return [jnp.concatenate(key, axis=1), jnp.concatenate(value, axis=1)]


def head_rows(matrix):
    zero = jnp.zeros((64, matrix.shape[1]), matrix.dtype)
    parts = []
    for m in range(MEM):
        parts += [matrix[192 * m : 192 * m + 192], zero]
    return jnp.concatenate(parts, axis=0)


def head_rows_back(matrix):
    return jnp.concatenate([matrix[256 * m : 256 * m + 192] for m in range(MEM)], axis=0)


def up_columns(matrix, devices):
    rows = matrix.shape[0]
    part = D // devices
    return matrix.reshape(rows, devices, 4, part).transpose(0, 2, 1, 3).reshape(rows, FF)


def up_columns_back(matrix, devices):
    rows = matrix.shape[0]
    part = D // devices
    return matrix.reshape(rows, 4, devices, part).transpose(0, 2, 1, 3).reshape(rows, FF)


def down_columns(matrix):
    part = matrix.shape[0] // 4
    return jnp.concatenate([matrix[c * part : (c + 1) * part] for c in range(4)], axis=1)


def down_columns_back(matrix):
    return jnp.concatenate([matrix[:, c * D : (c + 1) * D] for c in range(4)], axis=0)


def gather(matrix):
    return lax.all_gather(matrix, ALL, axis=0, tiled=True)


def scatter(matrix):
    return lax.psum_scatter(matrix, ALL, scatter_dimension=0, tiled=True).astype(F32)


def shards(
    tokens, frames, document_starts, cotangent,
    gain_self, gain_cross, gain_feed, gain_final,
    self_query, self_key, self_value, self_output,
    cross_query, cross_key, cross_value, cross_output,
    feed_up, feed_down,
):
    devices = lax.axis_size("fsdp") * lax.axis_size("grp") * MEM
    group, member = (lax.axis_index("grp"), lax.axis_index("mem"))
    groups = lax.axis_size("grp")
    starts = document_starts[0]
    inner = starts - SPAN * jnp.arange(groups, dtype=jnp.int32)
    late = jnp.concatenate([inner[1:], jnp.zeros((1,), jnp.int32)])
    scal = jnp.stack([
        member, member ^ 1, member ^ 2, member ^ 3,
        lax.dynamic_index_in_dim(inner, group, keepdims=False),
        lax.dynamic_index_in_dim(late, group, keepdims=False),
        member, member,
    ]).astype(jnp.int32)

    part = D // devices
    gains = jnp.stack([gain_self, gain_cross, gain_feed, gain_final], axis=1)
    gains = jnp.pad(gains, ((0, 0), (0, 124)))
    first = gather(jnp.concatenate([self_columns(self_query, self_key, self_value), gains], axis=1))
    second = gather(jnp.concatenate(
        [self_output, cross_output, query_columns(cross_query), frame_columns(cross_key, cross_value)], axis=1))
    third = gather(jnp.concatenate([up_columns(feed_up, devices), down_columns(feed_down)], axis=1))

    w_self = first[:, :2560]
    gain_rows = first[:, 2560:].T.astype(F32)
    w_so, w_co = (head_rows(second[:, :D]), head_rows(second[:, D : 2 * D]))
    w_cq, w_kv = (second[:, 1536:2560], second[:, 2560:])
    w_up = third[:, :FF]
    w_down = [third[:, FF + c * D : FF + (c + 1) * D] for c in range(4)]

    states = tokens.astype(F32)
    normed_self, back_self = jax.vjp(normalize, states, gain_rows[0])
    normed_self = normed_self.astype(BF)
    projected = product(normed_self, w_self).astype(BF)
    self_pieces = with_tail(member, spread(member, projected, 640))
    frame_rows = product(frames, w_kv).astype(BF)
    frame_pieces = spread(member, frame_rows, 384)

    mixed, self_kept = self_forward(scal, self_pieces)
    self_heads = collect(member, mixed)
    first_sum = states + product(self_heads, w_so)
    normed_cross, back_cross = jax.vjp(normalize, first_sum, gain_rows[1])
    normed_cross = normed_cross.astype(BF)
    cross_queries = product(normed_cross, w_cq).astype(BF)
    cross_pieces = with_tail(member, spread(member, cross_queries, 256))
    mixed, cross_kept = cross_forward(scal, cross_pieces, frame_pieces)
    cross_heads = collect(member, mixed)
    second_sum = first_sum + product(cross_heads, w_co)
    normed_feed, back_feed = jax.vjp(normalize, second_sum, gain_rows[2])
    normed_feed = normed_feed.astype(BF)
    inner_units = product(normed_feed, w_up)
    activated, back_gelu = jax.vjp(exact_gelu, inner_units)
    hidden = activated.astype(BF)
    third_sum = second_sum
    for c in range(4):
        third_sum = third_sum + product(hidden[:, c * D : (c + 1) * D], w_down[c])
    result, back_final = jax.vjp(normalize, third_sum, gain_rows[3])

    grad_third, grad_gain_final = back_final(cotangent.astype(F32))
    grad_feed_out = grad_third.astype(BF)
    grad_inner = jnp.concatenate([product_right(grad_feed_out, w_down[c]) for c in range(4)], axis=1)
    (grad_inner,) = back_gelu(grad_inner)
    grad_inner = grad_inner.astype(BF)
    grad_up = product_left(normed_feed, grad_inner).astype(BF)
    grad_down = [product_left(hidden[:, c * D : (c + 1) * D], grad_feed_out).astype(BF) for c in range(4)]
    sums_feed = scatter(jnp.concatenate([grad_up, *grad_down], axis=1))
    grad_second_part, grad_gain_feed = back_feed(product_right(grad_inner, w_up))
    grad_second = grad_third + grad_second_part

    grad_cross_out = grad_second.astype(BF)
    grad_cross_heads = product_right(grad_cross_out, w_co).astype(BF)
    grad_pieces = with_tail(member, spread(member, grad_cross_heads, 256))
    grad_co = head_rows_back(product_left(cross_heads, grad_cross_out)).astype(BF)
    query_pieces, frame_grads = cross_backward(scal, cross_pieces, frame_pieces, grad_pieces, cross_kept)
    grad_cross_queries = collect(member, query_pieces)
    frame_grad = join(member, [swap(frame_grads[j], j) for j in range(MEM)])
    grad_cq = product_left(normed_cross, grad_cross_queries).astype(BF)
    grad_first_part, grad_gain_cross = back_cross(product_right(grad_cross_queries, w_cq))
    grad_first = grad_second + grad_first_part

    grad_self_out = grad_first.astype(BF)
    grad_self_heads = product_right(grad_self_out, w_so).astype(BF)
    grad_pieces = with_tail(member, spread(member, grad_self_heads, 256))
    grad_so = head_rows_back(product_left(self_heads, grad_self_out)).astype(BF)
    grad_kv = product_left(frames, frame_grad).astype(BF)
    frames_gradient = product_right(frame_grad, w_kv)
    sums_cross = scatter(jnp.concatenate([grad_so, grad_co, grad_cq, grad_kv], axis=1))
    grad_projected = collect(member, self_backward(scal, self_pieces, grad_pieces, self_kept))
    grad_qkv = product_left(normed_self, grad_projected).astype(BF)
    grad_states_part, grad_gain_self = back_self(product_right(grad_projected, w_self))
    tokens_gradient = grad_first + grad_states_part
    grad_gains = jnp.stack([grad_gain_self, grad_gain_cross, grad_gain_feed, grad_gain_final])
    grad_gains = jnp.pad(grad_gains, ((0, 124), (0, 0))).T.astype(BF)
    sums_self = scatter(jnp.concatenate([grad_qkv, grad_gains], axis=1))

    gains_out = sums_self[:, 2560:2564].T
    query, key, value = self_columns_back(sums_self[:, :2560])
    cross_k, cross_v = frame_columns_back(sums_cross[:, 2560:])
    return (
        result.astype(BF),
        tokens_gradient,
        frames_gradient,
        gains_out[0],
        gains_out[1],
        gains_out[2],
        gains_out[3],
        query,
        key,
        value,
        sums_cross[:, :D],
        query_columns_back(sums_cross[:, 1536:2560]),
        cross_k,
        cross_v,
        sums_cross[:, D : 2 * D],
        up_columns_back(sums_feed[:, :FF], devices),
        down_columns_back(sums_feed[:, FF:]),
    )


def solution(mesh):
    fsdp, ctx = (mesh.shape["fsdp"], mesh.shape["ctx"])
    fine = Mesh(mesh.devices.reshape(fsdp, ctx // MEM, MEM), ALL)
    rows, flat = (P(ALL, None), P(ALL))
    in_specs = (rows, rows, P("fsdp", None), rows) + (flat,) * 4 + (rows,) * 10
    out_specs = (rows,) * 3 + (flat,) * 4 + (rows,) * 10
    return jax.shard_map(shards, mesh=fine, in_specs=in_specs, out_specs=out_specs, check_vma=False)
```

```python
import functools

import jax
import jax.numpy as jnp
from jax import lax
from jax.experimental import pallas as pl
from jax.experimental.pallas import tpu as pltpu
from jax.sharding import Mesh, PartitionSpec as P

D = 768
HD = 64
FF = 3072
SPAN = 1024
MEM = 4
ROWS = 256
WIDE = (MEM + 1) * ROWS
HEADS = 3
FR = 375
FP = 384
KEYS = MEM * FP
NEG = -1e30
ALL = ("fsdp", "grp", "mem")
LINE = ("grp", "mem")
F32 = jnp.float32
BF = jnp.bfloat16


def normalize(states, gain):
    center = states - jnp.mean(states, axis=-1, keepdims=True)
    spread = jnp.mean(center * center, axis=-1, keepdims=True)
    return center * lax.rsqrt(spread + 1e-05) * gain


def exact_gelu(values):
    return jax.nn.gelu(values, approximate=False)


def product(left, right):
    return jnp.dot(left, right, preferred_element_type=F32)


def product_left(left, right):
    return lax.dot_general(left, right, (((0,), (0,)), ((), ())), preferred_element_type=F32)


def product_right(left, right):
    return lax.dot_general(left, right, (((1,), (1,)), ((), ())), preferred_element_type=F32)


def lanes(rows):
    return lax.broadcasted_iota(jnp.int32, (rows, 128), 1)


def head_lanes(head, rows):
    lane = lanes(rows)
    return (lane >= HD) if head == 1 else (lane < HD)


def only(head, window):
    return jnp.where(head_lanes(head, window.shape[0]), window, jnp.zeros_like(window))


def swap_halves(window):
    return pltpu.roll(window.astype(F32), HD, 1).astype(BF)


def marked(head, window, value):
    spare = 0 if head == 1 else HD
    return jnp.where(lanes(window.shape[0]) == spare, value, window)


def scaled(window):
    return (window.astype(F32) * 0.125).astype(BF)


def valid_rows(scal, first, count):
    row = first + lax.broadcasted_iota(jnp.int32, (count, 128), 0)
    return (row >= scal[4]) & (row < MEM * ROWS + scal[5])


def gather_rows(scal, pieces, tail, whole, step):
    for j in range(MEM):
        start = pl.multiple_of(scal[j] * step, step)
        whole[pl.ds(start, pieces[j].shape[0]), :] = pieces[j][...]
    if tail is not None:
        whole[pl.ds(MEM * step, tail.shape[0]), :] = tail[...]


def scatter_rows(scal, whole, pieces, tail, step):
    for j in range(MEM):
        start = pl.multiple_of(scal[j] * step, step)
        pieces[j][...] = whole[pl.ds(start, pieces[j].shape[0]), :].astype(BF)
    if tail is not None:
        tail[...] = whole[pl.ds(MEM * step, tail.shape[0]), :].astype(BF)


def self_prepare(scal, whole, qa, ka):
    hidden = lax.broadcasted_iota(jnp.int32, (WIDE, 128), 0) < scal[4]
    for head in range(HEADS):
        if head < 2:
            query, key = whole[:, 0:128], whole[:, 128:256]
        else:
            query = whole[:, 384:512]
            key = swap_halves(query)
        qa[head] = marked(head, scaled(query), jnp.asarray(NEG, BF))
        ka[head] = marked(head, only(head, key), jnp.where(hidden, 1.0, 0.0).astype(BF))


def forward_finish(scal, ot, out, outs, tail):
    ot[HEADS * HD :, :] = jnp.zeros((HD, WIDE), F32)
    for i in range(MEM + 1):
        block = ot[:, i * ROWS : (i + 1) * ROWS].T
        keep = valid_rows(scal, i * ROWS, ROWS)[:, 0:1]
        out[i * ROWS : (i + 1) * ROWS, :] = jnp.where(keep, block, 0.0).astype(BF)
    scatter_rows(scal, out, outs, tail, ROWS)


def self_forward_kernel(scal, p0, p1, p2, p3, tail, o0, o1, o2, o3, otail, ot, lse, whole, qa, ka, vt, out):
    gather_rows(scal, (p0, p1, p2, p3), tail, whole, ROWS)
    self_prepare(scal, whole, qa, ka)
    turned = whole[:, 256:384].astype(F32).T.astype(BF)
    vt[0] = turned[0:HD]
    vt[1] = turned[HD:128]
    vt[2] = whole[:, 512:640].astype(F32).T.astype(BF)[0:HD]
    causal = lax.broadcasted_iota(jnp.int32, (ROWS, ROWS), 0) <= lax.broadcasted_iota(
        jnp.int32, (ROWS, ROWS), 1
    )

    def one_head(head, carry):
        for i in range(MEM + 1):
            a, b = i * ROWS, (i + 1) * ROWS
            query = qa[head, a:b, :]
            near = jnp.where(causal, product_right(ka[head, a:b, :], query), NEG)
            top = jnp.max(near, axis=0, keepdims=True)
            if i:
                far = product_right(ka[head, 0:a, :], query)
                top = jnp.maximum(top, jnp.max(far, axis=0, keepdims=True))
                far = jnp.exp(far - top)
            near = jnp.exp(near - top)
            total = jnp.sum(near, axis=0, keepdims=True)
            if i:
                total = total + jnp.sum(far, axis=0, keepdims=True)
            scale = 1.0 / total
            mixed = product(vt[head, :, a:b], (near * scale).astype(BF))
            if i:
                mixed = mixed + product(vt[head, :, 0:a], (far * scale).astype(BF))
            ot[pl.ds(pl.multiple_of(head * HD, HD), HD), a:b] = mixed
            lse[head, 0:1, a:b] = top + jnp.log(total)
        return carry

    lax.fori_loop(0, HEADS, one_head, 0)
    forward_finish(scal, ot, out, (o0, o1, o2, o3), otail)


def grads_prepare(scal, grads, ot, dm, delta):
    for i in range(MEM + 1):
        a, b = i * ROWS, (i + 1) * ROWS
        keep = valid_rows(scal, a, ROWS)[:, 0:1]
        clean = jnp.where(keep, grads[a:b, :].astype(F32), 0.0)
        turned = clean.T * ot[:, a:b]
        clean = clean.astype(BF)
        for head in range(HEADS):
            window = clean[:, 0:128] if head < 2 else clean[:, 128:256]
            dm[head, a:b, :] = only(head, window)
            delta[head, 0:1, a:b] = jnp.sum(turned[head * HD : (head + 1) * HD], axis=0, keepdims=True)


def self_backward_kernel(
    scal, p0, p1, p2, p3, tail, g0, g1, g2, g3, gtail, ot, lse,
    d0, d1, d2, d3, dtail,
    whole, grads, qa, ka, qm, kt, vm, dm, delta, dqt, dk, dv, out,
):
    gather_rows(scal, (p0, p1, p2, p3), tail, whole, ROWS)
    gather_rows(scal, (g0, g1, g2, g3), gtail, grads, ROWS)
    self_prepare(scal, whole, qa, ka)
    grads_prepare(scal, grads, ot, dm, delta)
    turned = whole[:, 128:256].astype(F32).T.astype(BF)
    kt[0] = turned[0:HD]
    kt[1] = turned[HD:128]
    kt[2] = whole[:, 384:512].astype(F32).T.astype(BF)[HD:128]
    for head in range(HEADS):
        qm[head] = only(head, scaled(whole[:, 0:128] if head < 2 else whole[:, 384:512]))
        vm[head] = only(head, whole[:, 256:384] if head < 2 else whole[:, 512:640])
    dk[...] = jnp.zeros_like(dk)
    dv[...] = jnp.zeros_like(dv)
    dqt[HEADS * HD :, :] = jnp.zeros((HD, WIDE), F32)
    causal = lax.broadcasted_iota(jnp.int32, (ROWS, ROWS), 0) <= lax.broadcasted_iota(
        jnp.int32, (ROWS, ROWS), 1
    )

    def one_head(head, carry):
        side = jnp.where(head == 2, 1, 0)
        for i in range(MEM + 1):
            a, b = i * ROWS, (i + 1) * ROWS
            query, grad, own = qa[head, a:b, :], dm[head, a:b, :], qm[head, a:b, :]
            level, offset = lse[head, 0:1, a:b], delta[head, 0:1, a:b]
            change = jnp.zeros((HD, ROWS), F32)
            for low, high in ((a, b), (0, a)):
                if low == high:
                    continue
                scores = product_right(ka[head, low:high, :], query)
                if low == a:
                    scores = jnp.where(causal, scores, NEG)
                probs = jnp.exp(scores - level)
                slopes = product_right(vm[head, low:high, :], grad)
                slopes = (probs * (slopes - offset)).astype(BF)
                dv[side, low:high, :] += product(probs.astype(BF), grad)
                dk[side, low:high, :] += product(slopes, own)
                change = change + product(kt[head, :, low:high], slopes)
            dqt[pl.ds(pl.multiple_of(head * HD, HD), HD), a:b] = change * 0.125
        return carry

    lax.fori_loop(0, HEADS, one_head, 0)
    for i in range(MEM + 1):
        a, b = i * ROWS, (i + 1) * ROWS
        query = dqt[:, a:b].T
        out[a:b, 0:128] = query[:, 0:128].astype(BF)
        out[a:b, 128:256] = dk[0, a:b, :].astype(BF)
        out[a:b, 256:384] = dv[0, a:b, :].astype(BF)
        out[a:b, 384:512] = (query[:, 128:256] + pltpu.roll(dk[1, a:b, :], HD, 1)).astype(BF)
        out[a:b, 512:640] = dv[1, a:b, :].astype(BF)
    scatter_rows(scal, out, (d0, d1, d2, d3), dtail, ROWS)


def cross_prepare(whole, queries, qa, ka):
    spare = (lax.broadcasted_iota(jnp.int32, (KEYS, 128), 0) % FP) >= FR
    for head in range(HEADS):
        query = queries[:, 0:128] if head < 2 else queries[:, 128:256]
        key = whole[:, 0:128] if head < 2 else whole[:, 256:384]
        qa[head] = marked(head, scaled(query), jnp.asarray(NEG, BF))
        ka[head] = marked(head, only(head, key), jnp.where(spare, 1.0, 0.0).astype(BF))


def cross_forward_kernel(
    scal, q0, q1, q2, q3, qtail, f0, f1, f2, f3,
    o0, o1, o2, o3, otail, ot, lse,
    whole, queries, qa, ka, vt, out,
):
    whole[...] = jnp.zeros_like(whole)
    gather_rows(scal, (f0, f1, f2, f3), None, whole, FP)
    gather_rows(scal, (q0, q1, q2, q3), qtail, queries, ROWS)
    cross_prepare(whole, queries, qa, ka)
    turned = whole[:, 128:256].astype(F32).T.astype(BF)
    vt[0] = turned[0:HD]
    vt[1] = turned[HD:128]
    vt[2] = whole[:, 256:384].astype(F32).T.astype(BF)[HD:128]

    def one_head(head, carry):
        for i in range(MEM + 1):
            a, b = i * ROWS, (i + 1) * ROWS
            scores = product_right(ka[head], qa[head, a:b, :])
            top = jnp.max(scores, axis=0, keepdims=True)
            scores = jnp.exp(scores - top)
            total = jnp.sum(scores, axis=0, keepdims=True)
            mixed = product(vt[head], (scores * (1.0 / total)).astype(BF))
            ot[pl.ds(pl.multiple_of(head * HD, HD), HD), a:b] = mixed
            lse[head, 0:1, a:b] = top + jnp.log(total)
        return carry

    lax.fori_loop(0, HEADS, one_head, 0)
    forward_finish(scal, ot, out, (o0, o1, o2, o3), otail)


def cross_backward_kernel(
    scal, q0, q1, q2, q3, qtail, f0, f1, f2, f3, g0, g1, g2, g3, gtail, ot, lse,
    d0, d1, d2, d3, dtail, e0, e1, e2, e3,
    whole, queries, grads, qa, ka, qm, kt, vm, dm, delta, dqt, dk, dv, out, fout,
):
    whole[...] = jnp.zeros_like(whole)
    gather_rows(scal, (f0, f1, f2, f3), None, whole, FP)
    gather_rows(scal, (q0, q1, q2, q3), qtail, queries, ROWS)
    gather_rows(scal, (g0, g1, g2, g3), gtail, grads, ROWS)
    cross_prepare(whole, queries, qa, ka)
    grads_prepare(scal, grads, ot, dm, delta)
    turned = whole[:, 0:128].astype(F32).T.astype(BF)
    kt[0] = turned[0:HD]
    kt[1] = turned[HD:128]
    kt[2] = whole[:, 256:384].astype(F32).T.astype(BF)[0:HD]
    for head in range(HEADS):
        qm[head] = only(head, scaled(queries[:, 0:128] if head < 2 else queries[:, 128:256]))
        vm[head] = only(head, whole[:, 128:256] if head < 2 else swap_halves(whole[:, 256:384]))
    dk[...] = jnp.zeros_like(dk)
    dv[...] = jnp.zeros_like(dv)
    dqt[HEADS * HD :, :] = jnp.zeros((HD, WIDE), F32)

    def one_head(head, carry):
        side = jnp.where(head == 2, 1, 0)
        for i in range(MEM + 1):
            a, b = i * ROWS, (i + 1) * ROWS
            grad = dm[head, a:b, :]
            scores = product_right(ka[head], qa[head, a:b, :])
            probs = jnp.exp(scores - lse[head, 0:1, a:b])
            slopes = product_right(vm[head], grad)
            slopes = (probs * (slopes - delta[head, 0:1, a:b])).astype(BF)
            dv[side] += product(probs.astype(BF), grad)
            dk[side] += product(slopes, qm[head, a:b, :])
            change = product(kt[head], slopes)
            dqt[pl.ds(pl.multiple_of(head * HD, HD), HD), a:b] = change * 0.125
        return carry

    lax.fori_loop(0, HEADS, one_head, 0)
    for i in range(MEM + 1):
        a, b = i * ROWS, (i + 1) * ROWS
        out[a:b, :] = dqt[:, a:b].T.astype(BF)
    scatter_rows(scal, out, (d0, d1, d2, d3), dtail, ROWS)
    fout[:, 0:128] = dk[0].astype(BF)
    fout[:, 128:256] = dv[0].astype(BF)
    fout[:, 256:384] = (dk[1] + pltpu.roll(dv[1], HD, 1)).astype(BF)
    scatter_rows(scal, fout, (e0, e1, e2, e3), None, FP)


def shape(*dims, dtype=BF):
    return jax.ShapeDtypeStruct(dims, dtype)


def vmem(*dims, dtype=BF):
    return pltpu.VMEM(dims, dtype)


def call(kernel, scal, args, outs, scratch, flops, exps):
    full = pl.BlockSpec(memory_space=pltpu.VMEM)
    return pl.pallas_call(
        kernel,
        out_shape=outs,
        in_specs=[pl.BlockSpec(memory_space=pltpu.SMEM)] + [full] * len(args),
        out_specs=[full] * len(outs),
        scratch_shapes=scratch,
        cost_estimate=pl.CostEstimate(flops=flops, transcendentals=exps, bytes_accessed=4 << 20),
        compiler_params=pltpu.CompilerParams(vmem_limit_bytes=60 << 20),
    )(scal, *args)


def self_forward(scal, pieces):
    outs = [shape(ROWS, 256)] * 5 + [shape(256, WIDE, dtype=F32), shape(HEADS, 8, WIDE, dtype=F32)]
    scratch = [vmem(WIDE, 640), vmem(HEADS, WIDE, 128), vmem(HEADS, WIDE, 128), vmem(HEADS, HD, WIDE), vmem(WIDE, 256)]
    got = call(self_forward_kernel, scal, pieces, outs, scratch, 3 << 30, 3 << 20)
    return (got[:5], got[5:])


def self_backward(scal, pieces, grads, kept):
    outs = [shape(ROWS, 640)] * 5
    head = vmem(HEADS, WIDE, 128)
    scratch = [
        vmem(WIDE, 640), vmem(WIDE, 256), head, head, head, vmem(HEADS, HD, WIDE), head, head,
        vmem(HEADS, 8, WIDE, dtype=F32), vmem(256, WIDE, dtype=F32),
        vmem(2, WIDE, 128, dtype=F32), vmem(2, WIDE, 128, dtype=F32), vmem(WIDE, 640),
    ]
    return call(self_backward_kernel, scal, [*pieces, *grads, *kept], outs, scratch, 8 << 30, 3 << 20)


def cross_forward(scal, queries, pieces):
    outs = [shape(ROWS, 256)] * 5 + [shape(256, WIDE, dtype=F32), shape(HEADS, 8, WIDE, dtype=F32)]
    scratch = [
        vmem(KEYS, 384), vmem(WIDE, 256), vmem(HEADS, WIDE, 128), vmem(HEADS, KEYS, 128),
        vmem(HEADS, HD, KEYS), vmem(WIDE, 256),
    ]
    got = call(cross_forward_kernel, scal, [*queries, *pieces], outs, scratch, 6 << 30, 6 << 20)
    return (got[:5], got[5:])


def cross_backward(scal, queries, pieces, grads, kept):
    outs = [shape(ROWS, 256)] * 5 + [shape(FR, 384)] * 4
    head, keys = (vmem(HEADS, WIDE, 128), vmem(HEADS, KEYS, 128))
    scratch = [
        vmem(KEYS, 384), vmem(WIDE, 256), vmem(WIDE, 256), head, keys, head, vmem(HEADS, HD, KEYS), keys, head,
        vmem(HEADS, 8, WIDE, dtype=F32), vmem(256, WIDE, dtype=F32),
        vmem(2, KEYS, 128, dtype=F32), vmem(2, KEYS, 128, dtype=F32), vmem(WIDE, 256), vmem(KEYS, 384),
    ]
    got = call(cross_backward_kernel, scal, [*queries, *pieces, *grads, *kept], outs, scratch, 16 << 30, 6 << 20)
    return (got[:5], got[5:])


def swap(value, mask):
    if mask == 0:
        return value
    count = lax.axis_size("grp") * MEM
    return lax.ppermute(value, LINE, [(s, s ^ mask) for s in range(count)])


def to_previous(value):
    count = lax.axis_size("grp") * MEM
    return lax.ppermute(value, LINE, [(s, s - MEM) for s in range(MEM, count)])


def to_next(value):
    count = lax.axis_size("grp") * MEM
    return lax.ppermute(value, LINE, [(s, s + MEM) for s in range(count - MEM)])


def spread(member, rows, width):
    return [
        swap(lax.dynamic_slice_in_dim(rows, (member ^ j) * width, width, axis=1), j)
        for j in range(MEM)
    ]


def with_tail(member, pieces):
    return [*pieces, to_previous(lax.select_n(member, *pieces))]


def join(member, pieces):
    return jnp.concatenate(
        [lax.select_n(member, *[pieces[s ^ m] for m in range(MEM)]) for s in range(MEM)], axis=1
    )


def collect(member, pieces):
    late = to_next(pieces[4])
    whole = []
    for j in range(MEM):
        piece = pieces[j].astype(F32) + jnp.where(member == j, late.astype(F32), 0.0)
        whole.append(swap(piece.astype(BF), j))
    return join(member, whole)


def self_columns(query, key, value):
    parts = []
    for m in range(MEM):
        a = 192 * m
        for matrix in (query, key, value):
            parts.append(matrix[:, a : a + 128])
        parts += [query[:, a + 128 : a + 192], key[:, a + 128 : a + 192], value[:, a + 128 : a + 192]]
        parts.append(jnp.zeros((query.shape[0], 64), query.dtype))
    return jnp.concatenate(parts, axis=1)


def self_columns_back(matrix):
    parts = [[], [], []]
    for m in range(MEM):
        a = 640 * m
        for n in range(3):
            parts[n] += [matrix[:, a + 128 * n : a + 128 * n + 128], matrix[:, a + 384 + 64 * n : a + 448 + 64 * n]]
    return [jnp.concatenate(part, axis=1) for part in parts]


def query_columns(matrix):
    zero = jnp.zeros((matrix.shape[0], 64), matrix.dtype)
    parts = []
    for m in range(MEM):
        parts += [matrix[:, 192 * m : 192 * m + 192], zero]
    return jnp.concatenate(parts, axis=1)


def query_columns_back(matrix):
    return jnp.concatenate([matrix[:, 256 * m : 256 * m + 192] for m in range(MEM)], axis=1)


def frame_columns(key, value):
    parts = []
    for m in range(MEM):
        a = 192 * m
        parts += [key[:, a : a + 128], value[:, a : a + 128], key[:, a + 128 : a + 192], value[:, a + 128 : a + 192]]
    return jnp.concatenate(parts, axis=1)


def frame_columns_back(matrix):
    key, value = ([], [])
    for m in range(MEM):
        a = 384 * m
        key += [matrix[:, a : a + 128], matrix[:, a + 256 : a + 320]]
        value += [matrix[:, a + 128 : a + 256], matrix[:, a + 320 : a + 384]]
    return [jnp.concatenate(key, axis=1), jnp.concatenate(value, axis=1)]


def head_rows(matrix):
    zero = jnp.zeros((64, matrix.shape[1]), matrix.dtype)
    parts = []
    for m in range(MEM):
        parts += [matrix[192 * m : 192 * m + 192], zero]
    return jnp.concatenate(parts, axis=0)


def head_rows_back(matrix):
    return jnp.concatenate([matrix[256 * m : 256 * m + 192] for m in range(MEM)], axis=0)


def up_columns(matrix, devices):
    rows = matrix.shape[0]
    part = D // devices
    return matrix.reshape(rows, devices, 4, part).transpose(0, 2, 1, 3).reshape(rows, FF)


def up_columns_back(matrix, devices):
    rows = matrix.shape[0]
    part = D // devices
    return matrix.reshape(rows, 4, devices, part).transpose(0, 2, 1, 3).reshape(rows, FF)


def down_columns(matrix):
    part = matrix.shape[0] // 4
    return jnp.concatenate([matrix[c * part : (c + 1) * part] for c in range(4)], axis=1)


def down_columns_back(matrix):
    return jnp.concatenate([matrix[:, c * D : (c + 1) * D] for c in range(4)], axis=0)


def gather(matrix):
    return lax.all_gather(matrix, ALL, axis=0, tiled=True)


def halve(matrix, turned):
    devices = lax.axis_size("fsdp") * lax.axis_size("grp") * MEM
    bits = devices.bit_length() - 1
    outer = [bits - 1, bits - 2] if turned else [bits - 2, bits - 1]
    order = [0, *outer, *range(1, bits - 2)]
    here = lax.axis_index(ALL)
    value = matrix.reshape([2] * bits + [matrix.shape[0] // devices, matrix.shape[1]])
    left = list(range(bits - 1, -1, -1))
    for bit in order:
        axis = left.index(bit)
        mine = (here >> bit) & 1
        away = lax.dynamic_index_in_dim(value, 1 - mine, axis, keepdims=False)
        kept = lax.dynamic_index_in_dim(value, mine, axis, keepdims=False)
        came = lax.ppermute(away, ALL, [(s, s ^ (1 << bit)) for s in range(devices)])
        value = kept.astype(F32) + came.astype(F32)
        if bit != order[-1]:
            value = value.astype(BF)
        left.remove(bit)
    return value


def shards(
    tokens, frames, document_starts, cotangent,
    gain_self, gain_cross, gain_feed, gain_final,
    self_query, self_key, self_value, self_output,
    cross_query, cross_key, cross_value, cross_output,
    feed_up, feed_down,
):
    devices = lax.axis_size("fsdp") * lax.axis_size("grp") * MEM
    group, member = (lax.axis_index("grp"), lax.axis_index("mem"))
    groups = lax.axis_size("grp")
    starts = document_starts[0]
    inner = starts - SPAN * jnp.arange(groups, dtype=jnp.int32)
    late = jnp.concatenate([inner[1:], jnp.zeros((1,), jnp.int32)])
    scal = jnp.stack([
        member, member ^ 1, member ^ 2, member ^ 3,
        lax.dynamic_index_in_dim(inner, group, keepdims=False),
        lax.dynamic_index_in_dim(late, group, keepdims=False),
        member, member,
    ]).astype(jnp.int32)

    part = D // devices
    gains = jnp.stack([gain_self, gain_cross, gain_feed, gain_final], axis=1)
    gains = jnp.pad(gains, ((0, 0), (0, 124)))
    first = gather(jnp.concatenate([self_columns(self_query, self_key, self_value), gains], axis=1))
    second = gather(jnp.concatenate(
        [self_output, cross_output, query_columns(cross_query), frame_columns(cross_key, cross_value)], axis=1))
    third = gather(jnp.concatenate([up_columns(feed_up, devices), down_columns(feed_down)], axis=1))

    w_self = first[:, :2560]
    gain_rows = first[:, 2560:].T.astype(F32)
    w_so, w_co = (head_rows(second[:, :D]), head_rows(second[:, D : 2 * D]))
    w_cq, w_kv = (second[:, 1536:2560], second[:, 2560:])
    w_up = third[:, :FF]
    w_down = [third[:, FF + c * D : FF + (c + 1) * D] for c in range(4)]

    states = tokens.astype(F32)
    normed_self, back_self = jax.vjp(normalize, states, gain_rows[0])
    normed_self = normed_self.astype(BF)
    projected = product(normed_self, w_self).astype(BF)
    self_pieces = with_tail(member, spread(member, projected, 640))
    frame_rows = product(frames, w_kv).astype(BF)
    frame_pieces = spread(member, frame_rows, 384)

    mixed, self_kept = self_forward(scal, self_pieces)
    self_heads = collect(member, mixed)
    first_sum = states + product(self_heads, w_so)
    normed_cross, back_cross = jax.vjp(normalize, first_sum, gain_rows[1])
    normed_cross = normed_cross.astype(BF)
    cross_queries = product(normed_cross, w_cq).astype(BF)
    cross_pieces = with_tail(member, spread(member, cross_queries, 256))
    mixed, cross_kept = cross_forward(scal, cross_pieces, frame_pieces)
    cross_heads = collect(member, mixed)
    second_sum = first_sum + product(cross_heads, w_co)
    normed_feed, back_feed = jax.vjp(normalize, second_sum, gain_rows[2])
    normed_feed = normed_feed.astype(BF)
    inner_units = product(normed_feed, w_up)
    activated, back_gelu = jax.vjp(exact_gelu, inner_units)
    hidden = activated.astype(BF)
    third_sum = second_sum
    for c in range(4):
        third_sum = third_sum + product(hidden[:, c * D : (c + 1) * D], w_down[c])
    result, back_final = jax.vjp(normalize, third_sum, gain_rows[3])

    grad_third, grad_gain_final = back_final(cotangent.astype(F32))
    grad_feed_out = grad_third.astype(BF)
    grad_inner = jnp.concatenate([product_right(grad_feed_out, w_down[c]) for c in range(4)], axis=1)
    (grad_inner,) = back_gelu(grad_inner)
    grad_inner = grad_inner.astype(BF)
    grad_up = product_left(normed_feed, grad_inner).astype(BF)
    grad_down = [product_left(hidden[:, c * D : (c + 1) * D], grad_feed_out).astype(BF) for c in range(4)]
    sums_up = halve(grad_up, False)
    sums_down = halve(jnp.concatenate(grad_down, axis=1), True)
    grad_second_part, grad_gain_feed = back_feed(product_right(grad_inner, w_up))
    grad_second = grad_third + grad_second_part

    grad_cross_out = grad_second.astype(BF)
    grad_cross_heads = product_right(grad_cross_out, w_co).astype(BF)
    grad_pieces = with_tail(member, spread(member, grad_cross_heads, 256))
    grad_co = head_rows_back(product_left(cross_heads, grad_cross_out)).astype(BF)
    query_pieces, frame_grads = cross_backward(scal, cross_pieces, frame_pieces, grad_pieces, cross_kept)
    grad_cross_queries = collect(member, query_pieces)
    frame_grad = join(member, [swap(frame_grads[j], j) for j in range(MEM)])
    grad_cq = product_left(normed_cross, grad_cross_queries).astype(BF)
    grad_first_part, grad_gain_cross = back_cross(product_right(grad_cross_queries, w_cq))
    grad_first = grad_second + grad_first_part

    grad_self_out = grad_first.astype(BF)
    grad_self_heads = product_right(grad_self_out, w_so).astype(BF)
    grad_pieces = with_tail(member, spread(member, grad_self_heads, 256))
    grad_so = head_rows_back(product_left(self_heads, grad_self_out)).astype(BF)
    grad_kv = product_left(frames, frame_grad).astype(BF)
    frames_gradient = product_right(frame_grad, w_kv)
    sums_out = halve(jnp.concatenate([grad_so, grad_co, grad_cq], axis=1), False)
    sums_kv = halve(grad_kv, True)
    grad_projected = collect(member, self_backward(scal, self_pieces, grad_pieces, self_kept))
    grad_qkv = product_left(normed_self, grad_projected).astype(BF)
    grad_states_part, grad_gain_self = back_self(product_right(grad_projected, w_self))
    tokens_gradient = grad_first + grad_states_part
    grad_gains = jnp.stack([grad_gain_self, grad_gain_cross, grad_gain_feed, grad_gain_final])
    grad_gains = jnp.pad(grad_gains, ((0, 124), (0, 0))).T.astype(BF)
    sums_self = halve(grad_qkv[:, :1280], False)
    sums_rest = halve(jnp.concatenate([grad_qkv[:, 1280:], grad_gains], axis=1), True)

    gains_out = sums_rest[:, 1280:1284].T
    query, key, value = self_columns_back(jnp.concatenate([sums_self, sums_rest[:, :1280]], axis=1))
    cross_k, cross_v = frame_columns_back(sums_kv)
    return (
        result.astype(BF),
        tokens_gradient,
        frames_gradient,
        gains_out[0],
        gains_out[1],
        gains_out[2],
        gains_out[3],
        query,
        key,
        value,
        sums_out[:, :D],
        query_columns_back(sums_out[:, 1536:]),
        cross_k,
        cross_v,
        sums_out[:, D : 2 * D],
        up_columns_back(sums_up, devices),
        down_columns_back(sums_down),
    )


def solution(mesh):
    fsdp, ctx = (mesh.shape["fsdp"], mesh.shape["ctx"])
    fine = Mesh(mesh.devices.reshape(fsdp, ctx // MEM, MEM), ALL)
    rows, flat = (P(ALL, None), P(ALL))
    in_specs = (rows, rows, P("fsdp", None), rows) + (flat,) * 4 + (rows,) * 10
    out_specs = (rows,) * 3 + (flat,) * 4 + (rows,) * 10
    return jax.shard_map(shards, mesh=fine, in_specs=in_specs, out_specs=out_specs, check_vma=False)
```

```python
import functools

import jax
import jax.numpy as jnp
from jax import lax
from jax.experimental import pallas as pl
from jax.experimental.pallas import tpu as pltpu
from jax.sharding import Mesh, PartitionSpec as P

D = 768
HD = 64
FF = 3072
SPAN = 1024
MEM = 4
ROWS = 256
WIDE = (MEM + 1) * ROWS
HEADS = 3
FR = 375
FP = 384
KEYS = MEM * FP
NEG = -1e30
ALL = ("fsdp", "grp", "mem")
LINE = ("grp", "mem")
F32 = jnp.float32
BF = jnp.bfloat16


def normalize(states, gain):
    center = states - jnp.mean(states, axis=-1, keepdims=True)
    spread = jnp.mean(center * center, axis=-1, keepdims=True)
    return center * lax.rsqrt(spread + 1e-05) * gain


def exact_gelu(values):
    return jax.nn.gelu(values, approximate=False)


def product(left, right):
    return jnp.dot(left, right, preferred_element_type=F32)


def product_left(left, right):
    return lax.dot_general(left, right, (((0,), (0,)), ((), ())), preferred_element_type=F32)


def product_right(left, right):
    return lax.dot_general(left, right, (((1,), (1,)), ((), ())), preferred_element_type=F32)


def lanes(rows):
    return lax.broadcasted_iota(jnp.int32, (rows, 128), 1)


def head_lanes(head, rows):
    lane = lanes(rows)
    return (lane >= HD) if head == 1 else (lane < HD)


def only(head, window):
    return jnp.where(head_lanes(head, window.shape[0]), window, jnp.zeros_like(window))


def swap_halves(window):
    return pltpu.roll(window.astype(F32), HD, 1).astype(BF)


def marked(head, window, value):
    spare = 0 if head == 1 else HD
    return jnp.where(lanes(window.shape[0]) == spare, value, window)


def scaled(window):
    return (window.astype(F32) * 0.125).astype(BF)


def valid_rows(scal, first, count):
    row = first + lax.broadcasted_iota(jnp.int32, (count, 128), 0)
    return (row >= scal[4]) & (row < MEM * ROWS + scal[5])


def gather_rows(scal, pieces, tail, whole, step):
    for j in range(MEM):
        start = pl.multiple_of(scal[j] * step, step)
        whole[pl.ds(start, pieces[j].shape[0]), :] = pieces[j][...]
    if tail is not None:
        whole[pl.ds(MEM * step, tail.shape[0]), :] = tail[...]


def parts_of(ref):
    return [ref.at[j * ROWS : (j + 1) * ROWS] for j in range(MEM + 1)]


def scatter_rows(scal, whole, pieces, tail, step):
    for j in range(MEM):
        start = pl.multiple_of(scal[j] * step, step)
        pieces[j][...] = whole[pl.ds(start, pieces[j].shape[0]), :].astype(BF)
    if tail is not None:
        tail[...] = whole[pl.ds(MEM * step, tail.shape[0]), :].astype(BF)


def self_prepare(scal, whole, qa, ka):
    hidden = lax.broadcasted_iota(jnp.int32, (WIDE, 128), 0) < scal[4]
    for head in range(HEADS):
        if head < 2:
            query, key = whole[:, 0:128], whole[:, 128:256]
        else:
            query = whole[:, 384:512]
            key = swap_halves(query)
        qa[head] = marked(head, scaled(query), jnp.asarray(NEG, BF))
        ka[head] = marked(head, only(head, key), jnp.where(hidden, 1.0, 0.0).astype(BF))


def forward_finish(scal, ot, out, outs, tail):
    ot[HEADS * HD :, :] = jnp.zeros((HD, WIDE), F32)
    for i in range(MEM + 1):
        block = ot[:, i * ROWS : (i + 1) * ROWS].T
        keep = valid_rows(scal, i * ROWS, ROWS)[:, 0:1]
        out[i * ROWS : (i + 1) * ROWS, :] = jnp.where(keep, block, 0.0).astype(BF)
    scatter_rows(scal, out, outs, tail, ROWS)


def self_forward_kernel(scal, rows, o0, o1, o2, o3, otail, ot, lse, whole, qa, ka, vt, out):
    *pieces, tail = parts_of(rows)
    gather_rows(scal, pieces, tail, whole, ROWS)
    self_prepare(scal, whole, qa, ka)
    turned = whole[:, 256:384].astype(F32).T.astype(BF)
    vt[0] = turned[0:HD]
    vt[1] = turned[HD:128]
    vt[2] = whole[:, 512:640].astype(F32).T.astype(BF)[0:HD]
    causal = lax.broadcasted_iota(jnp.int32, (ROWS, ROWS), 0) <= lax.broadcasted_iota(
        jnp.int32, (ROWS, ROWS), 1
    )

    def one_head(head, carry):
        for i in range(MEM + 1):
            a, b = i * ROWS, (i + 1) * ROWS
            query = qa[head, a:b, :]
            near = jnp.where(causal, product_right(ka[head, a:b, :], query), NEG)
            top = jnp.max(near, axis=0, keepdims=True)
            if i:
                far = product_right(ka[head, 0:a, :], query)
                top = jnp.maximum(top, jnp.max(far, axis=0, keepdims=True))
                far = jnp.exp(far - top)
            near = jnp.exp(near - top)
            total = jnp.sum(near, axis=0, keepdims=True)
            if i:
                total = total + jnp.sum(far, axis=0, keepdims=True)
            scale = 1.0 / total
            mixed = product(vt[head, :, a:b], (near * scale).astype(BF))
            if i:
                mixed = mixed + product(vt[head, :, 0:a], (far * scale).astype(BF))
            ot[pl.ds(pl.multiple_of(head * HD, HD), HD), a:b] = mixed
            lse[head, 0:1, a:b] = top + jnp.log(total)
        return carry

    lax.fori_loop(0, HEADS, one_head, 0)
    forward_finish(scal, ot, out, (o0, o1, o2, o3), otail)


def grads_prepare(scal, grads, ot, dm, delta):
    for i in range(MEM + 1):
        a, b = i * ROWS, (i + 1) * ROWS
        keep = valid_rows(scal, a, ROWS)[:, 0:1]
        clean = jnp.where(keep, grads[a:b, :].astype(F32), 0.0)
        turned = clean.T * ot[:, a:b]
        clean = clean.astype(BF)
        for head in range(HEADS):
            window = clean[:, 0:128] if head < 2 else clean[:, 128:256]
            dm[head, a:b, :] = only(head, window)
            delta[head, 0:1, a:b] = jnp.sum(turned[head * HD : (head + 1) * HD], axis=0, keepdims=True)


def self_backward_kernel(
    scal, rows, g0, g1, g2, g3, gtail, ot, lse, drows,
    whole, grads, qa, ka, qm, kt, vm, dm, delta, dqt, dk, dv, out,
):
    *pieces, tail = parts_of(rows)
    gather_rows(scal, pieces, tail, whole, ROWS)
    gather_rows(scal, (g0, g1, g2, g3), gtail, grads, ROWS)
    self_prepare(scal, whole, qa, ka)
    grads_prepare(scal, grads, ot, dm, delta)
    turned = whole[:, 128:256].astype(F32).T.astype(BF)
    kt[0] = turned[0:HD]
    kt[1] = turned[HD:128]
    kt[2] = whole[:, 384:512].astype(F32).T.astype(BF)[HD:128]
    for head in range(HEADS):
        qm[head] = only(head, scaled(whole[:, 0:128] if head < 2 else whole[:, 384:512]))
        vm[head] = only(head, whole[:, 256:384] if head < 2 else whole[:, 512:640])
    dk[...] = jnp.zeros_like(dk)
    dv[...] = jnp.zeros_like(dv)
    dqt[HEADS * HD :, :] = jnp.zeros((HD, WIDE), F32)
    causal = lax.broadcasted_iota(jnp.int32, (ROWS, ROWS), 0) <= lax.broadcasted_iota(
        jnp.int32, (ROWS, ROWS), 1
    )

    def one_head(head, carry):
        side = jnp.where(head == 2, 1, 0)
        for i in range(MEM + 1):
            a, b = i * ROWS, (i + 1) * ROWS
            query, grad, own = qa[head, a:b, :], dm[head, a:b, :], qm[head, a:b, :]
            level, offset = lse[head, 0:1, a:b], delta[head, 0:1, a:b]
            change = jnp.zeros((HD, ROWS), F32)
            for low, high in ((a, b), (0, a)):
                if low == high:
                    continue
                scores = product_right(ka[head, low:high, :], query)
                if low == a:
                    scores = jnp.where(causal, scores, NEG)
                probs = jnp.exp(scores - level)
                slopes = product_right(vm[head, low:high, :], grad)
                slopes = (probs * (slopes - offset)).astype(BF)
                dv[side, low:high, :] += product(probs.astype(BF), grad)
                dk[side, low:high, :] += product(slopes, own)
                change = change + product(kt[head, :, low:high], slopes)
            dqt[pl.ds(pl.multiple_of(head * HD, HD), HD), a:b] = change * 0.125
        return carry

    lax.fori_loop(0, HEADS, one_head, 0)
    for i in range(MEM + 1):
        a, b = i * ROWS, (i + 1) * ROWS
        query = dqt[:, a:b].T
        out[a:b, 0:128] = query[:, 0:128].astype(BF)
        out[a:b, 128:256] = dk[0, a:b, :].astype(BF)
        out[a:b, 256:384] = dv[0, a:b, :].astype(BF)
        out[a:b, 384:512] = (query[:, 128:256] + pltpu.roll(dk[1, a:b, :], HD, 1)).astype(BF)
        out[a:b, 512:640] = dv[1, a:b, :].astype(BF)
    *pieces, tail = parts_of(drows)
    scatter_rows(scal, out, pieces, tail, ROWS)


def cross_prepare(whole, queries, qa, ka):
    spare = (lax.broadcasted_iota(jnp.int32, (KEYS, 128), 0) % FP) >= FR
    for head in range(HEADS):
        query = queries[:, 0:128] if head < 2 else queries[:, 128:256]
        key = whole[:, 0:128] if head < 2 else whole[:, 256:384]
        qa[head] = marked(head, scaled(query), jnp.asarray(NEG, BF))
        ka[head] = marked(head, only(head, key), jnp.where(spare, 1.0, 0.0).astype(BF))


def cross_forward_kernel(
    scal, q0, q1, q2, q3, qtail, f0, f1, f2, f3,
    o0, o1, o2, o3, otail, ot, lse,
    whole, queries, qa, ka, vt, out,
):
    whole[...] = jnp.zeros_like(whole)
    for j, piece in enumerate((f0, f1, f2, f3)):
        whole[j * FP : j * FP + FR, :] = piece[...]
    gather_rows(scal, (q0, q1, q2, q3), qtail, queries, ROWS)
    cross_prepare(whole, queries, qa, ka)
    turned = whole[:, 128:256].astype(F32).T.astype(BF)
    vt[0] = turned[0:HD]
    vt[1] = turned[HD:128]
    vt[2] = whole[:, 256:384].astype(F32).T.astype(BF)[HD:128]

    def one_head(head, carry):
        for i in range(MEM + 1):
            a, b = i * ROWS, (i + 1) * ROWS
            scores = product_right(ka[head], qa[head, a:b, :])
            top = jnp.max(scores, axis=0, keepdims=True)
            scores = jnp.exp(scores - top)
            total = jnp.sum(scores, axis=0, keepdims=True)
            mixed = product(vt[head], (scores * (1.0 / total)).astype(BF))
            ot[pl.ds(pl.multiple_of(head * HD, HD), HD), a:b] = mixed
            lse[head, 0:1, a:b] = top + jnp.log(total)
        return carry

    lax.fori_loop(0, HEADS, one_head, 0)
    forward_finish(scal, ot, out, (o0, o1, o2, o3), otail)


def cross_backward_kernel(
    scal, q0, q1, q2, q3, qtail, f0, f1, f2, f3, g0, g1, g2, g3, gtail, ot, lse,
    d0, d1, d2, d3, dtail, e0, e1, e2, e3,
    whole, queries, grads, qa, ka, qm, kt, vm, dm, delta, dqt, dk, dv, out, fout,
):
    whole[...] = jnp.zeros_like(whole)
    for j, piece in enumerate((f0, f1, f2, f3)):
        whole[j * FP : j * FP + FR, :] = piece[...]
    gather_rows(scal, (q0, q1, q2, q3), qtail, queries, ROWS)
    gather_rows(scal, (g0, g1, g2, g3), gtail, grads, ROWS)
    cross_prepare(whole, queries, qa, ka)
    grads_prepare(scal, grads, ot, dm, delta)
    turned = whole[:, 0:128].astype(F32).T.astype(BF)
    kt[0] = turned[0:HD]
    kt[1] = turned[HD:128]
    kt[2] = whole[:, 256:384].astype(F32).T.astype(BF)[0:HD]
    for head in range(HEADS):
        qm[head] = only(head, scaled(queries[:, 0:128] if head < 2 else queries[:, 128:256]))
        vm[head] = only(head, whole[:, 128:256] if head < 2 else swap_halves(whole[:, 256:384]))
    dk[...] = jnp.zeros_like(dk)
    dv[...] = jnp.zeros_like(dv)
    dqt[HEADS * HD :, :] = jnp.zeros((HD, WIDE), F32)

    def one_head(head, carry):
        side = jnp.where(head == 2, 1, 0)
        for i in range(MEM + 1):
            a, b = i * ROWS, (i + 1) * ROWS
            grad = dm[head, a:b, :]
            scores = product_right(ka[head], qa[head, a:b, :])
            probs = jnp.exp(scores - lse[head, 0:1, a:b])
            slopes = product_right(vm[head], grad)
            slopes = (probs * (slopes - delta[head, 0:1, a:b])).astype(BF)
            dv[side] += product(probs.astype(BF), grad)
            dk[side] += product(slopes, qm[head, a:b, :])
            change = product(kt[head], slopes)
            dqt[pl.ds(pl.multiple_of(head * HD, HD), HD), a:b] = change * 0.125
        return carry

    lax.fori_loop(0, HEADS, one_head, 0)
    for i in range(MEM + 1):
        a, b = i * ROWS, (i + 1) * ROWS
        out[a:b, :] = dqt[:, a:b].T.astype(BF)
    scatter_rows(scal, out, (d0, d1, d2, d3), dtail, ROWS)
    fout[:, 0:128] = dk[0].astype(BF)
    fout[:, 128:256] = dv[0].astype(BF)
    fout[:, 256:384] = (dk[1] + pltpu.roll(dv[1], HD, 1)).astype(BF)
    for j, piece in enumerate((e0, e1, e2, e3)):
        piece[...] = fout[j * FP : j * FP + FR, :]


def shape(*dims, dtype=BF):
    return jax.ShapeDtypeStruct(dims, dtype)


def vmem(*dims, dtype=BF):
    return pltpu.VMEM(dims, dtype)


def call(kernel, scal, args, outs, scratch, flops, exps):
    full = pl.BlockSpec(memory_space=pltpu.VMEM)
    return pl.pallas_call(
        kernel,
        out_shape=outs,
        in_specs=[pl.BlockSpec(memory_space=pltpu.SMEM)] + [full] * len(args),
        out_specs=[full] * len(outs),
        scratch_shapes=scratch,
        cost_estimate=pl.CostEstimate(flops=flops, transcendentals=exps, bytes_accessed=4 << 20),
        compiler_params=pltpu.CompilerParams(vmem_limit_bytes=60 << 20),
    )(scal, *args)


def self_forward(scal, rows):
    outs = [shape(ROWS, 256)] * 5 + [shape(256, WIDE, dtype=F32), shape(HEADS, 8, WIDE, dtype=F32)]
    scratch = [vmem(WIDE, 640), vmem(HEADS, WIDE, 128), vmem(HEADS, WIDE, 128), vmem(HEADS, HD, WIDE), vmem(WIDE, 256)]
    got = call(self_forward_kernel, scal, [rows], outs, scratch, 3 << 30, 3 << 20)
    return (got[:5], got[5:])


def self_backward(scal, rows, grads, kept):
    outs = [shape(WIDE, 640)]
    head = vmem(HEADS, WIDE, 128)
    scratch = [
        vmem(WIDE, 640), vmem(WIDE, 256), head, head, head, vmem(HEADS, HD, WIDE), head, head,
        vmem(HEADS, 8, WIDE, dtype=F32), vmem(256, WIDE, dtype=F32),
        vmem(2, WIDE, 128, dtype=F32), vmem(2, WIDE, 128, dtype=F32), vmem(WIDE, 640),
    ]
    return call(self_backward_kernel, scal, [rows, *grads, *kept], outs, scratch, 8 << 30, 3 << 20)[0]


def cross_forward(scal, queries, frames):
    outs = [shape(ROWS, 256)] * 5 + [shape(256, WIDE, dtype=F32), shape(HEADS, 8, WIDE, dtype=F32)]
    scratch = [
        vmem(KEYS, 384), vmem(WIDE, 256), vmem(HEADS, WIDE, 128), vmem(HEADS, KEYS, 128),
        vmem(HEADS, HD, KEYS), vmem(WIDE, 256),
    ]
    got = call(cross_forward_kernel, scal, [*queries, *frames], outs, scratch, 6 << 30, 6 << 20)
    return (got[:5], got[5:])


def cross_backward(scal, queries, frames, grads, kept):
    outs = [shape(ROWS, 256)] * 5 + [shape(FR, 384)] * 4
    head, keys = (vmem(HEADS, WIDE, 128), vmem(HEADS, KEYS, 128))
    scratch = [
        vmem(KEYS, 384), vmem(WIDE, 256), vmem(WIDE, 256), head, keys, head, vmem(HEADS, HD, KEYS), keys, head,
        vmem(HEADS, 8, WIDE, dtype=F32), vmem(256, WIDE, dtype=F32),
        vmem(2, KEYS, 128, dtype=F32), vmem(2, KEYS, 128, dtype=F32), vmem(WIDE, 256), vmem(KEYS, 384),
    ]
    got = call(cross_backward_kernel, scal, [*queries, *frames, *grads, *kept], outs, scratch, 16 << 30, 6 << 20)
    return (got[:5], got[5:])


def swap(value, mask):
    if mask == 0:
        return value
    count = lax.axis_size("grp") * MEM
    return lax.ppermute(value, LINE, [(s, s ^ mask) for s in range(count)])


def to_previous(value):
    count = lax.axis_size("grp") * MEM
    return lax.ppermute(value, LINE, [(s, s - MEM) for s in range(MEM, count)])


def to_next(value):
    count = lax.axis_size("grp") * MEM
    return lax.ppermute(value, LINE, [(s, s + MEM) for s in range(count - MEM)])


def spread(member, rows, width):
    return [
        swap(lax.dynamic_slice_in_dim(rows, (member ^ j) * width, width, axis=1), j)
        for j in range(MEM)
    ]


def with_tail(member, pieces):
    return [*pieces, to_previous(lax.select_n(member, *pieces))]


def token_tail(member, pieces):
    count = lax.axis_size("grp") * MEM
    even = lax.ppermute(
        lax.select_n(member, *pieces), LINE, [(s, s - MEM) for s in range(MEM, count, 2)]
    )
    odd = lax.ppermute(even, LINE, [(s, s + 1) for s in range(0, count, 2)])
    return jnp.where(member % 2 == 0, even, odd)


def total_rows(member, partial):
    core = member % 2
    half = ROWS // 2
    tail = partial[MEM * ROWS :].reshape(2, half, D)
    late = swap(lax.dynamic_index_in_dim(tail, 1 - core, keepdims=False).astype(BF), 1).astype(F32)
    late = to_next((late + lax.dynamic_index_in_dim(tail, core, keepdims=False)).astype(BF)).astype(F32)
    late = jnp.concatenate([jnp.where(core == c, late, 0.0) for c in range(2)], axis=0)
    pieces = [
        partial[j * ROWS : (j + 1) * ROWS] + jnp.where(member == j, late, 0.0) for j in range(MEM)
    ]
    other = swap(jnp.concatenate([pieces[1], pieces[3]], axis=0).astype(BF), 1).astype(F32)
    far = (pieces[2] + other[ROWS:]).astype(BF)
    return pieces[0] + other[:ROWS] + swap(far, 2).astype(F32)


def join(member, pieces):
    return jnp.concatenate(
        [lax.select_n(member, *[pieces[s ^ m] for m in range(MEM)]) for s in range(MEM)], axis=1
    )


def collect(member, pieces):
    late = to_next(pieces[4])
    whole = []
    for j in range(MEM):
        piece = pieces[j].astype(F32) + jnp.where(member == j, late.astype(F32), 0.0)
        whole.append(swap(piece.astype(BF), j))
    return join(member, whole)


def self_columns(query, key, value, gains):
    parts = []
    for m in range(MEM):
        a = 192 * m
        for matrix in (query, key, value):
            parts.append(matrix[:, a : a + 128])
        parts += [query[:, a + 128 : a + 192], key[:, a + 128 : a + 192], value[:, a + 128 : a + 192]]
        parts += [gains, jnp.zeros((query.shape[0], 60), query.dtype)]
    return jnp.concatenate(parts, axis=1)


def self_columns_back(matrix):
    parts = [[], [], []]
    for m in range(MEM):
        a = 640 * m
        for n in range(3):
            parts[n] += [matrix[:, a + 128 * n : a + 128 * n + 128], matrix[:, a + 384 + 64 * n : a + 448 + 64 * n]]
    return [jnp.concatenate(part, axis=1) for part in parts]


def query_columns(matrix):
    zero = jnp.zeros((matrix.shape[0], 64), matrix.dtype)
    parts = []
    for m in range(MEM):
        parts += [matrix[:, 192 * m : 192 * m + 192], zero]
    return jnp.concatenate(parts, axis=1)


def query_columns_back(matrix):
    return jnp.concatenate([matrix[:, 256 * m : 256 * m + 192] for m in range(MEM)], axis=1)


def frame_columns(key, value):
    parts = []
    for m in range(MEM):
        a = 192 * m
        parts += [key[:, a : a + 128], value[:, a : a + 128], key[:, a + 128 : a + 192], value[:, a + 128 : a + 192]]
    return jnp.concatenate(parts, axis=1)


def frame_columns_back(matrix):
    key, value = ([], [])
    for m in range(MEM):
        a = 384 * m
        key += [matrix[:, a : a + 128], matrix[:, a + 256 : a + 320]]
        value += [matrix[:, a + 128 : a + 256], matrix[:, a + 320 : a + 384]]
    return [jnp.concatenate(key, axis=1), jnp.concatenate(value, axis=1)]


def head_rows(matrix):
    zero = jnp.zeros((64, matrix.shape[1]), matrix.dtype)
    parts = []
    for m in range(MEM):
        parts += [matrix[192 * m : 192 * m + 192], zero]
    return jnp.concatenate(parts, axis=0)


def head_rows_back(matrix):
    return jnp.concatenate([matrix[256 * m : 256 * m + 192] for m in range(MEM)], axis=0)


def column_blocks(matrix):
    return [matrix[:, c * D : (c + 1) * D] for c in range(FF // D)]


def gather(matrix):
    return lax.all_gather(matrix, ALL, axis=0, tiled=True)


class Halving:
    def __init__(self, matrix, turned, own=False):
        self.devices = lax.axis_size("fsdp") * lax.axis_size("grp") * MEM
        bits = self.devices.bit_length() - 1
        outer = [bits - 1, bits - 2] if turned else [bits - 2, bits - 1]
        self.order = ([] if own else [0]) + outer + list(range(2 if own else 1, bits - 2))
        self.here = lax.axis_index(ALL)
        self.left = list(range(bits - 1, -1, -1))
        self.value = matrix.reshape([2] * bits + [matrix.shape[0] // self.devices, matrix.shape[1]])
        self.own = own
        self.split()

    def split(self):
        self.bit = self.order.pop(0)
        axis = self.left.index(self.bit)
        self.left.remove(self.bit)
        mine = (self.here >> self.bit) & 1
        self.away = lax.dynamic_index_in_dim(self.value, 1 - mine, axis, keepdims=False)
        self.kept = lax.dynamic_index_in_dim(self.value, mine, axis, keepdims=False)

    def send(self):
        self.came = lax.ppermute(self.away, ALL, [(s, s ^ (1 << self.bit)) for s in range(self.devices)])

    def add(self):
        self.value = self.kept.astype(F32) + self.came.astype(F32)
        if self.order or self.own:
            self.value = self.value.astype(BF)
        self.came = None
        if self.order:
            self.split()

    def on(self):
        if self.order:
            self.add()
            self.send()

    def finish(self):
        while self.order:
            self.on()
        self.add()
        return self.value


def tie(value, chains, name):
    got = lax.optimization_barrier((value, [getattr(chain, name) for chain in chains]))
    for chain, array in zip(chains, got[1]):
        setattr(chain, name, array)
    return got[0]


def gather_own(member, shard, width):
    devices = lax.axis_size("fsdp") * lax.axis_size("grp") * MEM
    here = lax.axis_index(ALL)
    pieces = spread(member, shard, width)
    value = jnp.stack([lax.select_n(member, *[pieces[s ^ m] for m in range(MEM)]) for s in range(MEM)])
    for bit in range(2, devices.bit_length() - 1):
        mine = ((here >> bit) & 1) == 0
        came = lax.ppermute(value, ALL, [(s, s ^ (1 << bit)) for s in range(devices)])
        value = jnp.concatenate([jnp.where(mine, value, came), jnp.where(mine, came, value)])
    return value.reshape(devices * shard.shape[0], width)


def own_sets(member, value):
    value = value.reshape(MEM, *value.shape[2:])
    pieces = [
        swap(lax.dynamic_index_in_dim(value, member ^ j, keepdims=False), j) for j in range(MEM)
    ]
    return [lax.select_n(member, *[pieces[s ^ m] for m in range(MEM)]).astype(F32) for s in range(MEM)]


def moments(states):
    center = states - jnp.mean(states, axis=-1, keepdims=True)
    spread_ = jnp.mean(center * center, axis=-1, keepdims=True)
    rate = lax.rsqrt(spread_ + 1e-05)
    return (center * rate, rate)


def shards(
    tokens, frames, document_starts, cotangent,
    gain_self, gain_cross, gain_feed, gain_final,
    self_query, self_key, self_value, self_output,
    cross_query, cross_key, cross_value, cross_output,
    feed_up, feed_down,
):
    devices = lax.axis_size("fsdp") * lax.axis_size("grp") * MEM
    group, member = (lax.axis_index("grp"), lax.axis_index("mem"))
    groups = lax.axis_size("grp")
    starts = document_starts[0]
    inner = starts - SPAN * jnp.arange(groups, dtype=jnp.int32)
    late = jnp.concatenate([inner[1:], jnp.zeros((1,), jnp.int32)])
    scal = jnp.stack([
        member, member ^ 1, member ^ 2, member ^ 3,
        lax.dynamic_index_in_dim(inner, group, keepdims=False),
        lax.dynamic_index_in_dim(late, group, keepdims=False),
        member, member,
    ]).astype(jnp.int32)

    gains = jnp.stack([gain_self, gain_cross, gain_feed, gain_final], axis=1)
    w_own = gather_own(member, self_columns(self_query, self_key, self_value, gains), 640)
    two = swap(tokens, 2)
    other = swap(jnp.concatenate([tokens, two], axis=0), 1)
    near_tokens = [tokens, other[:ROWS], two, other[ROWS:]]
    near_tokens = jnp.concatenate([*near_tokens, token_tail(member, near_tokens)], axis=0)
    held_frames, two = lax.optimization_barrier((frames, two))
    two = swap(held_frames, 2)
    near_frames = [frames, swap(frames, 1), two, swap(two, 1)]
    scal, near_frames = lax.optimization_barrier((scal, near_frames))
    second = gather(jnp.concatenate(
        [self_output, cross_output, query_columns(cross_query), frame_columns(cross_key, cross_value)], axis=1))
    third = gather(jnp.concatenate([*column_blocks(feed_up), feed_down], axis=0))
    third = third.reshape(devices, 2 * FF // devices, D)
    part = D // devices

    gain_rows = w_own[:, 512:].T[64:68].astype(F32)
    w_so, w_co = (head_rows(second[:, :D]), head_rows(second[:, D : 2 * D]))
    w_cq, w_kv = (second[:, 1536:2560], second[:, 2560:])
    w_up = jnp.concatenate([third[:, c * part : (c + 1) * part].reshape(D, D) for c in range(4)], axis=1)
    w_down = third[:, 4 * part :].reshape(FF, D)

    states = tokens.astype(F32)
    unit, _ = moments(near_tokens.astype(F32))
    normed_self = (unit * gain_rows[0]).astype(BF)
    self_rows = product(normed_self, w_own).astype(BF)
    mixed, self_kept = self_forward(scal, self_rows)
    own_kv = lax.dynamic_slice_in_dim(w_kv, member * 384, 384, axis=1)
    frame_rows = [product(piece, own_kv).astype(BF) for piece in near_frames]
    self_heads = collect(member, mixed)
    first_sum = states + product(self_heads, w_so)
    normed_cross, back_cross = jax.vjp(normalize, first_sum, gain_rows[1])
    normed_cross = normed_cross.astype(BF)
    cross_queries = product(normed_cross, w_cq).astype(BF)
    cross_pieces = with_tail(member, spread(member, cross_queries, 256))
    mixed, cross_kept = cross_forward(scal, cross_pieces, frame_rows)
    cross_heads = collect(member, mixed)
    second_sum = first_sum + product(cross_heads, w_co)
    normed_feed, back_feed = jax.vjp(normalize, second_sum, gain_rows[2])
    normed_feed = normed_feed.astype(BF)
    inner_units = product(normed_feed, w_up)
    activated, back_gelu = jax.vjp(exact_gelu, inner_units)
    hidden = activated.astype(BF)
    third_sum = second_sum + product(hidden, w_down)
    result, back_final = jax.vjp(normalize, third_sum, gain_rows[3])

    grad_third, grad_gain_final = back_final(cotangent.astype(F32))
    grad_feed_out = grad_third.astype(BF)
    (grad_inner,) = back_gelu(product_right(grad_feed_out, w_down))
    grad_inner = grad_inner.astype(BF)
    grad_up = product_left(normed_feed, grad_inner).astype(BF)
    grad_down = product_left(hidden, grad_feed_out).astype(BF)
    feed = [Halving(grad_up, False), Halving(grad_down, True)]
    for chain in feed:
        chain.send()
    grad_second_part, grad_gain_feed = back_feed(product_right(grad_inner, w_up))
    grad_second = grad_third + grad_second_part

    grad_cross_out = grad_second.astype(BF)
    grad_cross_heads = product_right(grad_cross_out, w_co).astype(BF)
    grad_pieces = with_tail(member, spread(member, grad_cross_heads, 256))
    for chain in feed:
        chain.add()
    held = tie(scal, feed, "away")
    for chain in feed:
        chain.send()
    query_pieces, frame_grads = cross_backward(held, cross_pieces, frame_rows, grad_pieces, cross_kept)
    query_pieces = tie(query_pieces, feed, "came")
    for chain in feed:
        chain.on()
    grad_cross_queries = collect(member, query_pieces)
    grad_cross_queries = tie(grad_cross_queries, feed, "came")
    for chain in feed:
        chain.on()
    grad_cq = product_left(normed_cross, grad_cross_queries).astype(BF)
    grad_first_part, grad_gain_cross = back_cross(product_right(grad_cross_queries, w_cq))
    grad_first = grad_second + grad_first_part

    grad_self_out = grad_first.astype(BF)
    grad_self_heads = product_right(grad_self_out, w_so).astype(BF)
    grad_pieces = with_tail(member, spread(member, grad_self_heads, 256))
    grad_co = head_rows_back(product_left(cross_heads, grad_cross_out)).astype(BF)
    grad_so = head_rows_back(product_left(self_heads, grad_self_out)).astype(BF)
    grad_kv = sum(product_left(near_frames[j], frame_grads[j]) for j in range(MEM)).astype(BF)
    rest = [
        Halving(jnp.concatenate([grad_so, grad_cq[:, :512]], axis=1), False),
        Halving(jnp.concatenate([grad_co, grad_cq[:, 512:]], axis=1), True),
        Halving(grad_kv, True, True),
    ]
    held = tie(scal, rest, "away")
    for chain in rest:
        chain.send()
    for chain in feed:
        chain.add()
    held = tie(held, feed, "away")
    for chain in feed:
        chain.send()
    grad_rows = self_backward(held, self_rows, grad_pieces, self_kept)
    grad_rows = tie(grad_rows, [*rest, *feed], "came")
    for chain in rest:
        chain.on()
    grad_normed = product_right(grad_rows, w_own)
    grad_gain_self = jnp.sum(grad_normed * unit, axis=0)
    grad_gains = jnp.stack([grad_gain_self, grad_gain_cross, grad_gain_feed, grad_gain_final])
    grad_gains = jnp.pad(grad_gains, ((64, 60), (0, 0))).T
    grad_qkv = product_left(normed_self, grad_rows)
    grad_qkv = jnp.concatenate([grad_qkv[:, :512], grad_qkv[:, 512:] + grad_gains], axis=1).astype(BF)
    own = Halving(grad_qkv, False, True)
    own.send()
    total = total_rows(member, grad_normed)
    _, back_self = jax.vjp(normalize, states, gain_rows[0])
    tokens_gradient = grad_first + back_self(total)[0]
    frame_grad = join(member, [swap(frame_grads[j], j) for j in range(MEM)])
    frames_gradient = product_right(frame_grad, w_kv)

    sums_up, sums_down = [chain.finish() for chain in feed]
    for _ in range(8):
        for chain in (*rest, own):
            chain.on()
    sums_out, sums_mix, kv = [chain.finish() for chain in rest]
    sets = own_sets(member, jnp.concatenate([own.finish(), kv], axis=-1))
    gains_out = sum(part[:, 576:580] for part in sets).T
    query, key, value = self_columns_back(jnp.concatenate([part[:, :640] for part in sets], axis=1))
    cross_k, cross_v = frame_columns_back(jnp.concatenate([part[:, 640:] for part in sets], axis=1))
    grad_cq = jnp.concatenate([sums_out[:, D:], sums_mix[:, D:]], axis=1)
    return (
        result.astype(BF),
        tokens_gradient,
        frames_gradient,
        gains_out[0],
        gains_out[1],
        gains_out[2],
        gains_out[3],
        query,
        key,
        value,
        sums_out[:, :D],
        query_columns_back(grad_cq),
        cross_k,
        cross_v,
        sums_mix[:, :D],
        sums_up,
        sums_down,
    )


def solution(mesh):
    fsdp, ctx = (mesh.shape["fsdp"], mesh.shape["ctx"])
    fine = Mesh(mesh.devices.reshape(fsdp, ctx // MEM, MEM), ALL)
    rows, flat = (P(ALL, None), P(ALL))
    in_specs = (rows, rows, P("fsdp", None), rows) + (flat,) * 4 + (rows,) * 10
    out_specs = (rows,) * 3 + (flat,) * 4 + (rows,) * 10
    return jax.shard_map(shards, mesh=fine, in_specs=in_specs, out_specs=out_specs, check_vma=False)
```

```python
import functools

import jax
import jax.numpy as jnp
from jax import lax
from jax.experimental import pallas as pl
from jax.experimental.pallas import tpu as pltpu
from jax.sharding import Mesh, PartitionSpec as P

D = 768
HD = 64
FF = 3072
SPAN = 1024
MEM = 4
ROWS = 256
WIDE = (MEM + 1) * ROWS
HEADS = 3
FR = 375
FP = 384
KEYS = MEM * FP
NEG = -1e30
ALL = ("fsdp", "grp", "mem")
LINE = ("grp", "mem")
F32 = jnp.float32
BF = jnp.bfloat16


def normalize(states, gain):
    center = states - jnp.mean(states, axis=-1, keepdims=True)
    spread = jnp.mean(center * center, axis=-1, keepdims=True)
    return center * lax.rsqrt(spread + 1e-05) * gain


def exact_gelu(values):
    return jax.nn.gelu(values, approximate=False)


def product(left, right):
    return jnp.dot(left, right, preferred_element_type=F32)


def product_left(left, right):
    return lax.dot_general(left, right, (((0,), (0,)), ((), ())), preferred_element_type=F32)


def product_right(left, right):
    return lax.dot_general(left, right, (((1,), (1,)), ((), ())), preferred_element_type=F32)


def lanes(rows):
    return lax.broadcasted_iota(jnp.int32, (rows, 128), 1)


def head_lanes(head, rows):
    lane = lanes(rows)
    return (lane >= HD) if head == 1 else (lane < HD)


def only(head, window):
    return jnp.where(head_lanes(head, window.shape[0]), window, jnp.zeros_like(window))


def swap_halves(window):
    return pltpu.roll(window.astype(F32), HD, 1).astype(BF)


def marked(head, window, value):
    spare = 0 if head == 1 else HD
    return jnp.where(lanes(window.shape[0]) == spare, value, window)


def scaled(window):
    return (window.astype(F32) * 0.125).astype(BF)


def valid_rows(scal, first, count):
    row = first + lax.broadcasted_iota(jnp.int32, (count, 128), 0)
    return (row >= scal[4]) & (row < MEM * ROWS + scal[5])


def gather_rows(scal, pieces, tail, whole, step):
    for j in range(MEM):
        start = pl.multiple_of(scal[j] * step, step)
        whole[pl.ds(start, pieces[j].shape[0]), :] = pieces[j][...]
    if tail is not None:
        whole[pl.ds(MEM * step, tail.shape[0]), :] = tail[...]


def parts_of(ref):
    return [ref.at[j * ROWS : (j + 1) * ROWS] for j in range(MEM + 1)]


def scatter_rows(scal, whole, pieces, tail, step):
    for j in range(MEM):
        start = pl.multiple_of(scal[j] * step, step)
        pieces[j][...] = whole[pl.ds(start, pieces[j].shape[0]), :].astype(BF)
    if tail is not None:
        tail[...] = whole[pl.ds(MEM * step, tail.shape[0]), :].astype(BF)


def self_prepare(scal, whole, qa, ka):
    hidden = lax.broadcasted_iota(jnp.int32, (WIDE, 128), 0) < scal[4]
    for head in range(HEADS):
        if head < 2:
            query, key = whole[:, 0:128], whole[:, 128:256]
        else:
            query = whole[:, 384:512]
            key = swap_halves(query)
        qa[head] = marked(head, scaled(query), jnp.asarray(NEG, BF))
        ka[head] = marked(head, only(head, key), jnp.where(hidden, 1.0, 0.0).astype(BF))


def forward_finish(scal, ot, out, outs, tail):
    ot[HEADS * HD :, :] = jnp.zeros((HD, WIDE), F32)
    for i in range(MEM + 1):
        block = ot[:, i * ROWS : (i + 1) * ROWS].T
        keep = valid_rows(scal, i * ROWS, ROWS)[:, 0:1]
        out[i * ROWS : (i + 1) * ROWS, :] = jnp.where(keep, block, 0.0).astype(BF)
    scatter_rows(scal, out, outs, tail, ROWS)


def self_forward_kernel(scal, rows, o0, o1, o2, o3, otail, ot, lse, whole, qa, ka, vt, out):
    *pieces, tail = parts_of(rows)
    gather_rows(scal, pieces, tail, whole, ROWS)
    self_prepare(scal, whole, qa, ka)
    turned = whole[:, 256:384].astype(F32).T.astype(BF)
    vt[0] = turned[0:HD]
    vt[1] = turned[HD:128]
    vt[2] = whole[:, 512:640].astype(F32).T.astype(BF)[0:HD]
    causal = lax.broadcasted_iota(jnp.int32, (ROWS, ROWS), 0) <= lax.broadcasted_iota(
        jnp.int32, (ROWS, ROWS), 1
    )

    def one_head(head, carry):
        for i in range(MEM + 1):
            a, b = i * ROWS, (i + 1) * ROWS
            query = qa[head, a:b, :]
            near = jnp.where(causal, product_right(ka[head, a:b, :], query), NEG)
            top = jnp.max(near, axis=0, keepdims=True)
            if i:
                far = product_right(ka[head, 0:a, :], query)
                top = jnp.maximum(top, jnp.max(far, axis=0, keepdims=True))
                far = jnp.exp(far - top)
            near = jnp.exp(near - top)
            total = jnp.sum(near, axis=0, keepdims=True)
            if i:
                total = total + jnp.sum(far, axis=0, keepdims=True)
            scale = 1.0 / total
            mixed = product(vt[head, :, a:b], (near * scale).astype(BF))
            if i:
                mixed = mixed + product(vt[head, :, 0:a], (far * scale).astype(BF))
            ot[pl.ds(pl.multiple_of(head * HD, HD), HD), a:b] = mixed
            lse[head, 0:1, a:b] = top + jnp.log(total)
        return carry

    lax.fori_loop(0, HEADS, one_head, 0)
    forward_finish(scal, ot, out, (o0, o1, o2, o3), otail)


def grads_prepare(scal, grads, ot, dm, delta):
    for i in range(MEM + 1):
        a, b = i * ROWS, (i + 1) * ROWS
        keep = valid_rows(scal, a, ROWS)[:, 0:1]
        clean = jnp.where(keep, grads[a:b, :].astype(F32), 0.0)
        turned = clean.T * ot[:, a:b]
        clean = clean.astype(BF)
        for head in range(HEADS):
            window = clean[:, 0:128] if head < 2 else clean[:, 128:256]
            dm[head, a:b, :] = only(head, window)
            delta[head, 0:1, a:b] = jnp.sum(turned[head * HD : (head + 1) * HD], axis=0, keepdims=True)


def self_backward_kernel(
    scal, rows, g0, g1, g2, g3, gtail, ot, lse, drows,
    whole, grads, qa, ka, qm, kt, vm, dm, delta, dqt, dk, dv, out,
):
    *pieces, tail = parts_of(rows)
    gather_rows(scal, pieces, tail, whole, ROWS)
    gather_rows(scal, (g0, g1, g2, g3), gtail, grads, ROWS)
    self_prepare(scal, whole, qa, ka)
    grads_prepare(scal, grads, ot, dm, delta)
    turned = whole[:, 128:256].astype(F32).T.astype(BF)
    kt[0] = turned[0:HD]
    kt[1] = turned[HD:128]
    kt[2] = whole[:, 384:512].astype(F32).T.astype(BF)[HD:128]
    for head in range(HEADS):
        qm[head] = only(head, scaled(whole[:, 0:128] if head < 2 else whole[:, 384:512]))
        vm[head] = only(head, whole[:, 256:384] if head < 2 else whole[:, 512:640])
    dk[...] = jnp.zeros_like(dk)
    dv[...] = jnp.zeros_like(dv)
    dqt[HEADS * HD :, :] = jnp.zeros((HD, WIDE), F32)
    causal = lax.broadcasted_iota(jnp.int32, (ROWS, ROWS), 0) <= lax.broadcasted_iota(
        jnp.int32, (ROWS, ROWS), 1
    )

    def one_head(head, carry):
        side = jnp.where(head == 2, 1, 0)
        for i in range(MEM + 1):
            a, b = i * ROWS, (i + 1) * ROWS
            query, grad, own = qa[head, a:b, :], dm[head, a:b, :], qm[head, a:b, :]
            level, offset = lse[head, 0:1, a:b], delta[head, 0:1, a:b]
            change = jnp.zeros((HD, ROWS), F32)
            for low, high in ((a, b), (0, a)):
                if low == high:
                    continue
                scores = product_right(ka[head, low:high, :], query)
                if low == a:
                    scores = jnp.where(causal, scores, NEG)
                probs = jnp.exp(scores - level)
                slopes = product_right(vm[head, low:high, :], grad)
                slopes = (probs * (slopes - offset)).astype(BF)
                dv[side, low:high, :] += product(probs.astype(BF), grad)
                dk[side, low:high, :] += product(slopes, own)
                change = change + product(kt[head, :, low:high], slopes)
            dqt[pl.ds(pl.multiple_of(head * HD, HD), HD), a:b] = change * 0.125
        return carry

    lax.fori_loop(0, HEADS, one_head, 0)
    for i in range(MEM + 1):
        a, b = i * ROWS, (i + 1) * ROWS
        query = dqt[:, a:b].T
        out[a:b, 0:128] = query[:, 0:128].astype(BF)
        out[a:b, 128:256] = dk[0, a:b, :].astype(BF)
        out[a:b, 256:384] = dv[0, a:b, :].astype(BF)
        out[a:b, 384:512] = (query[:, 128:256] + pltpu.roll(dk[1, a:b, :], HD, 1)).astype(BF)
        out[a:b, 512:640] = dv[1, a:b, :].astype(BF)
    *pieces, tail = parts_of(drows)
    scatter_rows(scal, out, pieces, tail, ROWS)


def cross_prepare(whole, queries, qa, ka):
    spare = (lax.broadcasted_iota(jnp.int32, (KEYS, 128), 0) % FP) >= FR
    for head in range(HEADS):
        query = queries[:, 0:128] if head < 2 else queries[:, 128:256]
        key = whole[:, 0:128] if head < 2 else whole[:, 256:384]
        qa[head] = marked(head, scaled(query), jnp.asarray(NEG, BF))
        ka[head] = marked(head, only(head, key), jnp.where(spare, 1.0, 0.0).astype(BF))


def cross_forward_kernel(
    scal, q0, q1, q2, q3, qtail, f0, f1, f2, f3,
    o0, o1, o2, o3, otail, ot, lse,
    whole, queries, qa, ka, vt, out,
):
    whole[...] = jnp.zeros_like(whole)
    for j, piece in enumerate((f0, f1, f2, f3)):
        whole[j * FP : j * FP + FR, :] = piece[...]
    gather_rows(scal, (q0, q1, q2, q3), qtail, queries, ROWS)
    cross_prepare(whole, queries, qa, ka)
    turned = whole[:, 128:256].astype(F32).T.astype(BF)
    vt[0] = turned[0:HD]
    vt[1] = turned[HD:128]
    vt[2] = whole[:, 256:384].astype(F32).T.astype(BF)[HD:128]

    def one_block(step, carry):
        head = step // (MEM + 1)
        here = pl.ds(pl.multiple_of((step % (MEM + 1)) * ROWS, ROWS), ROWS)
        scores = product_right(ka[head], qa[head, here, :])
        top = jnp.max(scores, axis=0, keepdims=True)
        scores = jnp.exp(scores - top)
        total = jnp.sum(scores, axis=0, keepdims=True)
        mixed = product(vt[head], (scores * (1.0 / total)).astype(BF))
        ot[pl.ds(pl.multiple_of(head * HD, HD), HD), here] = mixed
        lse[head, 0:1, here] = top + jnp.log(total)
        return carry

    lax.fori_loop(0, HEADS * (MEM + 1), one_block, 0)
    forward_finish(scal, ot, out, (o0, o1, o2, o3), otail)


def cross_backward_kernel(
    scal, q0, q1, q2, q3, qtail, f0, f1, f2, f3, g0, g1, g2, g3, gtail, ot, lse,
    d0, d1, d2, d3, dtail, e0, e1, e2, e3,
    whole, queries, grads, qa, ka, qm, kt, vm, dm, delta, dqt, dk, dv, out, fout,
):
    whole[...] = jnp.zeros_like(whole)
    for j, piece in enumerate((f0, f1, f2, f3)):
        whole[j * FP : j * FP + FR, :] = piece[...]
    gather_rows(scal, (q0, q1, q2, q3), qtail, queries, ROWS)
    gather_rows(scal, (g0, g1, g2, g3), gtail, grads, ROWS)
    cross_prepare(whole, queries, qa, ka)
    grads_prepare(scal, grads, ot, dm, delta)
    turned = whole[:, 0:128].astype(F32).T.astype(BF)
    kt[0] = turned[0:HD]
    kt[1] = turned[HD:128]
    kt[2] = whole[:, 256:384].astype(F32).T.astype(BF)[0:HD]
    for head in range(HEADS):
        qm[head] = only(head, scaled(queries[:, 0:128] if head < 2 else queries[:, 128:256]))
        vm[head] = only(head, whole[:, 128:256] if head < 2 else swap_halves(whole[:, 256:384]))
    dk[...] = jnp.zeros_like(dk)
    dv[...] = jnp.zeros_like(dv)
    dqt[HEADS * HD :, :] = jnp.zeros((HD, WIDE), F32)

    def one_block(step, carry):
        head = step // (MEM + 1)
        side = jnp.where(head == 2, 1, 0)
        here = pl.ds(pl.multiple_of((step % (MEM + 1)) * ROWS, ROWS), ROWS)
        grad = dm[head, here, :]
        scores = product_right(ka[head], qa[head, here, :])
        probs = jnp.exp(scores - lse[head, 0:1, here])
        slopes = product_right(vm[head], grad)
        slopes = (probs * (slopes - delta[head, 0:1, here])).astype(BF)
        dv[side] += product(probs.astype(BF), grad)
        dk[side] += product(slopes, qm[head, here, :])
        change = product(kt[head], slopes)
        dqt[pl.ds(pl.multiple_of(head * HD, HD), HD), here] = change * 0.125
        return carry

    lax.fori_loop(0, HEADS * (MEM + 1), one_block, 0)
    for i in range(MEM + 1):
        a, b = i * ROWS, (i + 1) * ROWS
        out[a:b, :] = dqt[:, a:b].T.astype(BF)
    scatter_rows(scal, out, (d0, d1, d2, d3), dtail, ROWS)
    fout[:, 0:128] = dk[0].astype(BF)
    fout[:, 128:256] = dv[0].astype(BF)
    fout[:, 256:384] = (dk[1] + pltpu.roll(dv[1], HD, 1)).astype(BF)
    for j, piece in enumerate((e0, e1, e2, e3)):
        piece[...] = fout[j * FP : j * FP + FR, :]


def shape(*dims, dtype=BF):
    return jax.ShapeDtypeStruct(dims, dtype)


def vmem(*dims, dtype=BF):
    return pltpu.VMEM(dims, dtype)


def call(kernel, scal, args, outs, scratch, flops, exps):
    full = pl.BlockSpec(memory_space=pltpu.VMEM)
    return pl.pallas_call(
        kernel,
        out_shape=outs,
        in_specs=[pl.BlockSpec(memory_space=pltpu.SMEM)] + [full] * len(args),
        out_specs=[full] * len(outs),
        scratch_shapes=scratch,
        cost_estimate=pl.CostEstimate(flops=flops, transcendentals=exps, bytes_accessed=4 << 20),
        compiler_params=pltpu.CompilerParams(vmem_limit_bytes=60 << 20),
    )(scal, *args)


def self_forward(scal, rows):
    outs = [shape(ROWS, 256)] * 5 + [shape(256, WIDE, dtype=F32), shape(HEADS, 8, WIDE, dtype=F32)]
    scratch = [vmem(WIDE, 640), vmem(HEADS, WIDE, 128), vmem(HEADS, WIDE, 128), vmem(HEADS, HD, WIDE), vmem(WIDE, 256)]
    got = call(self_forward_kernel, scal, [rows], outs, scratch, 3 << 30, 3 << 20)
    return (got[:5], got[5:])


def self_backward(scal, rows, grads, kept):
    outs = [shape(WIDE, 640)]
    head = vmem(HEADS, WIDE, 128)
    scratch = [
        vmem(WIDE, 640), vmem(WIDE, 256), head, head, head, vmem(HEADS, HD, WIDE), head, head,
        vmem(HEADS, 8, WIDE, dtype=F32), vmem(256, WIDE, dtype=F32),
        vmem(2, WIDE, 128, dtype=F32), vmem(2, WIDE, 128, dtype=F32), vmem(WIDE, 640),
    ]
    return call(self_backward_kernel, scal, [rows, *grads, *kept], outs, scratch, 8 << 30, 3 << 20)[0]


def cross_forward(scal, queries, frames):
    outs = [shape(ROWS, 256)] * 5 + [shape(256, WIDE, dtype=F32), shape(HEADS, 8, WIDE, dtype=F32)]
    scratch = [
        vmem(KEYS, 384), vmem(WIDE, 256), vmem(HEADS, WIDE, 128), vmem(HEADS, KEYS, 128),
        vmem(HEADS, HD, KEYS), vmem(WIDE, 256),
    ]
    got = call(cross_forward_kernel, scal, [*queries, *frames], outs, scratch, 6 << 30, 6 << 20)
    return (got[:5], got[5:])


def cross_backward(scal, queries, frames, grads, kept):
    outs = [shape(ROWS, 256)] * 5 + [shape(FR, 384)] * 4
    head, keys = (vmem(HEADS, WIDE, 128), vmem(HEADS, KEYS, 128))
    scratch = [
        vmem(KEYS, 384), vmem(WIDE, 256), vmem(WIDE, 256), head, keys, head, vmem(HEADS, HD, KEYS), keys, head,
        vmem(HEADS, 8, WIDE, dtype=F32), vmem(256, WIDE, dtype=F32),
        vmem(2, KEYS, 128, dtype=F32), vmem(2, KEYS, 128, dtype=F32), vmem(WIDE, 256), vmem(KEYS, 384),
    ]
    got = call(cross_backward_kernel, scal, [*queries, *frames, *grads, *kept], outs, scratch, 16 << 30, 6 << 20)
    return (got[:5], got[5:])


def swap(value, mask):
    if mask == 0:
        return value
    count = lax.axis_size("grp") * MEM
    return lax.ppermute(value, LINE, [(s, s ^ mask) for s in range(count)])


def to_previous(value):
    count = lax.axis_size("grp") * MEM
    return lax.ppermute(value, LINE, [(s, s - MEM) for s in range(MEM, count)])


def to_next(value):
    count = lax.axis_size("grp") * MEM
    return lax.ppermute(value, LINE, [(s, s + MEM) for s in range(count - MEM)])


def spread(member, rows):
    parts = [jnp.pad(rows[:, 192 * m : 192 * m + 192], ((0, 0), (0, 64))) for m in range(MEM)]
    return [swap(lax.select_n(member, *[parts[m ^ j] for m in range(MEM)]), j) for j in range(MEM)]


def with_tail(member, pieces):
    return [*pieces, to_previous(lax.select_n(member, *pieces))]


def token_tail(member, pieces):
    count = lax.axis_size("grp") * MEM
    even = lax.ppermute(
        lax.select_n(member, *pieces), LINE, [(s, s - MEM) for s in range(MEM, count, 2)]
    )
    odd = lax.ppermute(even, LINE, [(s, s + 1) for s in range(0, count, 2)])
    return (jnp.where(member % 2 == 0, even, odd), even)


def total_rows(member, partial):
    core = member % 2
    half = ROWS // 2
    tail = partial[MEM * ROWS :].reshape(2, half, D)
    late = swap(lax.dynamic_index_in_dim(tail, 1 - core, keepdims=False).astype(BF), 1).astype(F32)
    late = to_next((late + lax.dynamic_index_in_dim(tail, core, keepdims=False)).astype(BF)).astype(F32)
    late = jnp.concatenate([jnp.where(core == c, late, 0.0) for c in range(2)], axis=0)
    pieces = [
        partial[j * ROWS : (j + 1) * ROWS] + jnp.where(member == j, late, 0.0) for j in range(MEM)
    ]
    other = swap(jnp.concatenate([pieces[1], pieces[3]], axis=0).astype(BF), 1).astype(F32)
    far = (pieces[2] + other[ROWS:]).astype(BF)
    return pieces[0] + other[:ROWS] + swap(far, 2).astype(F32)


def join(member, pieces, width):
    return jnp.concatenate(
        [lax.select_n(member, *[pieces[s ^ m][:, :width] for m in range(MEM)]) for s in range(MEM)], axis=1
    )


def collect(member, pieces):
    late = to_next(pieces[4])
    whole = []
    for j in range(MEM):
        piece = pieces[j].astype(F32) + jnp.where(member == j, late.astype(F32), 0.0)
        whole.append(swap(piece.astype(BF), j))
    return join(member, whole, 192)


def pack_kernel(query, key, value, gains, so, co, cq, ck, cv, up, down, own, second, third):
    rows = query.shape[0]
    for m in range(MEM):
        a = 192 * m
        for n, matrix in enumerate((query, key, value)):
            own[m, :, 128 * n : 128 * n + 128] = matrix[:, a : a + 128]
        own[m, :, 384:512] = jnp.concatenate([query[:, a + 128 : a + 192], key[:, a + 128 : a + 192]], axis=1)
        own[m, :, 512:640] = jnp.concatenate([value[:, a + 128 : a + 192], gains[:, 0:64]], axis=1)
        b = 3 * D + 384 * m
        second[:, b : b + 128] = ck[:, a : a + 128]
        second[:, b + 128 : b + 256] = cv[:, a : a + 128]
        second[:, b + 256 : b + 384] = jnp.concatenate([ck[:, a + 128 : a + 192], cv[:, a + 128 : a + 192]], axis=1)
    for n, matrix in enumerate((so, co, cq)):
        second[:, D * n : D * n + D] = matrix[...]
    for c in range(FF // D):
        third[c * rows : (c + 1) * rows, :] = up[:, c * D : (c + 1) * D]
    third[4 * rows :, :] = down[...]


def pack(*args):
    rows = args[0].shape[0]
    full = pl.BlockSpec(memory_space=pltpu.VMEM)
    return pl.pallas_call(
        pack_kernel,
        out_shape=[shape(MEM, rows, 640), shape(rows, 3 * D + 1536), shape(8 * rows, D)],
        in_specs=[full] * len(args),
        out_specs=[full] * 3,
    )(*args)


def unpack_kernel(scal, p0, p1, p2, p3, query, key, value, ck, cv, gains, sets):
    for j, piece in enumerate((p0, p1, p2, p3)):
        sets[scal[j]] = piece[...].astype(F32)
    total = jnp.zeros_like(gains)
    for m in range(MEM):
        a = 192 * m
        for n, out in enumerate((query, key, value)):
            out[:, a : a + 128] = sets[m, :, 128 * n : 128 * n + 128]
        last = sets[m, :, 512:640]
        query[:, a + 128 : a + 192] = sets[m, :, 384:448]
        key[:, a + 128 : a + 192] = sets[m, :, 448:512]
        value[:, a + 128 : a + 192] = last[:, 0:64]
        total = total + last
        ck[:, a : a + 128] = sets[m, :, 640:768]
        cv[:, a : a + 128] = sets[m, :, 768:896]
        ck[:, a + 128 : a + 192] = sets[m, :, 896:960]
        cv[:, a + 128 : a + 192] = sets[m, :, 960:1024]
    gains[...] = total


def unpack(scal, pieces):
    rows = pieces[0].shape[0]
    full = pl.BlockSpec(memory_space=pltpu.VMEM)
    return pl.pallas_call(
        unpack_kernel,
        out_shape=[shape(rows, D, dtype=F32)] * 5 + [shape(rows, 128, dtype=F32)],
        in_specs=[pl.BlockSpec(memory_space=pltpu.SMEM)] + [full] * MEM,
        out_specs=[full] * 6,
        scratch_shapes=[vmem(MEM, rows, 1024, dtype=F32)],
    )(scal, *pieces)


def gather(matrix):
    return lax.all_gather(matrix, ALL, axis=0, tiled=True)


class Halving:
    def __init__(self, matrix, turned, own=False):
        self.devices = lax.axis_size("fsdp") * lax.axis_size("grp") * MEM
        bits = self.devices.bit_length() - 1
        outer = [bits - 1, bits - 2] if turned else [bits - 2, bits - 1]
        self.order = ([] if own else [0]) + outer + list(range(2 if own else 1, bits - 2))
        self.here = lax.axis_index(ALL)
        self.left = list(range(bits - 1, -1, -1))
        self.value = matrix.reshape([2] * bits + [matrix.shape[0] // self.devices, matrix.shape[1]])
        self.own = own
        self.split()

    def split(self):
        self.bit = self.order.pop(0)
        axis = self.left.index(self.bit)
        self.left.remove(self.bit)
        mine = (self.here >> self.bit) & 1
        self.away = lax.dynamic_index_in_dim(self.value, 1 - mine, axis, keepdims=False)
        self.kept = lax.dynamic_index_in_dim(self.value, mine, axis, keepdims=False)

    def send(self):
        self.came = lax.ppermute(self.away, ALL, [(s, s ^ (1 << self.bit)) for s in range(self.devices)])

    def add(self):
        self.value = self.kept.astype(F32) + self.came.astype(F32)
        if self.order or self.own:
            self.value = self.value.astype(BF)
        self.came = None
        if self.order:
            self.split()

    def on(self):
        if self.order:
            self.add()
            self.send()

    def finish(self):
        while self.order:
            self.on()
        self.add()
        return self.value


def tie(value, chains, name):
    got = lax.optimization_barrier((value, [getattr(chain, name) for chain in chains]))
    for chain, array in zip(chains, got[1]):
        setattr(chain, name, array)
    return got[0]


def gather_own(member, shard, width):
    devices = lax.axis_size("fsdp") * lax.axis_size("grp") * MEM
    here = lax.axis_index(ALL)
    pieces = [swap(lax.dynamic_index_in_dim(shard, member ^ j, keepdims=False), j) for j in range(MEM)]
    value = jnp.stack([lax.select_n(member, *[pieces[s ^ m] for m in range(MEM)]) for s in range(MEM)])
    for bit in range(2, devices.bit_length() - 1):
        mine = ((here >> bit) & 1) == 0
        came = lax.ppermute(value, ALL, [(s, s ^ (1 << bit)) for s in range(devices)])
        value = jnp.concatenate([jnp.where(mine, value, came), jnp.where(mine, came, value)])
    return value.reshape(devices * shard.shape[1], width)


def own_sets(member, value):
    value = value.reshape(MEM, *value.shape[2:])
    return [swap(lax.dynamic_index_in_dim(value, member ^ j, keepdims=False), j) for j in range(MEM)]


def moments(states):
    center = states - jnp.mean(states, axis=-1, keepdims=True)
    spread_ = jnp.mean(center * center, axis=-1, keepdims=True)
    rate = lax.rsqrt(spread_ + 1e-05)
    return (center * rate, rate)


def shards(
    tokens, frames, document_starts, cotangent,
    gain_self, gain_cross, gain_feed, gain_final,
    self_query, self_key, self_value, self_output,
    cross_query, cross_key, cross_value, cross_output,
    feed_up, feed_down,
):
    devices = lax.axis_size("fsdp") * lax.axis_size("grp") * MEM
    group, member = (lax.axis_index("grp"), lax.axis_index("mem"))
    groups = lax.axis_size("grp")
    starts = document_starts[0]
    inner = starts - SPAN * jnp.arange(groups, dtype=jnp.int32)
    late = jnp.concatenate([inner[1:], jnp.zeros((1,), jnp.int32)])
    scal = jnp.stack([
        member, member ^ 1, member ^ 2, member ^ 3,
        lax.dynamic_index_in_dim(inner, group, keepdims=False),
        lax.dynamic_index_in_dim(late, group, keepdims=False),
        member, member,
    ]).astype(jnp.int32)

    gains = jnp.stack([gain_self, gain_cross, gain_feed, gain_final], axis=1)
    gains = jnp.pad(gains, ((0, 0), (0, 124)))
    own_part, second, third = pack(
        self_query, self_key, self_value, gains, self_output, cross_output,
        cross_query, cross_key, cross_value, feed_up, feed_down,
    )
    w_own = gather_own(member, own_part, 640)
    two = swap(tokens, 2)
    other = swap(jnp.concatenate([tokens, two], axis=0), 1)
    near_tokens = [tokens, other[:ROWS], two, other[ROWS:]]
    tail, even = token_tail(member, near_tokens)
    near_tokens = jnp.concatenate([*near_tokens, tail], axis=0)
    held_frames, even = lax.optimization_barrier((frames, even))
    two = swap(held_frames, 2)
    near_frames = [swap(held_frames, 1), two]
    second, third = (gather(second), gather(third))
    third = third.reshape(devices, 2 * FF // devices, D)
    part = D // devices

    gain_rows = w_own[:, 512:].T[64:68].astype(F32)
    w_so, w_co = (second[:, :D], second[:, D : 2 * D])
    w_cq, w_kv = (second[:, 2 * D : 3 * D], second[:, 3 * D :])
    w_up = jnp.concatenate([third[:, c * part : (c + 1) * part].reshape(D, D) for c in range(4)], axis=1)
    w_down = third[:, 4 * part :].reshape(FF, D)

    states = tokens.astype(F32)
    unit, _ = moments(near_tokens.astype(F32))
    normed_self = (unit * gain_rows[0]).astype(BF)
    self_rows = product(normed_self, w_own).astype(BF)
    mixed, self_kept = self_forward(scal, self_rows)
    mixed, near_frames = lax.optimization_barrier((mixed, near_frames))
    near_frames = [frames, *near_frames, swap(near_frames[1], 1)]
    own_kv = lax.dynamic_slice_in_dim(w_kv, member * 384, 384, axis=1)
    frame_rows = [product(piece, own_kv).astype(BF) for piece in near_frames]
    self_heads = collect(member, mixed)
    first_sum = states + product(self_heads, w_so)
    normed_cross, back_cross = jax.vjp(normalize, first_sum, gain_rows[1])
    normed_cross = normed_cross.astype(BF)
    cross_queries = product(normed_cross, w_cq).astype(BF)
    cross_pieces = with_tail(member, spread(member, cross_queries))
    mixed, cross_kept = cross_forward(scal, cross_pieces, frame_rows)
    cross_heads = collect(member, mixed)
    second_sum = first_sum + product(cross_heads, w_co)
    normed_feed, back_feed = jax.vjp(normalize, second_sum, gain_rows[2])
    normed_feed = normed_feed.astype(BF)
    inner_units = product(normed_feed, w_up)
    activated, back_gelu = jax.vjp(exact_gelu, inner_units)
    hidden = activated.astype(BF)
    third_sum = second_sum + product(hidden, w_down)
    result, back_final = jax.vjp(normalize, third_sum, gain_rows[3])

    grad_third, grad_gain_final = back_final(cotangent.astype(F32))
    grad_feed_out = grad_third.astype(BF)
    (grad_inner,) = back_gelu(product_right(grad_feed_out, w_down))
    grad_inner = grad_inner.astype(BF)
    grad_up = product_left(normed_feed, grad_inner).astype(BF)
    grad_down = product_left(hidden, grad_feed_out).astype(BF)
    down = Halving(grad_down, False)
    down.send()
    sums_up = lax.psum_scatter(grad_up, ALL, scatter_dimension=0, tiled=True)
    grad_second_part, grad_gain_feed = back_feed(product_right(grad_inner, w_up))
    grad_second = grad_third + grad_second_part

    grad_cross_out = grad_second.astype(BF)
    grad_cross_heads = product_right(grad_cross_out, w_co).astype(BF)
    grad_pieces = with_tail(member, spread(member, grad_cross_heads))
    down.add()
    held = tie(scal, [down], "away")
    down.send()
    query_pieces, frame_grads = cross_backward(held, cross_pieces, frame_rows, grad_pieces, cross_kept)
    query_pieces, frame_grads = tie((query_pieces, frame_grads), [down], "came")
    down.on()
    grad_cross_queries = collect(member, query_pieces)
    grad_cq = product_left(normed_cross, grad_cross_queries).astype(BF)
    grad_first_part, grad_gain_cross = back_cross(product_right(grad_cross_queries, w_cq))
    grad_first = grad_second + grad_first_part

    grad_self_out = grad_first.astype(BF)
    grad_self_heads = product_right(grad_self_out, w_so).astype(BF)
    grad_pieces = with_tail(member, spread(member, grad_self_heads))
    grad_co = product_left(cross_heads, grad_cross_out).astype(BF)
    grad_so = product_left(self_heads, grad_self_out).astype(BF)
    grad_kv = sum(product_left(near_frames[j], frame_grads[j]) for j in range(MEM))
    rest = [part.reshape(devices, D // devices, D) for part in (grad_so, grad_co, grad_cq)]
    rest = Halving(jnp.concatenate(rest, axis=1).reshape(3 * D, D), True)
    rest.send()
    down.add()
    rest.add()
    held = tie(scal, [down, rest], "away")
    down.send()
    rest.send()
    grad_rows = self_backward(held, self_rows, grad_pieces, self_kept)
    grad_rows = tie(grad_rows, [down, rest], "came")
    rest.on()
    down.on()
    grad_normed = product_right(grad_rows, w_own)
    grad_gain_self = jnp.sum(grad_normed * unit, axis=0)
    grad_gains = jnp.stack([grad_gain_self, grad_gain_cross, grad_gain_feed, grad_gain_final])
    grad_gains = jnp.pad(grad_gains, ((64, 60), (0, 0))).T
    grad_qkv = product_left(normed_self, grad_rows)
    grad_qkv = jnp.concatenate([grad_qkv[:, :512], grad_qkv[:, 512:] + grad_gains], axis=1).astype(BF)
    own = Halving(jnp.concatenate([grad_qkv, grad_kv.astype(BF)], axis=1), False, True)
    own.send()
    total = total_rows(member, grad_normed)
    _, back_self = jax.vjp(normalize, states, gain_rows[0])
    tokens_gradient = grad_first + back_self(total)[0]
    frame_grad = join(member, [swap(frame_grads[j], j) for j in range(MEM)], 384)
    frames_gradient = product_right(frame_grad, w_kv)

    sums_down = down.finish()
    for _ in range(8):
        rest.on()
        own.on()
    sums_rest = rest.finish()
    last, sums_up = lax.optimization_barrier((own.finish(), sums_up))
    sets = own_sets(member, last)
    sums_up = sums_up.astype(F32)
    query, key, value, cross_k, cross_v, gains_out = unpack(scal, sets)
    gains_out = gains_out.T[64:68]
    return (
        result.astype(BF),
        tokens_gradient,
        frames_gradient,
        gains_out[0],
        gains_out[1],
        gains_out[2],
        gains_out[3],
        query,
        key,
        value,
        sums_rest[:part],
        sums_rest[2 * part :],
        cross_k,
        cross_v,
        sums_rest[part : 2 * part],
        sums_up,
        sums_down,
    )


def solution(mesh):
    fsdp, ctx = (mesh.shape["fsdp"], mesh.shape["ctx"])
    fine = Mesh(mesh.devices.reshape(fsdp, ctx // MEM, MEM), ALL)
    rows, flat = (P(ALL, None), P(ALL))
    in_specs = (rows, rows, P("fsdp", None), rows) + (flat,) * 4 + (rows,) * 10
    out_specs = (rows,) * 3 + (flat,) * 4 + (rows,) * 10
    return jax.shard_map(shards, mesh=fine, in_specs=in_specs, out_specs=out_specs, check_vma=False)
```

```python
import functools

import jax
import jax.numpy as jnp
from jax import lax
from jax.experimental import pallas as pl
from jax.experimental.pallas import tpu as pltpu
from jax.sharding import Mesh, PartitionSpec as P

D = 768
HD = 64
FF = 3072
SPAN = 1024
MEM = 4
ROWS = 256
WIDE = (MEM + 1) * ROWS
HEADS = 3
FR = 375
FP = 384
KEYS = MEM * FP
NEG = -1e30
ALL = ("fsdp", "grp", "mem")
LINE = ("grp", "mem")
F32 = jnp.float32
BF = jnp.bfloat16


def normalize(states, gain):
    center = states - jnp.mean(states, axis=-1, keepdims=True)
    spread = jnp.mean(center * center, axis=-1, keepdims=True)
    return center * lax.rsqrt(spread + 1e-05) * gain


def exact_gelu(values):
    return jax.nn.gelu(values, approximate=False)


def product(left, right):
    return jnp.dot(left, right, preferred_element_type=F32)


def product_left(left, right):
    return lax.dot_general(left, right, (((0,), (0,)), ((), ())), preferred_element_type=F32)


def product_right(left, right):
    return lax.dot_general(left, right, (((1,), (1,)), ((), ())), preferred_element_type=F32)


def lanes(rows):
    return lax.broadcasted_iota(jnp.int32, (rows, 128), 1)


def head_lanes(head, rows):
    lane = lanes(rows)
    return (lane >= HD) if head == 1 else (lane < HD)


def only(head, window):
    return jnp.where(head_lanes(head, window.shape[0]), window, jnp.zeros_like(window))


def swap_halves(window):
    return pltpu.roll(window.astype(F32), HD, 1).astype(BF)


def marked(head, window, value):
    spare = 0 if head == 1 else HD
    return jnp.where(lanes(window.shape[0]) == spare, value, window)


def scaled(window):
    return (window.astype(F32) * 0.125).astype(BF)


def valid_rows(scal, first, count):
    row = first + lax.broadcasted_iota(jnp.int32, (count, 128), 0)
    return (row >= scal[4]) & (row < MEM * ROWS + scal[5])


def gather_rows(scal, pieces, tail, whole, step):
    for j in range(MEM):
        start = pl.multiple_of(scal[j] * step, step)
        whole[pl.ds(start, pieces[j].shape[0]), :] = pieces[j][...]
    if tail is not None:
        whole[pl.ds(MEM * step, tail.shape[0]), :] = tail[...]


def parts_of(ref):
    return [ref.at[j * ROWS : (j + 1) * ROWS] for j in range(MEM + 1)]


def scatter_rows(scal, whole, pieces, tail, step):
    for j in range(MEM):
        start = pl.multiple_of(scal[j] * step, step)
        pieces[j][...] = whole[pl.ds(start, pieces[j].shape[0]), :].astype(BF)
    if tail is not None:
        tail[...] = whole[pl.ds(MEM * step, tail.shape[0]), :].astype(BF)


def self_prepare(scal, whole, qa, ka):
    hidden = lax.broadcasted_iota(jnp.int32, (WIDE, 128), 0) < scal[4]
    for head in range(HEADS):
        if head < 2:
            query, key = whole[:, 0:128], whole[:, 128:256]
        else:
            query = whole[:, 384:512]
            key = swap_halves(query)
        qa[head] = marked(head, scaled(query), jnp.asarray(NEG, BF))
        ka[head] = marked(head, only(head, key), jnp.where(hidden, 1.0, 0.0).astype(BF))


def forward_finish(scal, ot, out, outs, tail):
    ot[HEADS * HD :, :] = jnp.zeros((HD, WIDE), F32)
    for i in range(MEM + 1):
        block = ot[:, i * ROWS : (i + 1) * ROWS].T
        keep = valid_rows(scal, i * ROWS, ROWS)[:, 0:1]
        out[i * ROWS : (i + 1) * ROWS, :] = jnp.where(keep, block, 0.0).astype(BF)
    scatter_rows(scal, out, outs, tail, ROWS)


def self_forward_kernel(scal, rows, o0, o1, o2, o3, otail, ot, lse, whole, qa, ka, vt, out):
    *pieces, tail = parts_of(rows)
    gather_rows(scal, pieces, tail, whole, ROWS)
    self_prepare(scal, whole, qa, ka)
    turned = whole[:, 256:384].astype(F32).T.astype(BF)
    vt[0] = turned[0:HD]
    vt[1] = turned[HD:128]
    vt[2] = whole[:, 512:640].astype(F32).T.astype(BF)[0:HD]
    causal = lax.broadcasted_iota(jnp.int32, (ROWS, ROWS), 0) <= lax.broadcasted_iota(
        jnp.int32, (ROWS, ROWS), 1
    )

    def one_head(head, carry):
        for i in range(MEM + 1):
            a, b = i * ROWS, (i + 1) * ROWS
            query = qa[head, a:b, :]
            near = jnp.where(causal, product_right(ka[head, a:b, :], query), NEG)
            top = jnp.max(near, axis=0, keepdims=True)
            if i:
                far = product_right(ka[head, 0:a, :], query)
                top = jnp.maximum(top, jnp.max(far, axis=0, keepdims=True))
                far = jnp.exp(far - top)
            near = jnp.exp(near - top)
            total = jnp.sum(near, axis=0, keepdims=True)
            if i:
                total = total + jnp.sum(far, axis=0, keepdims=True)
            scale = 1.0 / total
            mixed = product(vt[head, :, a:b], (near * scale).astype(BF))
            if i:
                mixed = mixed + product(vt[head, :, 0:a], (far * scale).astype(BF))
            ot[pl.ds(pl.multiple_of(head * HD, HD), HD), a:b] = mixed
            lse[head, 0:1, a:b] = top + jnp.log(total)
        return carry

    lax.fori_loop(0, HEADS, one_head, 0)
    forward_finish(scal, ot, out, (o0, o1, o2, o3), otail)


def grads_prepare(scal, grads, ot, dm, delta):
    for i in range(MEM + 1):
        a, b = i * ROWS, (i + 1) * ROWS
        keep = valid_rows(scal, a, ROWS)[:, 0:1]
        clean = jnp.where(keep, grads[a:b, :].astype(F32), 0.0)
        turned = clean.T * ot[:, a:b]
        clean = clean.astype(BF)
        for head in range(HEADS):
            window = clean[:, 0:128] if head < 2 else clean[:, 128:256]
            dm[head, a:b, :] = only(head, window)
            delta[head, 0:1, a:b] = jnp.sum(turned[head * HD : (head + 1) * HD], axis=0, keepdims=True)


def self_backward_kernel(
    scal, rows, g0, g1, g2, g3, gtail, ot, lse, drows,
    whole, grads, qa, ka, qm, kt, vm, dm, delta, dqt, dk, dv, out,
):
    *pieces, tail = parts_of(rows)
    gather_rows(scal, pieces, tail, whole, ROWS)
    gather_rows(scal, (g0, g1, g2, g3), gtail, grads, ROWS)
    self_prepare(scal, whole, qa, ka)
    grads_prepare(scal, grads, ot, dm, delta)
    turned = whole[:, 128:256].astype(F32).T.astype(BF)
    kt[0] = turned[0:HD]
    kt[1] = turned[HD:128]
    kt[2] = whole[:, 384:512].astype(F32).T.astype(BF)[HD:128]
    for head in range(HEADS):
        qm[head] = only(head, scaled(whole[:, 0:128] if head < 2 else whole[:, 384:512]))
        vm[head] = only(head, whole[:, 256:384] if head < 2 else whole[:, 512:640])
    dk[...] = jnp.zeros_like(dk)
    dv[...] = jnp.zeros_like(dv)
    dqt[HEADS * HD :, :] = jnp.zeros((HD, WIDE), F32)
    causal = lax.broadcasted_iota(jnp.int32, (ROWS, ROWS), 0) <= lax.broadcasted_iota(
        jnp.int32, (ROWS, ROWS), 1
    )

    def one_head(head, carry):
        side = jnp.where(head == 2, 1, 0)
        for i in range(MEM + 1):
            a, b = i * ROWS, (i + 1) * ROWS
            query, grad, own = qa[head, a:b, :], dm[head, a:b, :], qm[head, a:b, :]
            level, offset = lse[head, 0:1, a:b], delta[head, 0:1, a:b]
            change = jnp.zeros((HD, ROWS), F32)
            for low, high in ((a, b), (0, a)):
                if low == high:
                    continue
                scores = product_right(ka[head, low:high, :], query)
                if low == a:
                    scores = jnp.where(causal, scores, NEG)
                probs = jnp.exp(scores - level)
                slopes = product_right(vm[head, low:high, :], grad)
                slopes = (probs * (slopes - offset)).astype(BF)
                dv[side, low:high, :] += product(probs.astype(BF), grad)
                dk[side, low:high, :] += product(slopes, own)
                change = change + product(kt[head, :, low:high], slopes)
            dqt[pl.ds(pl.multiple_of(head * HD, HD), HD), a:b] = change * 0.125
        return carry

    lax.fori_loop(0, HEADS, one_head, 0)
    for i in range(MEM + 1):
        a, b = i * ROWS, (i + 1) * ROWS
        query = dqt[:, a:b].T
        out[a:b, 0:128] = query[:, 0:128].astype(BF)
        out[a:b, 128:256] = dk[0, a:b, :].astype(BF)
        out[a:b, 256:384] = dv[0, a:b, :].astype(BF)
        out[a:b, 384:512] = (query[:, 128:256] + pltpu.roll(dk[1, a:b, :], HD, 1)).astype(BF)
        out[a:b, 512:640] = dv[1, a:b, :].astype(BF)
    *pieces, tail = parts_of(drows)
    scatter_rows(scal, out, pieces, tail, ROWS)


def cross_prepare(whole, queries, qa, ka):
    spare = (lax.broadcasted_iota(jnp.int32, (KEYS, 128), 0) % FP) >= FR
    for head in range(HEADS):
        query = queries[:, 0:128] if head < 2 else queries[:, 128:256]
        key = whole[:, 0:128] if head < 2 else whole[:, 256:384]
        qa[head] = marked(head, scaled(query), jnp.asarray(NEG, BF))
        ka[head] = marked(head, only(head, key), jnp.where(spare, 1.0, 0.0).astype(BF))


def cross_forward_kernel(
    scal, q0, q1, q2, q3, qtail, f0, f1, f2, f3,
    o0, o1, o2, o3, otail, ot, lse,
    whole, queries, qa, ka, vt, out,
):
    whole[...] = jnp.zeros_like(whole)
    for j, piece in enumerate((f0, f1, f2, f3)):
        whole[j * FP : j * FP + FR, :] = piece[...]
    gather_rows(scal, (q0, q1, q2, q3), qtail, queries, ROWS)
    cross_prepare(whole, queries, qa, ka)
    turned = whole[:, 128:256].astype(F32).T.astype(BF)
    vt[0] = turned[0:HD]
    vt[1] = turned[HD:128]
    vt[2] = whole[:, 256:384].astype(F32).T.astype(BF)[HD:128]

    def one_block(step, carry):
        head = step // (MEM + 1)
        here = pl.ds(pl.multiple_of((step % (MEM + 1)) * ROWS, ROWS), ROWS)
        scores = product_right(ka[head], qa[head, here, :])
        top = jnp.max(scores, axis=0, keepdims=True)
        scores = jnp.exp(scores - top)
        total = jnp.sum(scores, axis=0, keepdims=True)
        mixed = product(vt[head], (scores * (1.0 / total)).astype(BF))
        ot[pl.ds(pl.multiple_of(head * HD, HD), HD), here] = mixed
        lse[head, 0:1, here] = top + jnp.log(total)
        return carry

    lax.fori_loop(0, HEADS * (MEM + 1), one_block, 0)
    forward_finish(scal, ot, out, (o0, o1, o2, o3), otail)


def cross_backward_kernel(
    scal, q0, q1, q2, q3, qtail, f0, f1, f2, f3, g0, g1, g2, g3, gtail, ot, lse,
    d0, d1, d2, d3, dtail, e0, e1, e2, e3,
    whole, queries, grads, qa, ka, qm, kt, vm, dm, delta, dqt, dk, dv, out, fout,
):
    whole[...] = jnp.zeros_like(whole)
    for j, piece in enumerate((f0, f1, f2, f3)):
        whole[j * FP : j * FP + FR, :] = piece[...]
    gather_rows(scal, (q0, q1, q2, q3), qtail, queries, ROWS)
    gather_rows(scal, (g0, g1, g2, g3), gtail, grads, ROWS)
    cross_prepare(whole, queries, qa, ka)
    grads_prepare(scal, grads, ot, dm, delta)
    turned = whole[:, 0:128].astype(F32).T.astype(BF)
    kt[0] = turned[0:HD]
    kt[1] = turned[HD:128]
    kt[2] = whole[:, 256:384].astype(F32).T.astype(BF)[0:HD]
    for head in range(HEADS):
        qm[head] = only(head, scaled(queries[:, 0:128] if head < 2 else queries[:, 128:256]))
        vm[head] = only(head, whole[:, 128:256] if head < 2 else swap_halves(whole[:, 256:384]))
    dk[...] = jnp.zeros_like(dk)
    dv[...] = jnp.zeros_like(dv)
    dqt[HEADS * HD :, :] = jnp.zeros((HD, WIDE), F32)

    def one_block(step, carry):
        head = step // (MEM + 1)
        side = jnp.where(head == 2, 1, 0)
        here = pl.ds(pl.multiple_of((step % (MEM + 1)) * ROWS, ROWS), ROWS)
        grad = dm[head, here, :]
        scores = product_right(ka[head], qa[head, here, :])
        probs = jnp.exp(scores - lse[head, 0:1, here])
        slopes = product_right(vm[head], grad)
        slopes = (probs * (slopes - delta[head, 0:1, here])).astype(BF)
        dv[side] += product(probs.astype(BF), grad)
        dk[side] += product(slopes, qm[head, here, :])
        change = product(kt[head], slopes)
        dqt[pl.ds(pl.multiple_of(head * HD, HD), HD), here] = change * 0.125
        return carry

    lax.fori_loop(0, HEADS * (MEM + 1), one_block, 0)
    for i in range(MEM + 1):
        a, b = i * ROWS, (i + 1) * ROWS
        out[a:b, :] = dqt[:, a:b].T.astype(BF)
    scatter_rows(scal, out, (d0, d1, d2, d3), dtail, ROWS)
    fout[:, 0:128] = dk[0].astype(BF)
    fout[:, 128:256] = dv[0].astype(BF)
    fout[:, 256:384] = (dk[1] + pltpu.roll(dv[1], HD, 1)).astype(BF)
    for j, piece in enumerate((e0, e1, e2, e3)):
        piece[...] = fout[j * FP : j * FP + FR, :]


def shape(*dims, dtype=BF):
    return jax.ShapeDtypeStruct(dims, dtype)


def vmem(*dims, dtype=BF):
    return pltpu.VMEM(dims, dtype)


def call(kernel, scal, args, outs, scratch, flops, exps):
    full = pl.BlockSpec(memory_space=pltpu.VMEM)
    return pl.pallas_call(
        kernel,
        out_shape=outs,
        in_specs=[pl.BlockSpec(memory_space=pltpu.SMEM)] + [full] * len(args),
        out_specs=[full] * len(outs),
        scratch_shapes=scratch,
        cost_estimate=pl.CostEstimate(flops=flops, transcendentals=exps, bytes_accessed=4 << 20),
        compiler_params=pltpu.CompilerParams(vmem_limit_bytes=60 << 20),
    )(scal, *args)


def self_forward(scal, rows):
    outs = [shape(ROWS, 256)] * 5 + [shape(256, WIDE, dtype=F32), shape(HEADS, 8, WIDE, dtype=F32)]
    scratch = [vmem(WIDE, 640), vmem(HEADS, WIDE, 128), vmem(HEADS, WIDE, 128), vmem(HEADS, HD, WIDE), vmem(WIDE, 256)]
    got = call(self_forward_kernel, scal, [rows], outs, scratch, 3 << 30, 3 << 20)
    return (got[:5], got[5:])


def self_backward(scal, rows, grads, kept):
    outs = [shape(WIDE, 640)]
    head = vmem(HEADS, WIDE, 128)
    scratch = [
        vmem(WIDE, 640), vmem(WIDE, 256), head, head, head, vmem(HEADS, HD, WIDE), head, head,
        vmem(HEADS, 8, WIDE, dtype=F32), vmem(256, WIDE, dtype=F32),
        vmem(2, WIDE, 128, dtype=F32), vmem(2, WIDE, 128, dtype=F32), vmem(WIDE, 640),
    ]
    return call(self_backward_kernel, scal, [rows, *grads, *kept], outs, scratch, 8 << 30, 3 << 20)[0]


def cross_forward(scal, queries, frames):
    outs = [shape(ROWS, 256)] * 5 + [shape(256, WIDE, dtype=F32), shape(HEADS, 8, WIDE, dtype=F32)]
    scratch = [
        vmem(KEYS, 384), vmem(WIDE, 256), vmem(HEADS, WIDE, 128), vmem(HEADS, KEYS, 128),
        vmem(HEADS, HD, KEYS), vmem(WIDE, 256),
    ]
    got = call(cross_forward_kernel, scal, [*queries, *frames], outs, scratch, 6 << 30, 6 << 20)
    return (got[:5], got[5:])


def cross_backward(scal, queries, frames, grads, kept):
    outs = [shape(ROWS, 256)] * 5 + [shape(FR, 384)] * 4
    head, keys = (vmem(HEADS, WIDE, 128), vmem(HEADS, KEYS, 128))
    scratch = [
        vmem(KEYS, 384), vmem(WIDE, 256), vmem(WIDE, 256), head, keys, head, vmem(HEADS, HD, KEYS), keys, head,
        vmem(HEADS, 8, WIDE, dtype=F32), vmem(256, WIDE, dtype=F32),
        vmem(2, KEYS, 128, dtype=F32), vmem(2, KEYS, 128, dtype=F32), vmem(WIDE, 256), vmem(KEYS, 384),
    ]
    got = call(cross_backward_kernel, scal, [*queries, *frames, *grads, *kept], outs, scratch, 16 << 30, 6 << 20)
    return (got[:5], got[5:])


def swap(value, mask):
    if mask == 0:
        return value
    count = lax.axis_size("grp") * MEM
    return lax.ppermute(value, LINE, [(s, s ^ mask) for s in range(count)])


def to_previous(value):
    count = lax.axis_size("grp") * MEM
    return lax.ppermute(value, LINE, [(s, s - MEM) for s in range(MEM, count)])


def to_next(value):
    count = lax.axis_size("grp") * MEM
    return lax.ppermute(value, LINE, [(s, s + MEM) for s in range(count - MEM)])


def spread(member, rows, straight):
    parts = [jnp.pad(rows[:, 192 * m : 192 * m + 192], ((0, 0), (0, 64))) for m in range(MEM)]
    pieces = [swap(lax.select_n(member, *[parts[m ^ j] for m in range(MEM)]), j) for j in range(MEM)]
    if not straight:
        return [*pieces, to_previous(lax.select_n(member, *pieces))]
    count = lax.axis_size("grp") * MEM
    tails = [
        lax.ppermute(parts[m], LINE, [(s, s - MEM + m) for s in range(MEM, count, MEM)])
        for m in range(MEM)
    ]
    return [*pieces, lax.select_n(member, *tails)]


def token_tail(member, pieces):
    count = lax.axis_size("grp") * MEM
    even = lax.ppermute(
        lax.select_n(member, *pieces), LINE, [(s, s - MEM) for s in range(MEM, count, 2)]
    )
    odd = lax.ppermute(even, LINE, [(s, s + 1) for s in range(0, count, 2)])
    return (jnp.where(member % 2 == 0, even, odd), even)


def total_rows(member, partial):
    core = member % 2
    half = ROWS // 2
    tail = partial[MEM * ROWS :].reshape(2, half, D)
    late = swap(lax.dynamic_index_in_dim(tail, 1 - core, keepdims=False).astype(BF), 1).astype(F32)
    late = to_next((late + lax.dynamic_index_in_dim(tail, core, keepdims=False)).astype(BF)).astype(F32)
    late = jnp.concatenate([jnp.where(core == c, late, 0.0) for c in range(2)], axis=0)
    pieces = [
        partial[j * ROWS : (j + 1) * ROWS] + jnp.where(member == j, late, 0.0) for j in range(MEM)
    ]
    other = swap(jnp.concatenate([pieces[1], pieces[3]], axis=0).astype(BF), 1).astype(F32)
    far = (pieces[2] + other[ROWS:]).astype(BF)
    return pieces[0] + other[:ROWS] + swap(far, 2).astype(F32)


def join(member, pieces, width):
    return jnp.concatenate(
        [lax.select_n(member, *[pieces[s ^ m][:, :width] for m in range(MEM)]) for s in range(MEM)], axis=1
    )


def collect(member, pieces):
    late = to_next(pieces[4])
    whole = []
    for j in range(MEM):
        piece = pieces[j].astype(F32) + jnp.where(member == j, late.astype(F32), 0.0)
        whole.append(swap(piece.astype(BF), j))
    return join(member, whole, 192)


def collect_straight(member, pieces, beside):
    count = lax.axis_size("grp") * MEM
    lates = [
        lax.ppermute(pieces[4], LINE, [(s - MEM + m, s) for s in range(MEM, count, MEM)])
        for m in range(MEM)
    ]
    near = [swap(pieces[j], j) for j in range(MEM)]
    near[3], beside = lax.optimization_barrier((near[3], beside))
    late = jnp.concatenate([piece[:, :192] for piece in lates], axis=1)
    total = join(member, near, 192).astype(F32) + late.astype(F32)
    return (total.astype(BF), beside)


def pack_kernel(query, key, value, gains, so, co, cq, ck, cv, up, down, own, second, third):
    rows = query.shape[0]
    for m in range(MEM):
        a = 192 * m
        for n, matrix in enumerate((query, key, value)):
            own[m, :, 128 * n : 128 * n + 128] = matrix[:, a : a + 128]
        own[m, :, 384:512] = jnp.concatenate([query[:, a + 128 : a + 192], key[:, a + 128 : a + 192]], axis=1)
        own[m, :, 512:640] = jnp.concatenate([value[:, a + 128 : a + 192], gains[:, 0:64]], axis=1)
        b = 3 * D + 384 * m
        second[:, b : b + 128] = ck[:, a : a + 128]
        second[:, b + 128 : b + 256] = cv[:, a : a + 128]
        second[:, b + 256 : b + 384] = jnp.concatenate([ck[:, a + 128 : a + 192], cv[:, a + 128 : a + 192]], axis=1)
    for n, matrix in enumerate((so, co, cq)):
        second[:, D * n : D * n + D] = matrix[...]
    for c in range(FF // D):
        third[c * rows : (c + 1) * rows, :] = up[:, c * D : (c + 1) * D]
    third[4 * rows :, :] = down[...]


def pack(*args):
    rows = args[0].shape[0]
    full = pl.BlockSpec(memory_space=pltpu.VMEM)
    return pl.pallas_call(
        pack_kernel,
        out_shape=[shape(MEM, rows, 640), shape(rows, 3 * D + 1536), shape(8 * rows, D)],
        in_specs=[full] * len(args),
        out_specs=[full] * 3,
    )(*args)


def unpack_kernel(scal, p0, p1, p2, p3, wq, wk, wv, query, key, value, ck, cv, gains, sets):
    for j, piece in enumerate((p0, p1, p2, p3)):
        sets[scal[j]] = piece[...].astype(F32)
    total = jnp.zeros_like(gains)
    for m in range(MEM):
        a = 192 * m
        for n, out in enumerate((query, key, value)):
            out[:, a : a + 128] = sets[m, :, 128 * n : 128 * n + 128]
        last = sets[m, :, 512:640]
        query[:, a + 128 : a + 192] = sets[m, :, 384:448]
        key[:, a + 128 : a + 192] = sets[m, :, 448:512]
        value[:, a + 128 : a + 192] = last[:, 0:64]
        total = total + last
        ck[:, a : a + 128] = sets[m, :, 640:768]
        cv[:, a : a + 128] = sets[m, :, 768:896]
        ck[:, a + 128 : a + 192] = sets[m, :, 896:960]
        cv[:, a + 128 : a + 192] = sets[m, :, 960:1024]
    dots = jnp.zeros_like(total[:, 0:1])
    for matrix, out in ((wq, query), (wk, key), (wv, value)):
        dots = dots + jnp.sum(matrix[...].astype(F32) * out[...], axis=1, keepdims=True)
    gains[...] = jnp.where(lanes(total.shape[0]) == 0, dots, total)


def unpack(scal, pieces, weights):
    rows = pieces[0].shape[0]
    full = pl.BlockSpec(memory_space=pltpu.VMEM)
    return pl.pallas_call(
        unpack_kernel,
        out_shape=[shape(rows, D, dtype=F32)] * 5 + [shape(rows, 128, dtype=F32)],
        in_specs=[pl.BlockSpec(memory_space=pltpu.SMEM)] + [full] * 7,
        out_specs=[full] * 6,
        scratch_shapes=[vmem(MEM, rows, 1024, dtype=F32)],
    )(scal, *pieces, *weights)


def row_dots(weight, gradient, gain):
    return jnp.sum(weight.astype(F32) * gradient, axis=1) / gain.astype(F32)


def gather(matrix):
    return lax.all_gather(matrix, ALL, axis=0, tiled=True)


class Halving:
    def __init__(self, matrix, turned, own=False):
        self.devices = lax.axis_size("fsdp") * lax.axis_size("grp") * MEM
        bits = self.devices.bit_length() - 1
        outer = [bits - 1, bits - 2] if turned else [bits - 2, bits - 1]
        self.order = ([] if own else [0]) + outer + list(range(2 if own else 1, bits - 2))
        self.here = lax.axis_index(ALL)
        self.left = list(range(bits - 1, -1, -1))
        self.value = matrix.reshape([2] * bits + [matrix.shape[0] // self.devices, matrix.shape[1]])
        self.own = own
        self.split()

    def split(self):
        self.bit = self.order.pop(0)
        axis = self.left.index(self.bit)
        self.left.remove(self.bit)
        mine = (self.here >> self.bit) & 1
        self.away = lax.dynamic_index_in_dim(self.value, 1 - mine, axis, keepdims=False)
        self.kept = lax.dynamic_index_in_dim(self.value, mine, axis, keepdims=False)

    def send(self):
        self.came = lax.ppermute(self.away, ALL, [(s, s ^ (1 << self.bit)) for s in range(self.devices)])

    def add(self):
        self.value = self.kept.astype(F32) + self.came.astype(F32)
        if self.order or self.own:
            self.value = self.value.astype(BF)
        self.came = None
        if self.order:
            self.split()

    def on(self):
        if self.order:
            self.add()
            self.send()

    def finish(self):
        while self.order:
            self.on()
        self.add()
        return self.value


def tie(value, chains, name):
    got = lax.optimization_barrier((value, [getattr(chain, name) for chain in chains]))
    for chain, array in zip(chains, got[1]):
        setattr(chain, name, array)
    return got[0]


def gather_own(member, shard, width):
    devices = lax.axis_size("fsdp") * lax.axis_size("grp") * MEM
    here = lax.axis_index(ALL)
    pieces = [swap(lax.dynamic_index_in_dim(shard, member ^ j, keepdims=False), j) for j in range(MEM)]
    value = jnp.stack([lax.select_n(member, *[pieces[s ^ m] for m in range(MEM)]) for s in range(MEM)])
    for bit in range(2, devices.bit_length() - 1):
        mine = ((here >> bit) & 1) == 0
        came = lax.ppermute(value, ALL, [(s, s ^ (1 << bit)) for s in range(devices)])
        value = jnp.concatenate([jnp.where(mine, value, came), jnp.where(mine, came, value)])
    return value.reshape(devices * shard.shape[1], width)


def own_sets(member, value):
    value = value.reshape(MEM, *value.shape[2:])
    return [swap(lax.dynamic_index_in_dim(value, member ^ j, keepdims=False), j) for j in range(MEM)]


def moments(states):
    center = states - jnp.mean(states, axis=-1, keepdims=True)
    spread_ = jnp.mean(center * center, axis=-1, keepdims=True)
    rate = lax.rsqrt(spread_ + 1e-05)
    return (center * rate, rate)


def shards(
    tokens, frames, document_starts, cotangent,
    gain_self, gain_cross, gain_feed, gain_final,
    self_query, self_key, self_value, self_output,
    cross_query, cross_key, cross_value, cross_output,
    feed_up, feed_down,
):
    devices = lax.axis_size("fsdp") * lax.axis_size("grp") * MEM
    group, member = (lax.axis_index("grp"), lax.axis_index("mem"))
    groups = lax.axis_size("grp")
    starts = document_starts[0]
    inner = starts - SPAN * jnp.arange(groups, dtype=jnp.int32)
    late = jnp.concatenate([inner[1:], jnp.zeros((1,), jnp.int32)])
    scal = jnp.stack([
        member, member ^ 1, member ^ 2, member ^ 3,
        lax.dynamic_index_in_dim(inner, group, keepdims=False),
        lax.dynamic_index_in_dim(late, group, keepdims=False),
        member, member,
    ]).astype(jnp.int32)

    gains = jnp.stack([gain_self, gain_cross, gain_feed, gain_final], axis=1)
    gains = jnp.pad(gains, ((0, 0), (0, 124)))
    own_part, second, third = pack(
        self_query, self_key, self_value, gains, self_output, cross_output,
        cross_query, cross_key, cross_value, feed_up, feed_down,
    )
    w_own = gather_own(member, own_part, 640)
    two = swap(tokens, 2)
    other = swap(jnp.concatenate([tokens, two], axis=0), 1)
    near_tokens = [tokens, other[:ROWS], two, other[ROWS:]]
    tail, even = token_tail(member, near_tokens)
    near_tokens = jnp.concatenate([*near_tokens, tail], axis=0)
    held_frames, even = lax.optimization_barrier((frames, even))
    two = swap(held_frames, 2)
    near_frames = [swap(held_frames, 1), two]
    second, third = (gather(second), gather(third))
    third = third.reshape(devices, 2 * FF // devices, D)
    part = D // devices

    gain_rows = w_own[:, 512:].T[64:68].astype(F32)
    w_so, w_co = (second[:, :D], second[:, D : 2 * D])
    w_cq, w_kv = (second[:, 2 * D : 3 * D], second[:, 3 * D :])
    w_up = jnp.concatenate([third[:, c * part : (c + 1) * part].reshape(D, D) for c in range(4)], axis=1)
    w_down = third[:, 4 * part :].reshape(FF, D)

    states = tokens.astype(F32)
    unit, _ = moments(near_tokens.astype(F32))
    normed_self = (unit * gain_rows[0]).astype(BF)
    self_rows = product(normed_self, w_own).astype(BF)
    mixed, self_kept = self_forward(scal, self_rows)
    self_heads, near_frames = collect_straight(member, mixed, near_frames)
    near_frames = [frames, *near_frames, swap(near_frames[1], 1)]
    own_kv = lax.dynamic_slice_in_dim(w_kv, member * 384, 384, axis=1)
    frame_rows = [product(piece, own_kv).astype(BF) for piece in near_frames]
    first_sum = states + product(self_heads, w_so)
    normed_cross, back_cross = jax.vjp(normalize, first_sum, gain_rows[1])
    normed_cross = normed_cross.astype(BF)
    cross_queries = product(normed_cross, w_cq).astype(BF)
    cross_pieces = spread(member, cross_queries, True)
    mixed, cross_kept = cross_forward(scal, cross_pieces, frame_rows)
    cross_heads = collect(member, mixed)
    second_sum = first_sum + product(cross_heads, w_co)
    normed_feed, back_feed = jax.vjp(normalize, second_sum, gain_rows[2])
    normed_feed = normed_feed.astype(BF)
    inner_units = product(normed_feed, w_up)
    activated, back_gelu = jax.vjp(exact_gelu, inner_units)
    hidden = activated.astype(BF)
    third_sum = second_sum + product(hidden, w_down)
    result, back_final = jax.vjp(normalize, third_sum, gain_rows[3])

    grad_third, grad_gain_final = back_final(cotangent.astype(F32))
    grad_feed_out = grad_third.astype(BF)
    (grad_inner,) = back_gelu(product_right(grad_feed_out, w_down))
    grad_inner = grad_inner.astype(BF)
    grad_up = product_left(normed_feed, grad_inner).astype(BF)
    grad_down = product_left(hidden, grad_feed_out).astype(BF)
    final_column = jnp.pad(grad_gain_final[None], ((64, 63), (0, 0))).T
    down = Halving(grad_down, False)
    down.send()
    sums_up = lax.psum_scatter(grad_up, ALL, scatter_dimension=0, tiled=True)
    grad_second_part = back_feed(product_right(grad_inner, w_up))[0]
    grad_second = grad_third + grad_second_part

    grad_cross_out = grad_second.astype(BF)
    grad_cross_heads = product_right(grad_cross_out, w_co).astype(BF)
    grad_pieces = spread(member, grad_cross_heads, False)
    down.add()
    held = tie(scal, [down], "away")
    down.send()
    query_pieces, frame_grads = cross_backward(held, cross_pieces, frame_rows, grad_pieces, cross_kept)
    query_pieces, frame_grads = tie((query_pieces, frame_grads), [down], "came")
    down.on()
    grad_cross_queries = collect(member, query_pieces)
    grad_cross_queries, late_grads = lax.optimization_barrier((grad_cross_queries, frame_grads))
    late_grads = [swap(late_grads[j], j) for j in range(MEM)]
    grad_cq = product_left(normed_cross, grad_cross_queries).astype(BF)
    grad_first_part = back_cross(product_right(grad_cross_queries, w_cq))[0]
    grad_first = grad_second + grad_first_part

    grad_self_out = grad_first.astype(BF)
    grad_self_heads = product_right(grad_self_out, w_so).astype(BF)
    grad_pieces = spread(member, grad_self_heads, False)
    grad_co = product_left(cross_heads, grad_cross_out).astype(BF)
    grad_so = product_left(self_heads, grad_self_out).astype(BF)
    grad_kv = sum(product_left(near_frames[j], frame_grads[j]) for j in range(MEM))
    rest = [part.reshape(devices, D // devices, D) for part in (grad_so, grad_co, grad_cq)]
    rest = Halving(jnp.concatenate(rest, axis=1).reshape(3 * D, D), True)
    kv = Halving(grad_kv.astype(BF), False, True)
    kv.send()
    rest.send()
    down.add()
    rest.add()
    kv.add()
    held = tie(scal, [down, rest, kv], "away")
    down.send()
    rest.send()
    kv.send()
    grad_rows = self_backward(held, self_rows, grad_pieces, self_kept)
    grad_rows = tie(grad_rows, [down, rest, kv], "came")
    grad_rows, late_grads = lax.optimization_barrier((grad_rows, late_grads))
    grad_qkv = product_left(normed_self, grad_rows)
    last = grad_qkv[:, 512:] + final_column
    own = Halving(jnp.concatenate([grad_qkv[:, :512], last], axis=1).astype(BF), True, True)
    rest.came, down.came, kv.came = tie((rest.came, down.came, kv.came), [own], "away")
    own.send()
    rest.on()
    down.on()
    kv.on()
    grad_normed = product_right(grad_rows, w_own)
    total = total_rows(member, grad_normed)
    _, back_self = jax.vjp(normalize, states, gain_rows[0])
    tokens_gradient = grad_first + back_self(total)[0]
    frame_grad = join(member, late_grads, 384)
    frames_gradient = product_right(frame_grad, w_kv)

    sums_down = down.finish()
    while own.order:
        own.add()
        rest.came = tie(rest.came, [own], "away")
        own.send()
        rest.on()
    own.add()
    rest.came, own.value = lax.optimization_barrier((rest.came, own.value))
    sums_rest = rest.finish()
    last = jnp.concatenate([own.value, kv.finish()], axis=-1)
    last, sums_up = lax.optimization_barrier((last, sums_up))
    sets = own_sets(member, last)
    sums_up = sums_up.astype(F32)
    query, key, value, cross_k, cross_v, gains_out = unpack(scal, sets, (self_query, self_key, self_value))
    gains_out = gains_out.T
    grad_cq = sums_rest[2 * part :]
    return (
        result.astype(BF),
        tokens_gradient,
        frames_gradient,
        gains_out[0] / gain_self.astype(F32),
        row_dots(cross_query, grad_cq, gain_cross),
        row_dots(feed_up, sums_up, gain_feed),
        gains_out[64],
        query,
        key,
        value,
        sums_rest[:part],
        grad_cq,
        cross_k,
        cross_v,
        sums_rest[part : 2 * part],
        sums_up,
        sums_down,
    )


def solution(mesh):
    fsdp, ctx = (mesh.shape["fsdp"], mesh.shape["ctx"])
    fine = Mesh(mesh.devices.reshape(fsdp, ctx // MEM, MEM), ALL)
    rows, flat = (P(ALL, None), P(ALL))
    in_specs = (rows, rows, P("fsdp", None), rows) + (flat,) * 4 + (rows,) * 10
    out_specs = (rows,) * 3 + (flat,) * 4 + (rows,) * 10
    return jax.shard_map(shards, mesh=fine, in_specs=in_specs, out_specs=out_specs, check_vma=False)
```

```python
import functools

import jax
import jax.numpy as jnp
from jax import lax
from jax.experimental import pallas as pl
from jax.experimental.pallas import tpu as pltpu
from jax.sharding import Mesh, PartitionSpec as P

D = 768
HD = 64
FF = 3072
SPAN = 1024
MEM = 4
ROWS = 256
WIDE = (MEM + 1) * ROWS
HEADS = 3
FR = 375
FP = 384
KEYS = MEM * FP
NEG = -1e30
ALL = ("fsdp", "grp", "mem")
LINE = ("grp", "mem")
F32 = jnp.float32
BF = jnp.bfloat16


def normalize(states, gain):
    center = states - jnp.mean(states, axis=-1, keepdims=True)
    spread = jnp.mean(center * center, axis=-1, keepdims=True)
    return center * lax.rsqrt(spread + 1e-05) * gain


def exact_gelu(values):
    return jax.nn.gelu(values, approximate=False)


def product(left, right):
    return jnp.dot(left, right, preferred_element_type=F32)


def product_left(left, right):
    return lax.dot_general(left, right, (((0,), (0,)), ((), ())), preferred_element_type=F32)


def product_right(left, right):
    return lax.dot_general(left, right, (((1,), (1,)), ((), ())), preferred_element_type=F32)


def lanes(rows):
    return lax.broadcasted_iota(jnp.int32, (rows, 128), 1)


def head_lanes(head, rows):
    lane = lanes(rows)
    return (lane >= HD) if head == 1 else (lane < HD)


def only(head, window):
    return jnp.where(head_lanes(head, window.shape[0]), window, jnp.zeros_like(window))


def swap_halves(window):
    return pltpu.roll(window.astype(F32), HD, 1).astype(BF)


def marked(head, window, value):
    spare = 0 if head == 1 else HD
    return jnp.where(lanes(window.shape[0]) == spare, value, window)


def scaled(window):
    return (window.astype(F32) * 0.125).astype(BF)


def valid_rows(scal, first, count):
    row = first + lax.broadcasted_iota(jnp.int32, (count, 128), 0)
    return (row >= scal[4]) & (row < MEM * ROWS + scal[5])


def gather_rows(scal, pieces, tail, whole, step):
    for j in range(MEM):
        start = pl.multiple_of(scal[j] * step, step)
        whole[pl.ds(start, pieces[j].shape[0]), :] = pieces[j][...]
    if tail is not None:
        whole[pl.ds(MEM * step, tail.shape[0]), :] = tail[...]


def parts_of(ref):
    return [ref.at[j * ROWS : (j + 1) * ROWS] for j in range(MEM + 1)]


def scatter_rows(scal, whole, pieces, tail, step):
    for j in range(MEM):
        start = pl.multiple_of(scal[j] * step, step)
        pieces[j][...] = whole[pl.ds(start, pieces[j].shape[0]), :].astype(BF)
    if tail is not None:
        tail[...] = whole[pl.ds(MEM * step, tail.shape[0]), :].astype(BF)


def self_prepare(scal, whole, qa, ka):
    hidden = lax.broadcasted_iota(jnp.int32, (WIDE, 128), 0) < scal[4]
    for head in range(HEADS):
        if head < 2:
            query, key = whole[:, 0:128], whole[:, 128:256]
        else:
            query = whole[:, 384:512]
            key = swap_halves(query)
        qa[head] = marked(head, scaled(query), jnp.asarray(NEG, BF))
        ka[head] = marked(head, only(head, key), jnp.where(hidden, 1.0, 0.0).astype(BF))


def forward_finish(scal, ot, out, outs, tail):
    ot[HEADS * HD :, :] = jnp.zeros((HD, WIDE), F32)
    for i in range(MEM + 1):
        block = ot[:, i * ROWS : (i + 1) * ROWS].T
        keep = valid_rows(scal, i * ROWS, ROWS)[:, 0:1]
        out[i * ROWS : (i + 1) * ROWS, :] = jnp.where(keep, block, 0.0).astype(BF)
    scatter_rows(scal, out, outs, tail, ROWS)


def self_forward_kernel(scal, rows, o0, o1, o2, o3, otail, ot, lse, whole, qa, ka, vt, out):
    *pieces, tail = parts_of(rows)
    gather_rows(scal, pieces, tail, whole, ROWS)
    self_prepare(scal, whole, qa, ka)
    turned = whole[:, 256:384].astype(F32).T.astype(BF)
    vt[0] = turned[0:HD]
    vt[1] = turned[HD:128]
    vt[2] = whole[:, 512:640].astype(F32).T.astype(BF)[0:HD]
    causal = lax.broadcasted_iota(jnp.int32, (ROWS, ROWS), 0) <= lax.broadcasted_iota(
        jnp.int32, (ROWS, ROWS), 1
    )

    def one_head(head, carry):
        for i in range(MEM + 1):
            a, b = i * ROWS, (i + 1) * ROWS
            query = qa[head, a:b, :]
            near = jnp.where(causal, product_right(ka[head, a:b, :], query), NEG)
            top = jnp.max(near, axis=0, keepdims=True)
            if i:
                far = product_right(ka[head, 0:a, :], query)
                top = jnp.maximum(top, jnp.max(far, axis=0, keepdims=True))
                far = jnp.exp(far - top)
            near = jnp.exp(near - top)
            total = jnp.sum(near, axis=0, keepdims=True)
            if i:
                total = total + jnp.sum(far, axis=0, keepdims=True)
            scale = 1.0 / total
            mixed = product(vt[head, :, a:b], (near * scale).astype(BF))
            if i:
                mixed = mixed + product(vt[head, :, 0:a], (far * scale).astype(BF))
            ot[pl.ds(pl.multiple_of(head * HD, HD), HD), a:b] = mixed
            lse[head, 0:1, a:b] = top + jnp.log(total)
        return carry

    lax.fori_loop(0, HEADS, one_head, 0)
    forward_finish(scal, ot, out, (o0, o1, o2, o3), otail)


def grads_prepare(scal, grads, ot, dm, delta):
    for i in range(MEM + 1):
        a, b = i * ROWS, (i + 1) * ROWS
        keep = valid_rows(scal, a, ROWS)[:, 0:1]
        clean = jnp.where(keep, grads[a:b, :].astype(F32), 0.0)
        turned = clean.T * ot[:, a:b]
        clean = clean.astype(BF)
        for head in range(HEADS):
            window = clean[:, 0:128] if head < 2 else clean[:, 128:256]
            dm[head, a:b, :] = only(head, window)
            delta[head, 0:1, a:b] = jnp.sum(turned[head * HD : (head + 1) * HD], axis=0, keepdims=True)


def self_backward_kernel(
    scal, rows, g0, g1, g2, g3, gtail, ot, lse, drows,
    whole, grads, qa, ka, qm, kt, vm, dm, delta, dqt, dk, dv, out,
):
    *pieces, tail = parts_of(rows)
    gather_rows(scal, pieces, tail, whole, ROWS)
    gather_rows(scal, (g0, g1, g2, g3), gtail, grads, ROWS)
    self_prepare(scal, whole, qa, ka)
    grads_prepare(scal, grads, ot, dm, delta)
    turned = whole[:, 128:256].astype(F32).T.astype(BF)
    kt[0] = turned[0:HD]
    kt[1] = turned[HD:128]
    kt[2] = whole[:, 384:512].astype(F32).T.astype(BF)[HD:128]
    for head in range(HEADS):
        qm[head] = only(head, scaled(whole[:, 0:128] if head < 2 else whole[:, 384:512]))
        vm[head] = only(head, whole[:, 256:384] if head < 2 else whole[:, 512:640])
    dk[...] = jnp.zeros_like(dk)
    dv[...] = jnp.zeros_like(dv)
    dqt[HEADS * HD :, :] = jnp.zeros((HD, WIDE), F32)
    causal = lax.broadcasted_iota(jnp.int32, (ROWS, ROWS), 0) <= lax.broadcasted_iota(
        jnp.int32, (ROWS, ROWS), 1
    )

    def one_head(head, carry):
        side = jnp.where(head == 2, 1, 0)
        for i in range(MEM + 1):
            a, b = i * ROWS, (i + 1) * ROWS
            query, grad, own = qa[head, a:b, :], dm[head, a:b, :], qm[head, a:b, :]
            level, offset = lse[head, 0:1, a:b], delta[head, 0:1, a:b]
            change = jnp.zeros((HD, ROWS), F32)
            for low, high in ((a, b), (0, a)):
                if low == high:
                    continue
                scores = product_right(ka[head, low:high, :], query)
                if low == a:
                    scores = jnp.where(causal, scores, NEG)
                probs = jnp.exp(scores - level)
                slopes = product_right(vm[head, low:high, :], grad)
                slopes = (probs * (slopes - offset)).astype(BF)
                dv[side, low:high, :] += product(probs.astype(BF), grad)
                dk[side, low:high, :] += product(slopes, own)
                change = change + product(kt[head, :, low:high], slopes)
            dqt[pl.ds(pl.multiple_of(head * HD, HD), HD), a:b] = change * 0.125
        return carry

    lax.fori_loop(0, HEADS, one_head, 0)
    for i in range(MEM + 1):
        a, b = i * ROWS, (i + 1) * ROWS
        query = dqt[:, a:b].T
        out[a:b, 0:128] = query[:, 0:128].astype(BF)
        out[a:b, 128:256] = dk[0, a:b, :].astype(BF)
        out[a:b, 256:384] = dv[0, a:b, :].astype(BF)
        out[a:b, 384:512] = (query[:, 128:256] + pltpu.roll(dk[1, a:b, :], HD, 1)).astype(BF)
        out[a:b, 512:640] = dv[1, a:b, :].astype(BF)
    *pieces, tail = parts_of(drows)
    scatter_rows(scal, out, pieces, tail, ROWS)


def cross_prepare(whole, queries, qa, ka):
    spare = (lax.broadcasted_iota(jnp.int32, (KEYS, 128), 0) % FP) >= FR
    for head in range(HEADS):
        query = queries[:, 0:128] if head < 2 else queries[:, 128:256]
        key = whole[:, 0:128] if head < 2 else whole[:, 256:384]
        qa[head] = marked(head, scaled(query), jnp.asarray(NEG, BF))
        ka[head] = marked(head, only(head, key), jnp.where(spare, 1.0, 0.0).astype(BF))


def cross_forward_kernel(
    scal, q0, q1, q2, q3, qtail, f0, f1, f2, f3,
    o0, o1, o2, o3, otail, ot, lse,
    whole, queries, qa, ka, vt, out,
):
    whole[...] = jnp.zeros_like(whole)
    for j, piece in enumerate((f0, f1, f2, f3)):
        whole[j * FP : j * FP + FR, :] = piece[...]
    gather_rows(scal, (q0, q1, q2, q3), qtail, queries, ROWS)
    cross_prepare(whole, queries, qa, ka)
    turned = whole[:, 128:256].astype(F32).T.astype(BF)
    vt[0] = turned[0:HD]
    vt[1] = turned[HD:128]
    vt[2] = whole[:, 256:384].astype(F32).T.astype(BF)[HD:128]

    def one_block(step, carry):
        head = step // (MEM + 1)
        here = pl.ds(pl.multiple_of((step % (MEM + 1)) * ROWS, ROWS), ROWS)
        scores = product_right(ka[head], qa[head, here, :])
        top = jnp.max(scores, axis=0, keepdims=True)
        scores = jnp.exp(scores - top)
        total = jnp.sum(scores, axis=0, keepdims=True)
        mixed = product(vt[head], (scores * (1.0 / total)).astype(BF))
        ot[pl.ds(pl.multiple_of(head * HD, HD), HD), here] = mixed
        lse[head, 0:1, here] = top + jnp.log(total)
        return carry

    lax.fori_loop(0, HEADS * (MEM + 1), one_block, 0)
    forward_finish(scal, ot, out, (o0, o1, o2, o3), otail)


def cross_backward_kernel(
    scal, q0, q1, q2, q3, qtail, f0, f1, f2, f3, g0, g1, g2, g3, gtail, ot, lse,
    d0, d1, d2, d3, dtail, e0, e1, e2, e3,
    whole, queries, grads, qa, ka, qm, kt, vm, dm, delta, dqt, dk, dv, out, fout,
):
    whole[...] = jnp.zeros_like(whole)
    for j, piece in enumerate((f0, f1, f2, f3)):
        whole[j * FP : j * FP + FR, :] = piece[...]
    gather_rows(scal, (q0, q1, q2, q3), qtail, queries, ROWS)
    gather_rows(scal, (g0, g1, g2, g3), gtail, grads, ROWS)
    cross_prepare(whole, queries, qa, ka)
    grads_prepare(scal, grads, ot, dm, delta)
    turned = whole[:, 0:128].astype(F32).T.astype(BF)
    kt[0] = turned[0:HD]
    kt[1] = turned[HD:128]
    kt[2] = whole[:, 256:384].astype(F32).T.astype(BF)[0:HD]
    for head in range(HEADS):
        qm[head] = only(head, scaled(queries[:, 0:128] if head < 2 else queries[:, 128:256]))
        vm[head] = only(head, whole[:, 128:256] if head < 2 else swap_halves(whole[:, 256:384]))
    dk[...] = jnp.zeros_like(dk)
    dv[...] = jnp.zeros_like(dv)
    dqt[HEADS * HD :, :] = jnp.zeros((HD, WIDE), F32)

    def one_block(step, carry):
        head = step // (MEM + 1)
        side = jnp.where(head == 2, 1, 0)
        here = pl.ds(pl.multiple_of((step % (MEM + 1)) * ROWS, ROWS), ROWS)
        grad = dm[head, here, :]
        scores = product_right(ka[head], qa[head, here, :])
        probs = jnp.exp(scores - lse[head, 0:1, here])
        slopes = product_right(vm[head], grad)
        slopes = (probs * (slopes - delta[head, 0:1, here])).astype(BF)
        dv[side] += product(probs.astype(BF), grad)
        dk[side] += product(slopes, qm[head, here, :])
        change = product(kt[head], slopes)
        dqt[pl.ds(pl.multiple_of(head * HD, HD), HD), here] = change * 0.125
        return carry

    lax.fori_loop(0, HEADS * (MEM + 1), one_block, 0)
    for i in range(MEM + 1):
        a, b = i * ROWS, (i + 1) * ROWS
        out[a:b, :] = dqt[:, a:b].T.astype(BF)
    scatter_rows(scal, out, (d0, d1, d2, d3), dtail, ROWS)
    fout[:, 0:128] = dk[0].astype(BF)
    fout[:, 128:256] = dv[0].astype(BF)
    fout[:, 256:384] = (dk[1] + pltpu.roll(dv[1], HD, 1)).astype(BF)
    for j, piece in enumerate((e0, e1, e2, e3)):
        piece[...] = fout[j * FP : j * FP + FR, :]


def shape(*dims, dtype=BF):
    return jax.ShapeDtypeStruct(dims, dtype)


def vmem(*dims, dtype=BF):
    return pltpu.VMEM(dims, dtype)


def call(kernel, scal, args, outs, scratch, flops, exps):
    full = pl.BlockSpec(memory_space=pltpu.VMEM)
    return pl.pallas_call(
        kernel,
        out_shape=outs,
        in_specs=[pl.BlockSpec(memory_space=pltpu.SMEM)] + [full] * len(args),
        out_specs=[full] * len(outs),
        scratch_shapes=scratch,
        cost_estimate=pl.CostEstimate(flops=flops, transcendentals=exps, bytes_accessed=4 << 20),
        compiler_params=pltpu.CompilerParams(vmem_limit_bytes=60 << 20),
    )(scal, *args)


def self_forward(scal, rows):
    outs = [shape(ROWS, 256)] * 5 + [shape(256, WIDE, dtype=F32), shape(HEADS, 8, WIDE, dtype=F32)]
    scratch = [vmem(WIDE, 640), vmem(HEADS, WIDE, 128), vmem(HEADS, WIDE, 128), vmem(HEADS, HD, WIDE), vmem(WIDE, 256)]
    got = call(self_forward_kernel, scal, [rows], outs, scratch, 3 << 30, 3 << 20)
    return (got[:5], got[5:])


def self_backward(scal, rows, grads, kept):
    outs = [shape(WIDE, 640)]
    head = vmem(HEADS, WIDE, 128)
    scratch = [
        vmem(WIDE, 640), vmem(WIDE, 256), head, head, head, vmem(HEADS, HD, WIDE), head, head,
        vmem(HEADS, 8, WIDE, dtype=F32), vmem(256, WIDE, dtype=F32),
        vmem(2, WIDE, 128, dtype=F32), vmem(2, WIDE, 128, dtype=F32), vmem(WIDE, 640),
    ]
    return call(self_backward_kernel, scal, [rows, *grads, *kept], outs, scratch, 8 << 30, 3 << 20)[0]


def cross_forward(scal, queries, frames):
    outs = [shape(ROWS, 256)] * 5 + [shape(256, WIDE, dtype=F32), shape(HEADS, 8, WIDE, dtype=F32)]
    scratch = [
        vmem(KEYS, 384), vmem(WIDE, 256), vmem(HEADS, WIDE, 128), vmem(HEADS, KEYS, 128),
        vmem(HEADS, HD, KEYS), vmem(WIDE, 256),
    ]
    got = call(cross_forward_kernel, scal, [*queries, *frames], outs, scratch, 6 << 30, 6 << 20)
    return (got[:5], got[5:])


def cross_backward(scal, queries, frames, grads, kept):
    outs = [shape(ROWS, 256)] * 5 + [shape(FR, 384)] * 4
    head, keys = (vmem(HEADS, WIDE, 128), vmem(HEADS, KEYS, 128))
    scratch = [
        vmem(KEYS, 384), vmem(WIDE, 256), vmem(WIDE, 256), head, keys, head, vmem(HEADS, HD, KEYS), keys, head,
        vmem(HEADS, 8, WIDE, dtype=F32), vmem(256, WIDE, dtype=F32),
        vmem(2, KEYS, 128, dtype=F32), vmem(2, KEYS, 128, dtype=F32), vmem(WIDE, 256), vmem(KEYS, 384),
    ]
    got = call(cross_backward_kernel, scal, [*queries, *frames, *grads, *kept], outs, scratch, 16 << 30, 6 << 20)
    return (got[:5], got[5:])


def swap(value, mask):
    if mask == 0:
        return value
    count = lax.axis_size("grp") * MEM
    return lax.ppermute(value, LINE, [(s, s ^ mask) for s in range(count)])


def to_previous(value):
    count = lax.axis_size("grp") * MEM
    return lax.ppermute(value, LINE, [(s, s - MEM) for s in range(MEM, count)])


def to_next(value):
    count = lax.axis_size("grp") * MEM
    return lax.ppermute(value, LINE, [(s, s + MEM) for s in range(count - MEM)])


def spread(member, rows, straight):
    parts = [jnp.pad(rows[:, 192 * m : 192 * m + 192], ((0, 0), (0, 64))) for m in range(MEM)]
    pieces = [swap(lax.select_n(member, *[parts[m ^ j] for m in range(MEM)]), j) for j in range(MEM)]
    if not straight:
        return [*pieces, to_previous(lax.select_n(member, *pieces))]
    count = lax.axis_size("grp") * MEM
    tails = [
        lax.ppermute(parts[m], LINE, [(s, s - MEM + m) for s in range(MEM, count, MEM)])
        for m in range(MEM)
    ]
    return [*pieces, lax.select_n(member, *tails)]


def token_tail(member, pieces):
    count = lax.axis_size("grp") * MEM
    even = lax.ppermute(
        lax.select_n(member, *pieces), LINE, [(s, s - MEM) for s in range(MEM, count, 2)]
    )
    odd = lax.ppermute(even, LINE, [(s, s + 1) for s in range(0, count, 2)])
    return (jnp.where(member % 2 == 0, even, odd), even)


def total_rows(member, partial):
    core = member % 2
    half = ROWS // 2
    tail = partial[MEM * ROWS :].reshape(2, half, D)
    late = swap(lax.dynamic_index_in_dim(tail, 1 - core, keepdims=False).astype(BF), 1).astype(F32)
    late = to_next((late + lax.dynamic_index_in_dim(tail, core, keepdims=False)).astype(BF)).astype(F32)
    late = jnp.concatenate([jnp.where(core == c, late, 0.0) for c in range(2)], axis=0)
    pieces = [
        partial[j * ROWS : (j + 1) * ROWS] + jnp.where(member == j, late, 0.0) for j in range(MEM)
    ]
    other = swap(jnp.concatenate([pieces[1], pieces[3]], axis=0).astype(BF), 1).astype(F32)
    far = (pieces[2] + other[ROWS:]).astype(BF)
    return pieces[0] + other[:ROWS] + swap(far, 2).astype(F32)


def join(member, pieces, width):
    return jnp.concatenate(
        [lax.select_n(member, *[pieces[s ^ m][:, :width] for m in range(MEM)]) for s in range(MEM)], axis=1
    )


def collect(member, pieces):
    late = to_next(pieces[4])
    whole = []
    for j in range(MEM):
        piece = pieces[j].astype(F32) + jnp.where(member == j, late.astype(F32), 0.0)
        whole.append(swap(piece.astype(BF), j))
    return join(member, whole, 192)


def collect_straight(member, pieces, beside):
    count = lax.axis_size("grp") * MEM
    lates = [
        lax.ppermute(pieces[4], LINE, [(s - MEM + m, s) for s in range(MEM, count, MEM)])
        for m in range(MEM)
    ]
    near = [swap(pieces[j], j) for j in range(MEM)]
    near[3], beside = lax.optimization_barrier((near[3], beside))
    late = jnp.concatenate([piece[:, :192] for piece in lates], axis=1)
    total = join(member, near, 192).astype(F32) + late.astype(F32)
    return (total.astype(BF), beside)


def pack_kernel(query, key, value, gains, so, co, cq, ck, cv, up, down, own, second, third):
    rows = query.shape[0]
    for m in range(MEM):
        a = 192 * m
        for n, matrix in enumerate((query, key, value)):
            own[m, :, 128 * n : 128 * n + 128] = matrix[:, a : a + 128]
        own[m, :, 384:512] = jnp.concatenate([query[:, a + 128 : a + 192], key[:, a + 128 : a + 192]], axis=1)
        own[m, :, 512:640] = jnp.concatenate([value[:, a + 128 : a + 192], gains[:, 0:64]], axis=1)
        b = 3 * D + 384 * m
        second[:, b : b + 128] = ck[:, a : a + 128]
        second[:, b + 128 : b + 256] = cv[:, a : a + 128]
        second[:, b + 256 : b + 384] = jnp.concatenate([ck[:, a + 128 : a + 192], cv[:, a + 128 : a + 192]], axis=1)
    for n, matrix in enumerate((so, co, cq)):
        second[:, D * n : D * n + D] = matrix[...]
    for c in range(FF // D):
        third[c * rows : (c + 1) * rows, :] = up[:, c * D : (c + 1) * D]
    third[4 * rows :, :] = down[...]


def pack(*args):
    rows = args[0].shape[0]
    full = pl.BlockSpec(memory_space=pltpu.VMEM)
    return pl.pallas_call(
        pack_kernel,
        out_shape=[shape(MEM, rows, 640), shape(rows, 3 * D + 1536), shape(8 * rows, D)],
        in_specs=[full] * len(args),
        out_specs=[full] * 3,
    )(*args)


def unpack_kernel(scal, p0, p1, p2, p3, wq, wk, wv, query, key, value, ck, cv, gains, sets):
    for j, piece in enumerate((p0, p1, p2, p3)):
        sets[scal[j]] = piece[...].astype(F32)
    total = jnp.zeros_like(gains)
    for m in range(MEM):
        a = 192 * m
        for n, out in enumerate((query, key, value)):
            out[:, a : a + 128] = sets[m, :, 128 * n : 128 * n + 128]
        last = sets[m, :, 512:640]
        query[:, a + 128 : a + 192] = sets[m, :, 384:448]
        key[:, a + 128 : a + 192] = sets[m, :, 448:512]
        value[:, a + 128 : a + 192] = last[:, 0:64]
        total = total + last
        ck[:, a : a + 128] = sets[m, :, 640:768]
        cv[:, a : a + 128] = sets[m, :, 768:896]
        ck[:, a + 128 : a + 192] = sets[m, :, 896:960]
        cv[:, a + 128 : a + 192] = sets[m, :, 960:1024]
    dots = jnp.zeros_like(total[:, 0:1])
    for matrix, out in ((wq, query), (wk, key), (wv, value)):
        dots = dots + jnp.sum(matrix[...].astype(F32) * out[...], axis=1, keepdims=True)
    gains[...] = jnp.where(lanes(total.shape[0]) == 0, dots, total)


def unpack(scal, pieces, weights):
    rows = pieces[0].shape[0]
    full = pl.BlockSpec(memory_space=pltpu.VMEM)
    return pl.pallas_call(
        unpack_kernel,
        out_shape=[shape(rows, D, dtype=F32)] * 5 + [shape(rows, 128, dtype=F32)],
        in_specs=[pl.BlockSpec(memory_space=pltpu.SMEM)] + [full] * 7,
        out_specs=[full] * 6,
        scratch_shapes=[vmem(MEM, rows, 1024, dtype=F32)],
    )(scal, *pieces, *weights)


def row_dots(weight, gradient, gain):
    return jnp.sum(weight.astype(F32) * gradient, axis=1) / gain.astype(F32)


def gather(matrix):
    return lax.all_gather(matrix, ALL, axis=0, tiled=True)


class Halving:
    def __init__(self, matrix, turned, own=False):
        self.devices = lax.axis_size("fsdp") * lax.axis_size("grp") * MEM
        bits = self.devices.bit_length() - 1
        outer = [bits - 1, bits - 2] if turned else [bits - 2, bits - 1]
        self.order = ([] if own else [0]) + outer + list(range(2 if own else 1, bits - 2))
        self.here = lax.axis_index(ALL)
        self.left = list(range(bits - 1, -1, -1))
        self.value = matrix.reshape([2] * bits + [matrix.shape[0] // self.devices, matrix.shape[1]])
        self.own = own
        self.split()

    def split(self):
        self.bit = self.order.pop(0)
        axis = self.left.index(self.bit)
        self.left.remove(self.bit)
        mine = (self.here >> self.bit) & 1
        self.away = lax.dynamic_index_in_dim(self.value, 1 - mine, axis, keepdims=False)
        self.kept = lax.dynamic_index_in_dim(self.value, mine, axis, keepdims=False)

    def send(self):
        self.came = lax.ppermute(self.away, ALL, [(s, s ^ (1 << self.bit)) for s in range(self.devices)])

    def add(self):
        self.value = self.kept.astype(F32) + self.came.astype(F32)
        if self.order or self.own:
            self.value = self.value.astype(BF)
        self.came = None
        if self.order:
            self.split()

    def on(self):
        if self.order:
            self.add()
            self.send()

    def finish(self):
        while self.order:
            self.on()
        self.add()
        return self.value


def tie(value, chains, name):
    got = lax.optimization_barrier((value, [getattr(chain, name) for chain in chains]))
    for chain, array in zip(chains, got[1]):
        setattr(chain, name, array)
    return got[0]


def gather_own(member, shard, width):
    devices = lax.axis_size("fsdp") * lax.axis_size("grp") * MEM
    here = lax.axis_index(ALL)
    pieces = [swap(lax.dynamic_index_in_dim(shard, member ^ j, keepdims=False), j) for j in range(MEM)]
    value = jnp.stack([lax.select_n(member, *[pieces[s ^ m] for m in range(MEM)]) for s in range(MEM)])
    for bit in range(2, devices.bit_length() - 1):
        mine = ((here >> bit) & 1) == 0
        came = lax.ppermute(value, ALL, [(s, s ^ (1 << bit)) for s in range(devices)])
        value = jnp.concatenate([jnp.where(mine, value, came), jnp.where(mine, came, value)])
    return value.reshape(devices * shard.shape[1], width)


def own_sets(member, value):
    value = value.reshape(MEM, *value.shape[2:])
    return [swap(lax.dynamic_index_in_dim(value, member ^ j, keepdims=False), j) for j in range(MEM)]


def moments(states):
    center = states - jnp.mean(states, axis=-1, keepdims=True)
    spread_ = jnp.mean(center * center, axis=-1, keepdims=True)
    rate = lax.rsqrt(spread_ + 1e-05)
    return (center * rate, rate)


def shards(
    tokens, frames, document_starts, cotangent,
    gain_self, gain_cross, gain_feed, gain_final,
    self_query, self_key, self_value, self_output,
    cross_query, cross_key, cross_value, cross_output,
    feed_up, feed_down,
):
    devices = lax.axis_size("fsdp") * lax.axis_size("grp") * MEM
    group, member = (lax.axis_index("grp"), lax.axis_index("mem"))
    groups = lax.axis_size("grp")
    starts = document_starts[0]
    inner = starts - SPAN * jnp.arange(groups, dtype=jnp.int32)
    late = jnp.concatenate([inner[1:], jnp.zeros((1,), jnp.int32)])
    scal = jnp.stack([
        member, member ^ 1, member ^ 2, member ^ 3,
        lax.dynamic_index_in_dim(inner, group, keepdims=False),
        lax.dynamic_index_in_dim(late, group, keepdims=False),
        member, member,
    ]).astype(jnp.int32)

    gains = jnp.stack([gain_self, gain_cross, gain_feed, gain_final], axis=1)
    gains = jnp.pad(gains, ((0, 0), (0, 124)))
    own_part, second, third = pack(
        self_query, self_key, self_value, gains, self_output, cross_output,
        cross_query, cross_key, cross_value, feed_up, feed_down,
    )
    w_own = gather_own(member, own_part, 640)
    two = swap(tokens, 2)
    other = swap(jnp.concatenate([tokens, two], axis=0), 1)
    near_tokens = [tokens, other[:ROWS], two, other[ROWS:]]
    tail, even = token_tail(member, near_tokens)
    near_tokens = jnp.concatenate([*near_tokens, tail], axis=0)
    held_frames, even = lax.optimization_barrier((frames, even))
    two = swap(held_frames, 2)
    near_frames = [swap(held_frames, 1), two]
    second, third = (gather(second), gather(third))
    third = third.reshape(devices, 2 * FF // devices, D)
    part = D // devices

    gain_rows = w_own[:, 512:].T[64:68].astype(F32)
    w_so, w_co = (second[:, :D], second[:, D : 2 * D])
    w_cq, w_kv = (second[:, 2 * D : 3 * D], second[:, 3 * D :])
    w_up = jnp.concatenate([third[:, c * part : (c + 1) * part].reshape(D, D) for c in range(4)], axis=1)
    w_down = third[:, 4 * part :].reshape(FF, D)

    states = tokens.astype(F32)
    unit, _ = moments(near_tokens.astype(F32))
    normed_self = (unit * gain_rows[0]).astype(BF)
    self_rows = product(normed_self, w_own).astype(BF)
    mixed, self_kept = self_forward(scal, self_rows)
    self_heads, near_frames = collect_straight(member, mixed, near_frames)
    near_frames = [frames, *near_frames, swap(near_frames[1], 1)]
    own_kv = lax.dynamic_slice_in_dim(w_kv, member * 384, 384, axis=1)
    frame_rows = [product(piece, own_kv).astype(BF) for piece in near_frames]
    first_sum = states + product(self_heads, w_so)
    normed_cross, back_cross = jax.vjp(normalize, first_sum, gain_rows[1])
    normed_cross = normed_cross.astype(BF)
    cross_queries = product(normed_cross, w_cq).astype(BF)
    cross_pieces = spread(member, cross_queries, True)
    mixed, cross_kept = cross_forward(scal, cross_pieces, frame_rows)
    cross_heads = collect(member, mixed)
    second_sum = first_sum + product(cross_heads, w_co)
    normed_feed, back_feed = jax.vjp(normalize, second_sum, gain_rows[2])
    normed_feed = normed_feed.astype(BF)
    inner_units = product(normed_feed, w_up)
    activated, back_gelu = jax.vjp(exact_gelu, inner_units)
    hidden = activated.astype(BF)
    third_sum = second_sum + product(hidden, w_down)
    result, back_final = jax.vjp(normalize, third_sum, gain_rows[3])

    grad_third, grad_gain_final = back_final(cotangent.astype(F32))
    grad_feed_out = grad_third.astype(BF)
    (grad_inner,) = back_gelu(product_right(grad_feed_out, w_down))
    grad_inner = grad_inner.astype(BF)
    grad_up = product_left(normed_feed, grad_inner).astype(BF)
    grad_down = product_left(hidden, grad_feed_out).astype(BF)
    final_column = jnp.pad(grad_gain_final[None], ((64, 63), (0, 0))).T
    down = Halving(grad_down, False)
    down.send()
    sums_up = lax.psum_scatter(grad_up, ALL, scatter_dimension=0, tiled=True)
    grad_second_part = back_feed(product_right(grad_inner, w_up))[0]
    grad_second = grad_third + grad_second_part

    grad_cross_out = grad_second.astype(BF)
    grad_cross_heads = product_right(grad_cross_out, w_co).astype(BF)
    grad_pieces = spread(member, grad_cross_heads, False)
    down.add()
    held = tie(scal, [down], "away")
    down.send()
    query_pieces, frame_grads = cross_backward(held, cross_pieces, frame_rows, grad_pieces, cross_kept)
    query_pieces, frame_grads = tie((query_pieces, frame_grads), [down], "came")
    down.on()
    grad_cross_queries = collect(member, query_pieces)
    grad_cq = product_left(normed_cross, grad_cross_queries).astype(BF)
    grad_first_part = back_cross(product_right(grad_cross_queries, w_cq))[0]
    grad_first = grad_second + grad_first_part

    grad_self_out = grad_first.astype(BF)
    grad_self_heads = product_right(grad_self_out, w_so).astype(BF)
    grad_pieces = spread(member, grad_self_heads, False)
    grad_co = product_left(cross_heads, grad_cross_out).astype(BF)
    grad_so = product_left(self_heads, grad_self_out).astype(BF)
    grad_kv = sum(product_left(near_frames[j], frame_grads[j]) for j in range(MEM))
    rest = [part.reshape(devices, D // devices, D) for part in (grad_so, grad_co, grad_cq)]
    rest = Halving(jnp.concatenate(rest, axis=1).reshape(3 * D, D), True)
    rest.send()
    down.add()
    rest.add()
    held = tie(scal, [down, rest], "away")
    down.send()
    rest.send()
    held, late_grads = lax.optimization_barrier((held, frame_grads))
    grad_rows = self_backward(held, self_rows, grad_pieces, self_kept)
    grad_rows = tie(grad_rows, [down, rest], "came")
    grad_qkv = product_left(normed_self, grad_rows)
    last = grad_qkv[:, 512:] + final_column
    own = Halving(jnp.concatenate([grad_qkv[:, :512], last, grad_kv], axis=1).astype(BF), True, True)
    rest.came, down.came = tie((rest.came, down.came), [own], "away")
    own.send()
    rest.on()
    down.on()
    grad_normed = product_right(grad_rows, w_own)
    total = total_rows(member, grad_normed)
    _, back_self = jax.vjp(normalize, states, gain_rows[0])
    tokens_gradient = grad_first + back_self(total)[0]
    frame_grad = join(member, [swap(late_grads[j], j) for j in range(MEM)], 384)
    frames_gradient = product_right(frame_grad, w_kv)

    sums_down = down.finish()
    while own.order:
        own.add()
        rest.came = tie(rest.came, [own], "away")
        own.send()
        rest.on()
    own.add()
    rest.came, own.value = lax.optimization_barrier((rest.came, own.value))
    sums_rest = rest.finish()
    own.add = lambda: None
    last, sums_up = lax.optimization_barrier((own.finish(), sums_up))
    sets = own_sets(member, last)
    sums_up = sums_up.astype(F32)
    query, key, value, cross_k, cross_v, gains_out = unpack(scal, sets, (self_query, self_key, self_value))
    gains_out = gains_out.T
    grad_cq = sums_rest[2 * part :]
    return (
        result.astype(BF),
        tokens_gradient,
        frames_gradient,
        gains_out[0] / gain_self.astype(F32),
        row_dots(cross_query, grad_cq, gain_cross),
        row_dots(feed_up, sums_up, gain_feed),
        gains_out[64],
        query,
        key,
        value,
        sums_rest[:part],
        grad_cq,
        cross_k,
        cross_v,
        sums_rest[part : 2 * part],
        sums_up,
        sums_down,
    )


def solution(mesh):
    fsdp, ctx = (mesh.shape["fsdp"], mesh.shape["ctx"])
    fine = Mesh(mesh.devices.reshape(fsdp, ctx // MEM, MEM), ALL)
    rows, flat = (P(ALL, None), P(ALL))
    in_specs = (rows, rows, P("fsdp", None), rows) + (flat,) * 4 + (rows,) * 10
    out_specs = (rows,) * 3 + (flat,) * 4 + (rows,) * 10
    return jax.shard_map(shards, mesh=fine, in_specs=in_specs, out_specs=out_specs, check_vma=False)
```
